256 devices in a mesh: dp: 4 (over y), graph: 64 (over z, x, core).
Axes of the slice: x: 4, y: 4, z: 8, core: 2. Of those that a mesh axis runs over, the one named last changes fastest.
Arguments:
- edge_state: bfloat16 [4, 131072, 512], P('dp', 'graph'), may hold values from -6 to 6
- cotangent: bfloat16 [4, 131072, 512], P('dp', 'graph'), may hold values from -6 to 6
- edge_count: int32 [4, 64], P('dp', 'graph'), may hold values from 1024 to 2048, as said below
- triplet_basis: bfloat16 [4, 16, 524288], P('dp', None, 'graph'), may hold values from -6 to 6
- triplet_in: int32 [4, 524288], P('dp', 'graph'), may hold values from 0 to 2047, as said below
- triplet_out: int32 [4, 524288], P('dp', 'graph'), may hold values from 0 to 2047, as said below
- down_weight: bfloat16 [512, 64], replicated, may hold values from -0.25 to 0.25
- basis_weight: bfloat16 [16, 64], replicated, may hold values from -1.5 to 1.5
- bilinear_weight: bfloat16 [64, 64], replicated, may hold values from -0.75 to 0.75
- up_weight: bfloat16 [64, 512], replicated, may hold values from -0.75 to 0.75
- first_weight: bfloat16 [512, 512], replicated, may hold values from -0.25 to 0.25
- second_weight: bfloat16 [512, 512], replicated, may hold values from -0.25 to 0.25
Outputs:
- edge_grad: bfloat16 [4, 131072, 512], P('dp', 'graph')
- down_grad: float32 [512, 64], replicated
- basis_grad: float32 [16, 64], replicated
- bilinear_grad: float32 [64, 64], replicated
- up_grad: float32 [64, 512], replicated
- first_grad: float32 [512, 512], replicated
- second_grad: float32 [512, 512], replicated
The draws below stay inside these ranges and needn't reach their ends.
Inputs may be any that keep to these rules, and one draw needn't show every extreme that they name: `edge_count`: every entry is a multiple of 128; in every batch some shard holds all 2048 slots live. Slot s * 8192 + j * 128 + k (s and j below 64, k below 128) holds a triplet of shard s whose in-edge is row triplet_in of shard j, a live row: below edge_count[b, j]. Slot s * 8192 + t holds a triplet whose out-edge is row triplet_out of shard s, a live row: below edge_count[b, s].
All inputs are finite; a program needn't handle non-finite values.
Results may differ from the reference program's by a relative error of at most 0.0096.
Values may be sent and summed in bfloat16 or wider, within the bound.
A program may use at most 128 MiB of HBM per device.

```python
import math
import jax
import jax.numpy as jnp
from jax import lax

H = 512
K = 64
NB = 16
E_DEV = 2048
BATCHES = 4
SHARDS = 64
EDGES = 131072
TRI_DEV = 8192
TRIPLETS = 524288
CAP = 128


def edge_counts(key):
    base_key = jax.random.fold_in(key, 11)
    low_blocks = E_DEV // 256
    high_blocks = E_DEV // 128 + 1
    block_count = jax.random.randint(base_key, (BATCHES, SHARDS), low_blocks, high_blocks)
    full_shard = jax.random.randint(jax.random.fold_in(base_key, 1), (BATCHES, 1), 0, SHARDS)
    shard_ids = jnp.arange(SHARDS, dtype=jnp.int32)[None, :]
    block_count = jnp.where(shard_ids == full_shard, E_DEV // 128, block_count)
    return (block_count * 128).astype(jnp.int32)


def draw_edge_count(key, part):
    return edge_counts(key)


def draw_triplet_in(key, part):
    counts = edge_counts(key)
    slot_ids = jnp.arange(SHARDS * TRI_DEV, dtype=jnp.int32)
    owner_ids = slot_ids % TRI_DEV // CAP
    limit_rows = counts[:, owner_ids]
    raw_bits = jax.random.randint(jax.random.fold_in(key, 23), (BATCHES, SHARDS * TRI_DEV), 0, 1 << 30)
    picked = raw_bits % limit_rows
    first_slot = (slot_ids < TRI_DEV) & (slot_ids % CAP == 0)
    return jnp.where(first_slot[None, :], limit_rows - 1, picked).astype(jnp.int32)


def draw_triplet_out(key, part):
    counts = edge_counts(key)
    slot_ids = jnp.arange(SHARDS * TRI_DEV, dtype=jnp.int32)
    owner_ids = slot_ids // TRI_DEV
    limit_rows = counts[:, owner_ids]
    raw_bits = jax.random.randint(jax.random.fold_in(key, 37), (BATCHES, SHARDS * TRI_DEV), 0, 1 << 30)
    picked = raw_bits % limit_rows
    first_slot = slot_ids % TRI_DEV == 0
    return jnp.where(first_slot[None, :], limit_rows - 1, picked).astype(jnp.int32)


def level_of(rng, dims, pieces, smallest, high):
    loudness, own = 1.0, jax.random.fold_in(rng, 6)
    for axis_at, parts in pieces:
        steps = jnp.exp(jax.random.uniform(jax.random.fold_in(own, axis_at), (parts,), jnp.float32, smallest / len(pieces), high / len(pieces)))
        loudness = loudness * jnp.repeat(steps, dims[axis_at] // parts).reshape([-1 if axis == axis_at else 1 for axis in range(len(dims))])
    return loudness


def normal_values(rng, shape, scale, limit, split=(), held_as=jnp.bfloat16):
    result = scale * jax.random.normal(rng, shape, jnp.float32)
    if split:
        result = result * level_of(rng, shape, split, -0.22, 0.18)
    return jnp.clip(result, -limit, limit).astype(held_as)


def setup_inputs(seed: int = 0) -> dict:
    keys = jax.random.split(jax.random.key(seed), 13)
    edge_state = normal_values(keys[0], (BATCHES, EDGES, H), 1.0, 6.0, ((0, 4), (1, 64)))
    cotangent = normal_values(keys[1], (BATCHES, EDGES, H), 1.0, 6.0, ((0, 4), (1, 64)))
    edge_count = draw_edge_count(jax.random.fold_in(keys[12], 71), 0)
    triplet_basis = normal_values(keys[3], (BATCHES, NB, TRIPLETS), 1.0, 6.0, ((0, 4), (2, 64)))
    triplet_in = draw_triplet_in(jax.random.fold_in(keys[12], 71), 0)
    triplet_out = draw_triplet_out(jax.random.fold_in(keys[12], 71), 0)
    down_weight = normal_values(keys[6], (H, K), H ** -0.5, 0.25)
    basis_weight = normal_values(keys[7], (NB, K), NB ** -0.5, 1.5)
    bilinear_weight = normal_values(keys[8], (K, K), K ** -0.5, 0.75)
    up_weight = normal_values(keys[9], (K, H), K ** -0.5, 0.75)
    first_weight = normal_values(keys[10], (H, H), H ** -0.5, 0.25)
    second_weight = normal_values(keys[11], (H, H), H ** -0.5, 0.25)
    return dict(edge_state=edge_state, cotangent=cotangent, edge_count=edge_count, triplet_basis=triplet_basis, triplet_in=triplet_in, triplet_out=triplet_out, down_weight=down_weight, basis_weight=basis_weight, bilinear_weight=bilinear_weight, up_weight=up_weight, first_weight=first_weight, second_weight=second_weight)


HALF = 0.7071067811865476

def silu_slope(argument):
    logistic = jax.nn.sigmoid(argument)
    return logistic * (1.0 + argument * (1.0 - logistic))

def contract(left, right, left_dim, right_dim):
    return lax.dot_general(left, right, (((left_dim,), (right_dim,)), ((), ())), preferred_element_type=jnp.float32)

def one_batch(edge_state, cotangent, counts, triplet_basis, triplet_in, triplet_out, down_weight, basis_weight, bilinear_weight, up_weight, first_weight, second_weight):
    edge_ids = jnp.arange(EDGES, dtype=jnp.int32)
    live_mask = (edge_ids % E_DEV < counts[edge_ids // E_DEV]).astype(jnp.float32)
    slot_ids = jnp.arange(TRIPLETS, dtype=jnp.int32)
    in_edge = slot_ids % TRI_DEV // CAP * E_DEV + triplet_in
    out_edge = slot_ids // TRI_DEV * E_DEV + triplet_out
    pre_down = contract(down_weight, edge_state, 0, 1)
    down_rows = jax.nn.silu(pre_down).astype(jnp.bfloat16)
    tri_coef = contract(basis_weight, triplet_basis, 0, 0)
    fetched = jnp.take(down_rows, in_edge, axis=1)
    message = tri_coef * fetched.astype(jnp.float32)
    gathered = jnp.zeros((K, EDGES), jnp.float32).at[:, out_edge].add(message).astype(jnp.bfloat16)
    mixed_rows = contract(bilinear_weight, gathered, 0, 0).astype(jnp.bfloat16)
    pre_up = contract(mixed_rows, up_weight, 0, 0)
    summed = edge_state.astype(jnp.float32) + jax.nn.silu(pre_up)
    summed_half = summed.astype(jnp.bfloat16)
    pre_first = jnp.dot(summed_half, first_weight, preferred_element_type=jnp.float32)
    first_rows = jax.nn.silu(pre_first).astype(jnp.bfloat16)
    pre_second = jnp.dot(first_rows, second_weight, preferred_element_type=jnp.float32)
    back_top = cotangent.astype(jnp.float32) * live_mask[:, None] * HALF
    back_second = (back_top * silu_slope(pre_second)).astype(jnp.bfloat16)
    back_first = (contract(back_second, second_weight, 1, 1) * silu_slope(pre_first)).astype(jnp.bfloat16)
    back_summed = back_top + contract(back_first, first_weight, 1, 1)
    back_up = (back_summed * silu_slope(pre_up)).astype(jnp.bfloat16)
    back_mixed = contract(up_weight, back_up, 1, 1).astype(jnp.bfloat16)
    back_gathered = contract(bilinear_weight, back_mixed, 1, 0)
    back_message = jnp.take(back_gathered, out_edge, axis=1)
    back_coef = (back_message * fetched.astype(jnp.float32)).astype(jnp.bfloat16)
    back_down = jnp.zeros((K, EDGES), jnp.float32).at[:, in_edge].add(back_message * tri_coef)
    back_pre = (back_down * silu_slope(pre_down)).astype(jnp.bfloat16)
    edge_grad = (back_summed + contract(back_pre, down_weight, 0, 1)).astype(jnp.bfloat16)
    totals = (contract(edge_state, back_pre, 0, 1), contract(triplet_basis, back_coef, 1, 1), contract(gathered, back_mixed, 1, 1), contract(mixed_rows, back_up, 1, 0), contract(summed_half, back_first, 0, 0), contract(first_rows, back_second, 0, 0))
    return (edge_grad, totals)

def reference(edge_state, cotangent, edge_count, triplet_basis, triplet_in, triplet_out, down_weight, basis_weight, bilinear_weight, up_weight, first_weight, second_weight):
    grads = []
    running = None
    for batch_id in range(BATCHES):
        edge_grad, totals = one_batch(edge_state[batch_id], cotangent[batch_id], edge_count[batch_id], triplet_basis[batch_id], triplet_in[batch_id], triplet_out[batch_id], down_weight, basis_weight, bilinear_weight, up_weight, first_weight, second_weight)
        grads.append(edge_grad)
        if running is None:
            running = totals
        else:
            running = tuple((old + new for old, new in zip(running, totals)))
    grad_scale = 1.0 / math.sqrt(BATCHES * EDGES)
    return (jnp.stack(grads), running[0] * grad_scale, running[1] * grad_scale, running[2] * grad_scale, running[3] * grad_scale, running[4] * grad_scale, running[5] * grad_scale)
```

```python
import functools
import math

import jax
import jax.numpy as jnp
from jax import lax
from jax.experimental import pallas as pl
from jax.experimental.pallas import tpu as pltpu
from jax.sharding import PartitionSpec as P

HALF = 0.7071067811865476
LOW = 256
MESH = pl.DeviceIdType.MESH
F32 = jnp.float32
BF16 = jnp.bfloat16
VMEM_LIMIT = 60 * 1024 * 1024


def silu_slope(argument):
    logistic = jax.nn.sigmoid(argument)
    return logistic * (1.0 + argument * (1.0 - logistic))


def contract(left, right, left_dim, right_dim):
    return lax.dot_general(
        left, right, (((left_dim,), (right_dim,)), ((), ())), preferred_element_type=jnp.float32
    )


def low_hot(low, width):
    rows = lax.broadcasted_iota(jnp.int32, (LOW, width), 0)
    return jnp.where(rows == low, 1.0, 0.0).astype(BF16)


def pick(table, index, narrow):
    width = index.shape[1]
    high = table.shape[0] // narrow
    hot = low_hot(index & (LOW - 1), width)
    upper = index >> 8
    wide = jnp.dot(table, hot, preferred_element_type=F32)
    out = wide[:narrow]
    for h in range(1, high):
        out = jnp.where(upper == h, wide[h * narrow : (h + 1) * narrow], out)
    return out


def spread(value, index, high):
    hot = low_hot(index & (LOW - 1), index.shape[1])
    upper = index >> 8
    parts = [jnp.where(upper == h, value, 0.0).astype(BF16) for h in range(high)]
    return contract(jnp.concatenate(parts, axis=0), hot, 1, 1)


def serve_kernel(table_ref, index_ref, out_ref):
    narrow = out_ref.shape[1]
    table = table_ref[...]

    @pl.loop(0, index_ref.shape[0])
    def _(i):
        got = pick(table, index_ref[i], narrow).astype(BF16)
        out_ref[2 * i] = got[:, :128]
        out_ref[2 * i + 1] = got[:, 128:]


def coef_of(weight, basis):
    return contract(weight, basis, 0, 0)


def pair_of(ref, i):
    return jnp.concatenate([ref[2 * i], ref[2 * i + 1]], axis=1).astype(F32)


def gather_kernel(fetched_ref, basis_ref, index_ref, weight_ref, out_ref, acc_ref):
    narrow = fetched_ref.shape[1]
    high = acc_ref.shape[0] // narrow
    acc_ref[...] = jnp.zeros_like(acc_ref)

    @pl.loop(0, index_ref.shape[0])
    def _(i):
        columns = pl.ds(pl.multiple_of(i * LOW, LOW), LOW)
        coef = coef_of(weight_ref[...], basis_ref[:, columns])
        message = coef * pair_of(fetched_ref, i)
        acc_ref[...] += spread(message, index_ref[i], high)

    for h in range(high):
        out_ref[:, h * LOW : (h + 1) * LOW] = acc_ref[h * narrow : (h + 1) * narrow].astype(BF16)


def back_kernel(table_ref, fetched_ref, basis_ref, index_ref, weight_ref, out_ref, grad_ref):
    narrow = fetched_ref.shape[1]
    table = table_ref[...]
    grad_ref[...] = jnp.zeros_like(grad_ref)

    @pl.loop(0, index_ref.shape[0])
    def _(i):
        columns = pl.ds(pl.multiple_of(i * LOW, LOW), LOW)
        basis = basis_ref[:, columns]
        got = pick(table, index_ref[i], narrow)
        back_coef = (got * pair_of(fetched_ref, i)).astype(BF16)
        grad_ref[...] += contract(basis, back_coef, 1, 1)
        back = (got * coef_of(weight_ref[...], basis)).astype(BF16)
        out_ref[2 * i] = back[:, :128]
        out_ref[2 * i + 1] = back[:, 128:]


def return_kernel(returned_ref, index_ref, pre_ref, out_ref, acc_ref):
    narrow = returned_ref.shape[1]
    high = acc_ref.shape[0] // narrow
    acc_ref[...] = jnp.zeros_like(acc_ref)

    @pl.loop(0, index_ref.shape[0])
    def _(i):
        acc_ref[...] += spread(pair_of(returned_ref, i), index_ref[i], high)

    for h in range(high):
        columns = slice(h * LOW, (h + 1) * LOW)
        back = acc_ref[h * narrow : (h + 1) * narrow]
        out_ref[:, columns] = (back * silu_slope(pre_ref[:, columns])).astype(BF16)


def local_call(kernel, out_shape, *args, scratch=()):
    vmem = pl.BlockSpec(memory_space=pltpu.VMEM)
    return pl.pallas_call(
        kernel,
        out_shape=out_shape,
        in_specs=[vmem] * len(args),
        out_specs=jax.tree.map(lambda _: vmem, out_shape),
        scratch_shapes=list(scratch),
        compiler_params=pltpu.CompilerParams(vmem_limit_bytes=VMEM_LIMIT),
    )(*args)


def reduce_kernel(scale, first_ref, second_ref, small_ref, first_out, second_out, small_out,
                  send, got_a, part, got_b, held, sem_a, sem_ar, sem_b, sem_br, sem_c, sem_cr):
    wide = first_ref.shape[1]
    rows = send.shape[1]
    group = send.shape[0]
    depth = got_b.shape[0]
    y = lax.axis_index("dp")
    g = lax.axis_index("graph")
    z, x, c = g // 8, (g // 2) % 4, g % 2
    mine = y * 8 + x * 2 + c

    def member(j):
        py = (y + j // 8) % 4
        px = (x + (j // 2) % 4) % 4
        pc = (c + j % 2) % 2
        return (py, z * 8 + px * 2 + pc), py * 8 + px * 2 + pc

    def along(j):
        pz = (z + j) % depth
        return (y, pz * 8 + x * 2 + c)

    barrier = pltpu.get_barrier_semaphore()

    @pl.loop(1, group)
    def _(j):
        pl.semaphore_signal(barrier, inc=1, device_id=member(j)[0], device_id_type=MESH)

    @pl.loop(1, depth)
    def _(j):
        pl.semaphore_signal(barrier, inc=1, device_id=along(j), device_id_type=MESH)

    @pl.loop(0, group)
    def _(m):
        at = pl.ds(pl.multiple_of(m * rows, rows), rows)
        send[m, :, :wide] = first_ref[at, :].astype(BF16)
        send[m, :, wide : 2 * wide] = second_ref[at, :].astype(BF16)
        send[m, :, 2 * wide :] = small_ref[at, :].astype(BF16)

    pl.semaphore_wait(barrier, group - 1 + depth - 1)

    def copy_a(j):
        device, index = member(j)
        return pltpu.make_async_remote_copy(
            src_ref=send.at[index], dst_ref=got_a.at[j], send_sem=sem_a.at[j],
            recv_sem=sem_ar.at[j], device_id=device, device_id_type=MESH)

    def copy_b(j):
        return pltpu.make_async_remote_copy(
            src_ref=part, dst_ref=got_b.at[z], send_sem=sem_b.at[j],
            recv_sem=sem_br.at[j], device_id=along(j), device_id_type=MESH)

    def copy_c(j):
        device, _ = member(j)
        return pltpu.make_async_remote_copy(
            src_ref=held.at[mine], dst_ref=held.at[mine], send_sem=sem_c.at[j],
            recv_sem=sem_cr.at[j], device_id=device, device_id_type=MESH)

    @pl.loop(1, group)
    def _(j):
        copy_a(j).start()

    got_a[0] = send[mine]

    @pl.loop(1, group)
    def _(j):
        copy_a(j).wait()

    total = got_a[0].astype(F32)
    for j in range(1, group):
        total = total + got_a[j].astype(F32)
    part[...] = total.astype(BF16)
    got_b[z] = total.astype(BF16)

    @pl.loop(1, depth)
    def _(j):
        copy_b(j).start()

    @pl.loop(1, depth)
    def _(j):
        copy_b(j).wait()

    total = got_b[0].astype(F32)
    for j in range(1, depth):
        total = total + got_b[j].astype(F32)
    held[mine] = (total * scale).astype(BF16)

    @pl.loop(1, group)
    def _(j):
        copy_c(j).start()

    @pl.loop(1, group)
    def _(j):
        copy_c(j).wait()

    @pl.loop(0, group)
    def _(m):
        at = pl.ds(pl.multiple_of(m * rows, rows), rows)
        first_out[at, :] = held[m, :, :wide].astype(F32)
        second_out[at, :] = held[m, :, wide : 2 * wide].astype(F32)
        small_out[at, :] = held[m, :, 2 * wide :].astype(F32)


def reduce_all(scale, first, second, small):
    group, depth = 32, 8
    rows = first.shape[0] // group
    width = 2 * first.shape[1] + small.shape[1]
    vmem = pl.BlockSpec(memory_space=pltpu.VMEM)
    dma = pltpu.SemaphoreType.DMA
    return pl.pallas_call(
        functools.partial(reduce_kernel, scale),
        out_shape=(
            jax.ShapeDtypeStruct(first.shape, F32),
            jax.ShapeDtypeStruct(second.shape, F32),
            jax.ShapeDtypeStruct(small.shape, F32),
        ),
        in_specs=[vmem] * 3,
        out_specs=(vmem,) * 3,
        scratch_shapes=[
            pltpu.VMEM((group, rows, width), BF16),
            pltpu.VMEM((group, rows, width), BF16),
            pltpu.VMEM((rows, width), BF16),
            pltpu.VMEM((depth, rows, width), BF16),
            pltpu.VMEM((group, rows, width), BF16),
            dma((group,)), dma((group,)), dma((depth,)), dma((depth,)), dma((group,)), dma((group,)),
        ],
        compiler_params=pltpu.CompilerParams(
            collective_id=0, has_side_effects=True, vmem_limit_bytes=VMEM_LIMIT),
    )(first, second, small)


def local(
    edge_state,
    cotangent,
    edge_count,
    triplet_basis,
    triplet_in,
    triplet_out,
    down_weight,
    basis_weight,
    bilinear_weight,
    up_weight,
    first_weight,
    second_weight,
):
    edge_rows = edge_state[0]
    row_count, wide = edge_rows.shape
    shards = lax.axis_size("graph")
    narrow = down_weight.shape[1]
    high = row_count // LOW
    in_local = triplet_in[0]
    tri_rows = in_local.shape[0]
    slot_count = tri_rows // shards
    steps = tri_rows // LOW
    basis = triplet_basis[0]
    out_index = triplet_out[0].reshape(steps, 1, LOW)
    live_mask = (jnp.arange(row_count, dtype=jnp.int32) < edge_count[0, 0]).astype(jnp.float32)
    wanted = lax.all_to_all(
        in_local.reshape(shards, slot_count), "graph", split_axis=0, concat_axis=0, tiled=True
    ).reshape(steps, 1, LOW)
    pre_down = contract(down_weight, edge_rows, 0, 1)
    down_rows = jax.nn.silu(pre_down).astype(jnp.bfloat16)
    block = jax.ShapeDtypeStruct((shards, narrow, slot_count), BF16)

    def to_table(rows):
        return rows.reshape(narrow, high, LOW).transpose(1, 0, 2).reshape(high * narrow, LOW)

    served = local_call(serve_kernel, block, to_table(down_rows), wanted)
    fetched = lax.all_to_all(served, "graph", split_axis=0, concat_axis=0, tiled=True)
    acc = pltpu.VMEM((high * narrow, LOW), F32)
    gathered = local_call(
        gather_kernel, jax.ShapeDtypeStruct((narrow, row_count), BF16),
        fetched, basis, out_index, basis_weight, scratch=(acc,))
    mixed_rows = contract(bilinear_weight, gathered, 0, 0).astype(jnp.bfloat16)
    pre_up = contract(mixed_rows, up_weight, 0, 0)
    summed = edge_rows.astype(jnp.float32) + jax.nn.silu(pre_up)
    summed_half = summed.astype(jnp.bfloat16)
    pre_first = jnp.dot(summed_half, first_weight, preferred_element_type=jnp.float32)
    first_rows = jax.nn.silu(pre_first).astype(jnp.bfloat16)
    pre_second = jnp.dot(first_rows, second_weight, preferred_element_type=jnp.float32)
    back_top = cotangent[0].astype(jnp.float32) * live_mask[:, None] * HALF
    back_second = (back_top * silu_slope(pre_second)).astype(jnp.bfloat16)
    back_first = (contract(back_second, second_weight, 1, 1) * silu_slope(pre_first)).astype(
        jnp.bfloat16
    )
    first_grad = contract(summed_half, back_first, 0, 0)
    second_grad = contract(first_rows, back_second, 0, 0)
    back_summed = back_top + contract(back_first, first_weight, 1, 1)
    back_up = (back_summed * silu_slope(pre_up)).astype(jnp.bfloat16)
    back_mixed = contract(up_weight, back_up, 1, 1).astype(jnp.bfloat16)
    back_gathered = contract(bilinear_weight, back_mixed, 1, 0)
    back_fetched, basis_grad = local_call(
        back_kernel, (block, jax.ShapeDtypeStruct(basis_weight.shape, F32)),
        to_table(back_gathered.astype(BF16)), fetched, basis, out_index, basis_weight)
    returned = lax.all_to_all(back_fetched, "graph", split_axis=0, concat_axis=0, tiled=True)
    back_pre = local_call(
        return_kernel, jax.ShapeDtypeStruct((narrow, row_count), BF16),
        returned, wanted, pre_down, scratch=(acc,))
    up_grad = contract(back_up, mixed_rows, 0, 1)
    bilinear_grad = contract(gathered, back_mixed, 1, 1)
    down_grad = contract(edge_rows, back_pre, 0, 1)
    edge_grad = (back_summed + contract(back_pre, down_weight, 0, 1)).astype(jnp.bfloat16)
    corner = jnp.concatenate([bilinear_grad, basis_grad], axis=0)
    corner = jnp.pad(corner, ((0, wide - corner.shape[0]), (0, 128 - narrow)))
    small = jnp.concatenate([down_grad, up_grad, corner], axis=1)
    grad_scale = 1.0 / math.sqrt(lax.axis_size("dp") * shards * row_count)
    first_grad, second_grad, small = reduce_all(grad_scale, first_grad, second_grad, small)
    return (
        edge_grad[None],
        small[:, :narrow],
        small[narrow : narrow + basis_weight.shape[0], 2 * narrow : 3 * narrow],
        small[:narrow, 2 * narrow : 3 * narrow],
        small[:, narrow : 2 * narrow].T,
        first_grad,
        second_grad,
    )


def solution(mesh):
    in_specs = (
        P("dp", "graph", None),
        P("dp", "graph", None),
        P("dp", "graph"),
        P("dp", None, "graph"),
        P("dp", "graph"),
        P("dp", "graph"),
        P(),
        P(),
        P(),
        P(),
        P(),
        P(),
    )
    out_specs = (P("dp", "graph", None), P(), P(), P(), P(), P(), P())
    return jax.shard_map(local, mesh=mesh, in_specs=in_specs, out_specs=out_specs, check_vma=False)
```

```python
import functools
import math

import jax
import jax.numpy as jnp
from jax import lax
from jax.experimental import pallas as pl
from jax.experimental.pallas import tpu as pltpu
from jax.sharding import PartitionSpec as P

HALF = 0.7071067811865476
LOW = 256
MESH = pl.DeviceIdType.MESH
F32 = jnp.float32
BF16 = jnp.bfloat16
VMEM_LIMIT = 60 * 1024 * 1024


def silu_slope(argument):
    logistic = jax.nn.sigmoid(argument)
    return logistic * (1.0 + argument * (1.0 - logistic))


def contract(left, right, left_dim, right_dim):
    return lax.dot_general(
        left, right, (((left_dim,), (right_dim,)), ((), ())), preferred_element_type=jnp.float32
    )


def low_hot(low, width):
    rows = lax.broadcasted_iota(jnp.int32, (LOW, width), 0)
    return jnp.where(rows == low, 1.0, 0.0).astype(BF16)


def pick(table, index, narrow):
    width = index.shape[1]
    high = table.shape[0] // narrow
    hot = low_hot(index & (LOW - 1), width)
    upper = index >> 8
    wide = jnp.dot(table, hot, preferred_element_type=F32)
    out = wide[:narrow]
    for h in range(1, high):
        out = jnp.where(upper == h, wide[h * narrow : (h + 1) * narrow], out)
    return out


def spread(value, index, high):
    hot = low_hot(index & (LOW - 1), index.shape[1])
    upper = index >> 8
    parts = [jnp.where(upper == h, value, 0.0).astype(BF16) for h in range(high)]
    return contract(jnp.concatenate(parts, axis=0), hot, 1, 1)


def coef_of(weight, basis):
    return contract(weight, basis, 0, 0)


def place():
    g = lax.axis_index("graph")
    return lax.axis_index("dp"), g // 8, (g // 2) % 4, g % 2


def chip_at(k, a, sign):
    _, z, x, _ = place()
    dz, dx = (k + 2 * a) % 8, a
    if sign < 0:
        dz, dx = 8 - dz, 4 - dx
    return (z + dz) % 8 * 4 + (x + dx) % 4


def for_peers(k, a, sign, fn):
    q = chip_at(k, a, sign)
    if a:
        fn(2 * q)
        fn(2 * q + 1)
        return

    @pl.when(k > 0)
    def _():
        fn(2 * q)
        fn(2 * q + 1)

    @pl.when(k == 0)
    def _():
        g = lax.axis_index("graph")
        fn(g + 1 - 2 * (g % 2))


def row_of(ref, k, sign):
    return jnp.concatenate([ref[chip_at(k, a, sign)] for a in range(4)], axis=1)


def pairs_of(ref, k, sign):
    chips = [chip_at(k, a, sign) for a in range(4)]
    return jnp.concatenate([ref[2 * q + c] for q in chips for c in range(2)], axis=1)


def columns_of(ref, k, sign):
    chips = [chip_at(k, a, sign) for a in range(4)]
    return jnp.concatenate(
        [ref[:, pl.ds(pl.multiple_of(q * LOW, LOW), LOW)] for q in chips], axis=1)


def put_pairs(ref, k, sign, value):
    for a in range(4):
        q = chip_at(k, a, sign)
        for c in range(2):
            at = (2 * a + c) * 128
            ref[2 * q + c] = value[:, at : at + 128]


def exchange(src, dst, send_sem, recv_sem):
    y = lax.axis_index("dp")
    g = lax.axis_index("graph")

    def out(p):
        return pltpu.make_async_remote_copy(
            src_ref=src.at[p], dst_ref=dst.at[g], send_sem=send_sem.at[p],
            recv_sem=recv_sem.at[g], device_id=(y, p), device_id_type=MESH)

    def back(p):
        return pltpu.make_async_remote_copy(
            src_ref=src.at[p], dst_ref=dst.at[p], send_sem=send_sem.at[p],
            recv_sem=recv_sem.at[p], device_id=(y, p), device_id_type=MESH)

    return out, back


def forward_kernel(edge_ref, in_ref, out_ref, basis_ref, down_ref, weight_ref,
                   fetched, wanted, pre_ref, gathered_ref,
                   table, outbox, acc, is_sem, ir_sem, rs_sem, rr_sem):
    shards, narrow = fetched.shape[:2]
    high = table.shape[0] // narrow
    y = lax.axis_index("dp")
    g = lax.axis_index("graph")
    barrier = pltpu.get_barrier_semaphore()

    @pl.loop(1, shards)
    def _(j):
        pl.semaphore_signal(barrier, inc=1, device_id=(y, (g + j) % shards), device_id_type=MESH)

    wanted[g] = in_ref[g]
    for h in range(high):
        pre = jnp.dot(edge_ref[h * LOW : (h + 1) * LOW], down_ref[...], preferred_element_type=F32)
        pre = pre.T
        pre_ref[:, h * LOW : (h + 1) * LOW] = pre
        table[h * narrow : (h + 1) * narrow] = (pre * jax.nn.sigmoid(pre)).astype(BF16)
    acc[...] = jnp.zeros_like(acc)
    pl.semaphore_wait(barrier, shards - 1)
    ask, asked = exchange(in_ref, wanted, is_sem, ir_sem)
    give, given = exchange(outbox, fetched, rs_sem, rr_sem)

    @pl.loop(0, 8)
    def _(k):
        for a in range(4):
            for_peers(k, a, -1, lambda p: ask(p).start())

    @pl.loop(0, 8)
    def _(k):
        for a in range(4):
            for_peers(k, a, 1, lambda p: asked(p).wait_recv())
        index = pairs_of(wanted, k, 1)
        put_pairs(outbox, k, 1, pick(table[...], index, narrow).astype(BF16))
        for a in range(4):
            for_peers(k, a, 1, lambda p: give(p).start())

    fetched[g] = outbox[g]

    @pl.loop(0, 8)
    def _(k):
        for a in range(4):
            for_peers(k, a, -1, lambda p: given(p).wait_recv())
        coef = coef_of(weight_ref[...], columns_of(basis_ref, k, -1))
        message = coef * pairs_of(fetched, k, -1).astype(F32)
        acc[...] += spread(message, row_of(out_ref, k, -1), high)

    for h in range(high):
        gathered_ref[:, h * LOW : (h + 1) * LOW] = acc[h * narrow : (h + 1) * narrow].astype(BF16)

    @pl.loop(1, shards)
    def _(j):
        p = (g + j) % shards
        ask(p).wait_send()
        give(p).wait_send()


VM = pl.BlockSpec(memory_space=pltpu.VMEM)


def forward(edge_rows, in_index, out_index, basis, down_weight, basis_weight):
    shards, _, slots = in_index.shape
    rows = edge_rows.shape[0]
    narrow = down_weight.shape[1]
    high = rows // LOW
    dma = pltpu.SemaphoreType.DMA
    return pl.pallas_call(
        forward_kernel,
        out_shape=(
            jax.ShapeDtypeStruct((shards, narrow, slots), BF16),
            jax.ShapeDtypeStruct(in_index.shape, jnp.int32),
            jax.ShapeDtypeStruct((narrow, rows), F32),
            jax.ShapeDtypeStruct((narrow, rows), BF16),
        ),
        in_specs=[VM] * 6,
        out_specs=(VM,) * 4,
        scratch_shapes=[
            pltpu.VMEM((high * narrow, LOW), BF16),
            pltpu.VMEM((shards, narrow, slots), BF16),
            pltpu.VMEM((high * narrow, LOW), F32),
            dma((shards,)), dma((shards,)), dma((shards,)), dma((shards,)),
        ],
        compiler_params=pltpu.CompilerParams(
            collective_id=1, has_side_effects=True, vmem_limit_bytes=VMEM_LIMIT),
        name="forward_exchange",
    )(edge_rows, in_index, out_index, basis, down_weight, basis_weight)


def slope_from(value, logistic):
    return logistic * (1.0 + value * (1.0 - logistic))


def dense_kernel(edge_ref, cot_ref, count_ref, gathered_ref, bil_ref, up_ref, w1_ref, w2_ref,
                 summed_ref, table_ref, first_ref, second_ref, upg_ref, bilg_ref):
    narrow = gathered_ref.shape[0]
    block = LOW
    steps = edge_ref.shape[0] // block
    first_ref[...] = jnp.zeros_like(first_ref)
    second_ref[...] = jnp.zeros_like(second_ref)
    upg_ref[...] = jnp.zeros_like(upg_ref)
    bilg_ref[...] = jnp.zeros_like(bilg_ref)
    count = count_ref[0, 0]

    @pl.loop(0, steps)
    def _(i):
        at = pl.ds(pl.multiple_of(i * block, block), block)
        gat = gathered_ref[:, at]
        mixed = contract(bil_ref[...], gat, 0, 0).astype(BF16)
        pre_up = contract(mixed, up_ref[...], 0, 0)
        s_up = jax.nn.sigmoid(pre_up)
        half = (edge_ref[at, :].astype(F32) + pre_up * s_up).astype(BF16)
        pre_first = jnp.dot(half, w1_ref[...], preferred_element_type=F32)
        s_first = jax.nn.sigmoid(pre_first)
        rows1 = (pre_first * s_first).astype(BF16)
        pre_second = jnp.dot(rows1, w2_ref[...], preferred_element_type=F32)
        live = lax.broadcasted_iota(jnp.int32, (block, 1), 0) + i * block < count
        top = cot_ref[at, :].astype(F32) * jnp.where(live, HALF, 0.0)
        back2 = (top * slope_from(pre_second, jax.nn.sigmoid(pre_second))).astype(BF16)
        back1 = contract(back2, w2_ref[...], 1, 1) * slope_from(pre_first, s_first)
        back1 = back1.astype(BF16)
        total = top + contract(back1, w1_ref[...], 1, 1)
        summed_ref[at, :] = total
        back_up = (total * slope_from(pre_up, s_up)).astype(BF16)
        back_mixed = contract(up_ref[...], back_up, 1, 1).astype(BF16)
        where = pl.ds(pl.multiple_of(i * narrow, narrow), narrow)
        table_ref[where, :] = jnp.dot(
            bil_ref[...], back_mixed, preferred_element_type=F32).astype(BF16)
        first_ref[...] += contract(half, back1, 0, 0)
        second_ref[...] += contract(rows1, back2, 0, 0)
        upg_ref[...] += jnp.dot(mixed, back_up, preferred_element_type=F32)
        bilg_ref[...] += contract(gat, back_mixed, 1, 1)


def dense(edge_rows, cotangent, count, gathered, bilinear, up, first, second):
    rows, wide = edge_rows.shape
    narrow = gathered.shape[0]
    shape = jax.ShapeDtypeStruct
    return pl.pallas_call(
        dense_kernel,
        out_shape=(
            shape((rows, wide), F32),
            shape((rows // LOW * narrow, LOW), BF16),
            shape((wide, wide), F32),
            shape((wide, wide), F32),
            shape((narrow, wide), F32),
            shape((narrow, narrow), F32),
        ),
        in_specs=[VM, VM, pl.BlockSpec(memory_space=pltpu.SMEM)] + [VM] * 5,
        out_specs=(VM,) * 6,
        compiler_params=pltpu.CompilerParams(vmem_limit_bytes=VMEM_LIMIT),
        name="dense",
    )(edge_rows, cotangent, count, gathered, bilinear, up, first, second)


def pair_of(ref, i):
    return jnp.concatenate([ref[8 * i + a] for a in range(8)], axis=1).astype(F32)


def back_kernel(table_ref, fetched_ref, basis_ref, index_ref, weight_ref, out_ref, grad_ref):
    narrow = fetched_ref.shape[1]
    table = table_ref[...]
    width = index_ref.shape[2]
    grad_ref[...] = jnp.zeros_like(grad_ref)

    @pl.loop(0, index_ref.shape[0])
    def _(i):
        columns = pl.ds(pl.multiple_of(i * width, width), width)
        basis = basis_ref[:, columns]
        got = pick(table, index_ref[i], narrow)
        back_coef = (got * pair_of(fetched_ref, i)).astype(BF16)
        grad_ref[...] += contract(basis, back_coef, 1, 1)
        back = (got * coef_of(weight_ref[...], basis)).astype(BF16)
        for a in range(8):
            out_ref[8 * i + a] = back[:, a * 128 : (a + 1) * 128]


def return_kernel(returned_ref, index_ref, pre_ref, out_ref, acc_ref):
    narrow = returned_ref.shape[1]
    high = acc_ref.shape[0] // narrow
    acc_ref[...] = jnp.zeros_like(acc_ref)

    @pl.loop(0, index_ref.shape[0])
    def _(i):
        acc_ref[...] += spread(pair_of(returned_ref, i), index_ref[i], high)

    for h in range(high):
        columns = slice(h * LOW, (h + 1) * LOW)
        back = acc_ref[h * narrow : (h + 1) * narrow]
        out_ref[:, columns] = (back * silu_slope(pre_ref[:, columns])).astype(BF16)


def local_call(kernel, out_shape, *args, scratch=()):
    return pl.pallas_call(
        kernel,
        out_shape=out_shape,
        in_specs=[VM] * len(args),
        out_specs=jax.tree.map(lambda _: VM, out_shape),
        scratch_shapes=list(scratch),
        compiler_params=pltpu.CompilerParams(vmem_limit_bytes=VMEM_LIMIT),
    )(*args)


def reduce_kernel(scale, first_ref, second_ref, small_ref, first_out, second_out, small_out,
                  send, got_a, part, got_b, held, sem_a, sem_ar, sem_b, sem_br, sem_c, sem_cr):
    wide = first_ref.shape[1]
    rows = send.shape[1]
    group = send.shape[0]
    depth = got_b.shape[0]
    y = lax.axis_index("dp")
    g = lax.axis_index("graph")
    z, x, c = g // 8, (g // 2) % 4, g % 2
    mine = y * 8 + x * 2 + c

    def member(j):
        py = (y + j // 8) % 4
        px = (x + (j // 2) % 4) % 4
        pc = (c + j % 2) % 2
        return (py, z * 8 + px * 2 + pc), py * 8 + px * 2 + pc

    def along(j):
        pz = (z + j) % depth
        return (y, pz * 8 + x * 2 + c)

    barrier = pltpu.get_barrier_semaphore()

    @pl.loop(1, group)
    def _(j):
        pl.semaphore_signal(barrier, inc=1, device_id=member(j)[0], device_id_type=MESH)

    @pl.loop(1, depth)
    def _(j):
        pl.semaphore_signal(barrier, inc=1, device_id=along(j), device_id_type=MESH)

    @pl.loop(0, group)
    def _(m):
        at = pl.ds(pl.multiple_of(m * rows, rows), rows)
        send[m, :, :wide] = first_ref[at, :].astype(BF16)
        send[m, :, wide : 2 * wide] = second_ref[at, :].astype(BF16)
        send[m, :, 2 * wide :] = small_ref[at, :].astype(BF16)

    pl.semaphore_wait(barrier, group - 1 + depth - 1)

    def copy_a(j):
        device, index = member(j)
        return pltpu.make_async_remote_copy(
            src_ref=send.at[index], dst_ref=got_a.at[j], send_sem=sem_a.at[j],
            recv_sem=sem_ar.at[j], device_id=device, device_id_type=MESH)

    def copy_b(j):
        return pltpu.make_async_remote_copy(
            src_ref=part, dst_ref=got_b.at[z], send_sem=sem_b.at[j],
            recv_sem=sem_br.at[j], device_id=along(j), device_id_type=MESH)

    def copy_c(j):
        device, _ = member(j)
        return pltpu.make_async_remote_copy(
            src_ref=held.at[mine], dst_ref=held.at[mine], send_sem=sem_c.at[j],
            recv_sem=sem_cr.at[j], device_id=device, device_id_type=MESH)

    @pl.loop(1, group)
    def _(j):
        copy_a(j).start()

    got_a[0] = send[mine]

    @pl.loop(1, group)
    def _(j):
        copy_a(j).wait()

    total = got_a[0].astype(F32)
    for j in range(1, group):
        total = total + got_a[j].astype(F32)
    part[...] = total.astype(BF16)
    got_b[z] = total.astype(BF16)

    @pl.loop(1, depth)
    def _(j):
        copy_b(j).start()

    @pl.loop(1, depth)
    def _(j):
        copy_b(j).wait()

    total = got_b[0].astype(F32)
    for j in range(1, depth):
        total = total + got_b[j].astype(F32)
    held[mine] = (total * scale).astype(BF16)

    @pl.loop(1, group)
    def _(j):
        copy_c(j).start()

    @pl.loop(1, group)
    def _(j):
        copy_c(j).wait()

    @pl.loop(0, group)
    def _(m):
        at = pl.ds(pl.multiple_of(m * rows, rows), rows)
        first_out[at, :] = held[m, :, :wide].astype(F32)
        second_out[at, :] = held[m, :, wide : 2 * wide].astype(F32)
        small_out[at, :] = held[m, :, 2 * wide :].astype(F32)


def reduce_all(scale, first, second, small):
    group, depth = 32, 8
    rows = first.shape[0] // group
    width = 2 * first.shape[1] + small.shape[1]
    vmem = pl.BlockSpec(memory_space=pltpu.VMEM)
    dma = pltpu.SemaphoreType.DMA
    return pl.pallas_call(
        functools.partial(reduce_kernel, scale),
        out_shape=(
            jax.ShapeDtypeStruct(first.shape, F32),
            jax.ShapeDtypeStruct(second.shape, F32),
            jax.ShapeDtypeStruct(small.shape, F32),
        ),
        in_specs=[vmem] * 3,
        out_specs=(vmem,) * 3,
        scratch_shapes=[
            pltpu.VMEM((group, rows, width), BF16),
            pltpu.VMEM((group, rows, width), BF16),
            pltpu.VMEM((rows, width), BF16),
            pltpu.VMEM((depth, rows, width), BF16),
            pltpu.VMEM((group, rows, width), BF16),
            dma((group,)), dma((group,)), dma((depth,)), dma((depth,)), dma((group,)), dma((group,)),
        ],
        compiler_params=pltpu.CompilerParams(
            collective_id=0, has_side_effects=True, vmem_limit_bytes=VMEM_LIMIT),
    )(first, second, small)


def local(
    edge_state,
    cotangent,
    edge_count,
    triplet_basis,
    triplet_in,
    triplet_out,
    down_weight,
    basis_weight,
    bilinear_weight,
    up_weight,
    first_weight,
    second_weight,
):
    edge_rows = edge_state[0]
    row_count, wide = edge_rows.shape
    shards = lax.axis_size("graph")
    narrow = down_weight.shape[1]
    high = row_count // LOW
    tri_rows = triplet_in.shape[1]
    slot_count = tri_rows // shards
    basis = triplet_basis[0]
    out_index = triplet_out[0].reshape(tri_rows // LOW, 1, LOW)
    in_index = triplet_in[0].reshape(shards, 1, slot_count)
    fetched, wanted, pre_down, gathered = forward(
        edge_rows, in_index, out_index, basis, down_weight, basis_weight)
    back_summed, table, first_grad, second_grad, up_grad, bilinear_grad = dense(
        edge_rows, cotangent[0], edge_count, gathered, bilinear_weight, up_weight,
        first_weight, second_weight)
    block = jax.ShapeDtypeStruct((shards, narrow, slot_count), BF16)
    back_fetched, basis_grad = local_call(
        back_kernel, (block, jax.ShapeDtypeStruct(basis_weight.shape, F32)),
        table, fetched, basis, out_index.reshape(8, 1, 1024), basis_weight)
    returned = lax.all_to_all(back_fetched, "graph", split_axis=0, concat_axis=0, tiled=True)
    back_pre = local_call(
        return_kernel, jax.ShapeDtypeStruct((narrow, row_count), BF16),
        returned, wanted.reshape(8, 1, 1024), pre_down,
        scratch=(pltpu.VMEM((high * narrow, LOW), F32),))
    down_grad = contract(edge_rows, back_pre, 0, 1)
    edge_grad = (back_summed + contract(back_pre, down_weight, 0, 1)).astype(jnp.bfloat16)
    corner = jnp.concatenate([bilinear_grad, basis_grad], axis=0)
    corner = jnp.pad(corner, ((0, wide - corner.shape[0]), (0, 128 - narrow)))
    small = jnp.concatenate([down_grad, up_grad.T, corner], axis=1)
    grad_scale = 1.0 / math.sqrt(lax.axis_size("dp") * shards * row_count)
    first_grad, second_grad, small = reduce_all(grad_scale, first_grad, second_grad, small)
    return (
        edge_grad[None],
        small[:, :narrow],
        small[narrow : narrow + basis_weight.shape[0], 2 * narrow : 3 * narrow],
        small[:narrow, 2 * narrow : 3 * narrow],
        small[:, narrow : 2 * narrow].T,
        first_grad,
        second_grad,
    )


def solution(mesh):
    in_specs = (
        P("dp", "graph", None),
        P("dp", "graph", None),
        P("dp", "graph"),
        P("dp", None, "graph"),
        P("dp", "graph"),
        P("dp", "graph"),
        P(),
        P(),
        P(),
        P(),
        P(),
        P(),
    )
    out_specs = (P("dp", "graph", None), P(), P(), P(), P(), P(), P())
    return jax.shard_map(local, mesh=mesh, in_specs=in_specs, out_specs=out_specs, check_vma=False)
```

```python
import functools
import math

import jax
import jax.numpy as jnp
from jax import lax
from jax.experimental import pallas as pl
from jax.experimental.pallas import tpu as pltpu
from jax.sharding import PartitionSpec as P

HALF = 0.7071067811865476
LOW = 256
MESH = pl.DeviceIdType.MESH
F32 = jnp.float32
BF16 = jnp.bfloat16
VMEM_LIMIT = 60 * 1024 * 1024


def silu_slope(argument):
    logistic = jax.nn.sigmoid(argument)
    return logistic * (1.0 + argument * (1.0 - logistic))


def contract(left, right, left_dim, right_dim):
    return lax.dot_general(
        left, right, (((left_dim,), (right_dim,)), ((), ())), preferred_element_type=jnp.float32
    )


def low_hot(low, width):
    rows = lax.broadcasted_iota(jnp.int32, (LOW, width), 0)
    return jnp.where(rows == low, 1.0, 0.0).astype(BF16)


def pick(table, index, narrow):
    width = index.shape[1]
    high = table.shape[0] // narrow
    hot = low_hot(index & (LOW - 1), width)
    upper = index >> 8
    wide = jnp.dot(table, hot, preferred_element_type=F32)
    out = wide[:narrow]
    for h in range(1, high):
        out = jnp.where(upper == h, wide[h * narrow : (h + 1) * narrow], out)
    return out


def spread(value, index, high):
    hot = low_hot(index & (LOW - 1), index.shape[1])
    upper = index >> 8
    parts = [jnp.where(upper == h, value, 0.0).astype(BF16) for h in range(high)]
    return contract(jnp.concatenate(parts, axis=0), hot, 1, 1)


def coef_of(weight, basis):
    return contract(weight, basis, 0, 0)


def place():
    g = lax.axis_index("graph")
    return lax.axis_index("dp"), g // 8, (g // 2) % 4, g % 2


def chip_at(k, a, sign):
    _, z, x, _ = place()
    dz, dx = (k + 2 * a) % 8, a
    if sign < 0:
        dz, dx = 8 - dz, 4 - dx
    return (z + dz) % 8 * 4 + (x + dx) % 4


def for_peers(k, a, sign, fn):
    q = chip_at(k, a, sign)
    if a:
        fn(2 * q)
        fn(2 * q + 1)
        return

    @pl.when(k > 0)
    def _():
        fn(2 * q)
        fn(2 * q + 1)

    @pl.when(k == 0)
    def _():
        g = lax.axis_index("graph")
        fn(g + 1 - 2 * (g % 2))


def row_of(ref, k, sign):
    return jnp.concatenate([ref[chip_at(k, a, sign)] for a in range(4)], axis=1)


def pairs_of(ref, k, sign):
    chips = [chip_at(k, a, sign) for a in range(4)]
    return jnp.concatenate([ref[2 * q + c] for q in chips for c in range(2)], axis=1)


def columns_of(ref, k, sign):
    chips = [chip_at(k, a, sign) for a in range(4)]
    return jnp.concatenate(
        [ref[:, pl.ds(pl.multiple_of(q * LOW, LOW), LOW)] for q in chips], axis=1)


def put_pairs(ref, k, sign, value):
    for a in range(4):
        q = chip_at(k, a, sign)
        for c in range(2):
            at = (2 * a + c) * 128
            ref[2 * q + c] = value[:, at : at + 128]


def exchange(src, dst, send_sem, recv_sem):
    y = lax.axis_index("dp")
    g = lax.axis_index("graph")

    def out(p):
        return pltpu.make_async_remote_copy(
            src_ref=src.at[p], dst_ref=dst.at[g], send_sem=send_sem.at[p],
            recv_sem=recv_sem.at[g], device_id=(y, p), device_id_type=MESH)

    def back(p):
        return pltpu.make_async_remote_copy(
            src_ref=src.at[p], dst_ref=dst.at[p], send_sem=send_sem.at[p],
            recv_sem=recv_sem.at[p], device_id=(y, p), device_id_type=MESH)

    return out, back


def forward_kernel(edge_ref, in_ref, out_ref, basis_ref, down_ref, weight_ref,
                   fetched, wanted, pre_ref, gathered_ref,
                   table, outbox, acc, is_sem, ir_sem, rs_sem, rr_sem):
    shards, narrow = fetched.shape[:2]
    high = table.shape[0] // narrow
    y = lax.axis_index("dp")
    g = lax.axis_index("graph")
    barrier = pltpu.get_barrier_semaphore()

    @pl.loop(1, shards)
    def _(j):
        pl.semaphore_signal(barrier, inc=1, device_id=(y, (g + j) % shards), device_id_type=MESH)

    wanted[g] = in_ref[g]
    for h in range(high):
        pre = jnp.dot(edge_ref[h * LOW : (h + 1) * LOW], down_ref[...], preferred_element_type=F32)
        pre = pre.T
        pre_ref[:, h * LOW : (h + 1) * LOW] = pre
        table[h * narrow : (h + 1) * narrow] = (pre * jax.nn.sigmoid(pre)).astype(BF16)
    acc[...] = jnp.zeros_like(acc)
    pl.semaphore_wait(barrier, shards - 1)
    ask, asked = exchange(in_ref, wanted, is_sem, ir_sem)
    give, given = exchange(outbox, fetched, rs_sem, rr_sem)

    @pl.loop(0, 8)
    def _(k):
        for a in range(4):
            for_peers(k, a, -1, lambda p: ask(p).start())

    @pl.loop(0, 8)
    def _(k):
        for a in range(4):
            for_peers(k, a, 1, lambda p: asked(p).wait_recv())
        index = pairs_of(wanted, k, 1)
        put_pairs(outbox, k, 1, pick(table[...], index, narrow).astype(BF16))
        for a in range(4):
            for_peers(k, a, 1, lambda p: give(p).start())

    fetched[g] = outbox[g]

    @pl.loop(0, 8)
    def _(k):
        for a in range(4):
            for_peers(k, a, -1, lambda p: given(p).wait_recv())
        coef = coef_of(weight_ref[...], columns_of(basis_ref, k, -1))
        message = coef * pairs_of(fetched, k, -1).astype(F32)
        acc[...] += spread(message, row_of(out_ref, k, -1), high)

    for h in range(high):
        gathered_ref[:, h * LOW : (h + 1) * LOW] = acc[h * narrow : (h + 1) * narrow].astype(BF16)

    @pl.loop(1, shards)
    def _(j):
        p = (g + j) % shards
        ask(p).wait_send()
        give(p).wait_send()


VM = pl.BlockSpec(memory_space=pltpu.VMEM)


def forward(edge_rows, in_index, out_index, basis, down_weight, basis_weight):
    shards, _, slots = in_index.shape
    rows = edge_rows.shape[0]
    narrow = down_weight.shape[1]
    high = rows // LOW
    dma = pltpu.SemaphoreType.DMA
    return pl.pallas_call(
        forward_kernel,
        out_shape=(
            jax.ShapeDtypeStruct((shards, narrow, slots), BF16),
            jax.ShapeDtypeStruct(in_index.shape, jnp.int32),
            jax.ShapeDtypeStruct((narrow, rows), F32),
            jax.ShapeDtypeStruct((narrow, rows), BF16),
        ),
        in_specs=[VM] * 6,
        out_specs=(VM,) * 4,
        scratch_shapes=[
            pltpu.VMEM((high * narrow, LOW), BF16),
            pltpu.VMEM((shards, narrow, slots), BF16),
            pltpu.VMEM((high * narrow, LOW), F32),
            dma((shards,)), dma((shards,)), dma((shards,)), dma((shards,)),
        ],
        compiler_params=pltpu.CompilerParams(
            collective_id=1, has_side_effects=True, vmem_limit_bytes=VMEM_LIMIT),
        name="forward_exchange",
    )(edge_rows, in_index, out_index, basis, down_weight, basis_weight)


def slope_from(value, logistic):
    return logistic * (1.0 + value * (1.0 - logistic))


def dense_kernel(edge_ref, cot_ref, count_ref, gathered_ref, bil_ref, up_ref, w1_ref, w2_ref,
                 summed_ref, table_ref, first_ref, second_ref, upg_ref, bilg_ref):
    narrow = gathered_ref.shape[0]
    block = LOW
    steps = edge_ref.shape[0] // block
    first_ref[...] = jnp.zeros_like(first_ref)
    second_ref[...] = jnp.zeros_like(second_ref)
    upg_ref[...] = jnp.zeros_like(upg_ref)
    bilg_ref[...] = jnp.zeros_like(bilg_ref)
    count = count_ref[0, 0]

    @pl.loop(0, steps)
    def _(i):
        at = pl.ds(pl.multiple_of(i * block, block), block)
        gat = gathered_ref[:, at]
        mixed = contract(bil_ref[...], gat, 0, 0).astype(BF16)
        pre_up = contract(mixed, up_ref[...], 0, 0)
        s_up = jax.nn.sigmoid(pre_up)
        half = (edge_ref[at, :].astype(F32) + pre_up * s_up).astype(BF16)
        pre_first = jnp.dot(half, w1_ref[...], preferred_element_type=F32)
        s_first = jax.nn.sigmoid(pre_first)
        rows1 = (pre_first * s_first).astype(BF16)
        pre_second = jnp.dot(rows1, w2_ref[...], preferred_element_type=F32)
        live = lax.broadcasted_iota(jnp.int32, (block, 1), 0) + i * block < count
        top = cot_ref[at, :].astype(F32) * jnp.where(live, HALF, 0.0)
        back2 = (top * slope_from(pre_second, jax.nn.sigmoid(pre_second))).astype(BF16)
        back1 = contract(back2, w2_ref[...], 1, 1) * slope_from(pre_first, s_first)
        back1 = back1.astype(BF16)
        total = top + contract(back1, w1_ref[...], 1, 1)
        summed_ref[at, :] = total
        back_up = (total * slope_from(pre_up, s_up)).astype(BF16)
        back_mixed = contract(up_ref[...], back_up, 1, 1).astype(BF16)
        where = pl.ds(pl.multiple_of(i * narrow, narrow), narrow)
        table_ref[where, :] = jnp.dot(
            bil_ref[...], back_mixed, preferred_element_type=F32).astype(BF16)
        first_ref[...] += contract(half, back1, 0, 0)
        second_ref[...] += contract(rows1, back2, 0, 0)
        upg_ref[...] += jnp.dot(mixed, back_up, preferred_element_type=F32)
        bilg_ref[...] += contract(gat, back_mixed, 1, 1)


def dense(edge_rows, cotangent, count, gathered, bilinear, up, first, second):
    rows, wide = edge_rows.shape
    narrow = gathered.shape[0]
    shape = jax.ShapeDtypeStruct
    return pl.pallas_call(
        dense_kernel,
        out_shape=(
            shape((rows, wide), F32),
            shape((rows // LOW * narrow, LOW), BF16),
            shape((wide, wide), F32),
            shape((wide, wide), F32),
            shape((narrow, wide), F32),
            shape((narrow, narrow), F32),
        ),
        in_specs=[VM, VM, pl.BlockSpec(memory_space=pltpu.SMEM)] + [VM] * 5,
        out_specs=(VM,) * 6,
        compiler_params=pltpu.CompilerParams(vmem_limit_bytes=VMEM_LIMIT),
        name="dense",
    )(edge_rows, cotangent, count, gathered, bilinear, up, first, second)


def backward_kernel(scale, table_ref, fetched_ref, basis_ref, index_ref, weight_ref, wanted_ref,
                    pre_ref, edge_ref, summed_ref, down_ref, first_ref, second_ref, up_ref, bil_ref,
                    edge_out, first_out, second_out, tail_out, corner_out,
                    outbox, returned, acc, grad, back_pre,
                    send_a, got_a, part_b, got_b, full_b, held,
                    send_t, got_t, part_z, got_z, held_t,
                    rs_sem, rr_sem, as_sem, ar_sem, bs_sem, br_sem, cs_sem, cr_sem, ds_sem, dr_sem,
                    ts_sem, tr_sem, zs_sem, zr_sem, us_sem, ur_sem):
    shards, narrow = fetched_ref.shape[:2]
    wide = first_ref.shape[1]
    high = table_ref.shape[0] // narrow
    y, z, x, c = place()
    g = lax.axis_index("graph")
    chip = z * 4 + x
    barrier = pltpu.get_barrier_semaphore()

    def signal(device):
        pl.semaphore_signal(barrier, inc=1, device_id=device, device_id_type=MESH)

    @pl.loop(1, shards)
    def _(j):
        signal((y, (g + j) % shards))

    @pl.loop(8, 32)
    def _(j):
        signal(((y + j // 8) % 4, z * 8 + (x + j // 2 % 4) % 4 * 2 + (c + j % 2) % 2))

    mine8 = y * 2 + c

    def member8(j):
        py, pc = (y + j // 2) % 4, (c + j % 2) % 2
        return (py, chip * 2 + pc), py * 2 + pc

    def copy_a(j):
        device, index = member8(j)
        return pltpu.make_async_remote_copy(
            src_ref=send_a.at[index], dst_ref=got_a.at[j], send_sem=as_sem.at[j],
            recv_sem=ar_sem.at[j], device_id=device, device_id_type=MESH)

    def to_chip(src, dst, send_sem, recv_sem, j, block):
        q = (chip + j) % 32
        return pltpu.make_async_remote_copy(
            src_ref=src.at[q if block is None else block], dst_ref=dst.at[chip],
            send_sem=send_sem.at[q], recv_sem=recv_sem.at[chip], device_id=(y, 2 * q + c),
            device_id_type=MESH)

    def from_chip(src, dst, send_sem, recv_sem, j):
        q = (chip + j) % 32
        return pltpu.make_async_remote_copy(
            src_ref=src.at[0], dst_ref=dst.at[q], send_sem=send_sem.at[q],
            recv_sem=recv_sem.at[q], device_id=(y, 2 * q + c), device_id_type=MESH)

    def copy_d(j):
        device, _ = member8(j)
        return pltpu.make_async_remote_copy(
            src_ref=full_b, dst_ref=held.at[mine8], send_sem=ds_sem.at[j],
            recv_sem=dr_sem.at[j], device_id=device, device_id_type=MESH)

    mine32 = y * 8 + x * 2 + c

    def member32(j):
        py, px, pc = (y + j // 8) % 4, (x + j // 2 % 4) % 4, (c + j % 2) % 2
        return (py, z * 8 + px * 2 + pc), py * 8 + px * 2 + pc

    def copy_t(j):
        device, index = member32(j)
        return pltpu.make_async_remote_copy(
            src_ref=send_t.at[index], dst_ref=got_t.at[j], send_sem=ts_sem.at[j],
            recv_sem=tr_sem.at[j], device_id=device, device_id_type=MESH)

    def copy_z(j):
        return pltpu.make_async_remote_copy(
            src_ref=part_z, dst_ref=got_z.at[z], send_sem=zs_sem.at[j],
            recv_sem=zr_sem.at[j], device_id=(y, (z + j) % 8 * 8 + x * 2 + c), device_id_type=MESH)

    def copy_u(j):
        device, _ = member32(j)
        return pltpu.make_async_remote_copy(
            src_ref=part_z, dst_ref=held_t.at[mine32], send_sem=us_sem.at[j],
            recv_sem=ur_sem.at[j], device_id=device, device_id_type=MESH)

    def each(count, fn):
        @pl.loop(1, count)
        def _(j):
            fn(j)

    rows8 = wide // 8
    for m in range(8):
        at = slice(m * rows8, (m + 1) * rows8)
        send_a[m, :, :wide] = first_ref[at, :].astype(BF16)
        send_a[m, :, wide:] = second_ref[at, :].astype(BF16)
    acc[...] = jnp.zeros_like(acc)
    grad[...] = jnp.zeros_like(grad)
    send_t[...] = jnp.zeros_like(send_t)
    pl.semaphore_wait(barrier, shards - 1 + 24)
    each(8, lambda j: copy_a(j).start())
    give, given = exchange(outbox, returned, rs_sem, rr_sem)

    @pl.loop(0, 8)
    def _(k):
        basis = columns_of(basis_ref, k, 1)
        got = pick(table_ref[...], row_of(index_ref, k, 1), narrow)
        back_coef = (got * pairs_of(fetched_ref, k, 1).astype(F32)).astype(BF16)
        grad[...] += contract(basis, back_coef, 1, 1)
        put_pairs(outbox, k, 1, (got * coef_of(weight_ref[...], basis)).astype(BF16))
        for a in range(4):
            for_peers(k, a, 1, lambda p: give(p).start())

    returned[g] = outbox[g]

    def collect(k):
        for a in range(4):
            for_peers(k, a, -1, lambda p: given(p).wait_recv())
        value = pairs_of(returned, k, -1).astype(F32)
        acc[...] += spread(value, pairs_of(wanted_ref, k, -1), high)

    pl.loop(0, 4)(collect)

    got_a[0] = send_a[mine8]
    each(8, lambda j: copy_a(j).wait_recv())

    for r in range(4):
        at = slice(r * 16, (r + 1) * 16)
        total = got_a[0, at, :].astype(F32)
        for j in range(1, 8):
            total = total + got_a[j, at, :].astype(F32)
        total = total.astype(BF16)
        for s in range(8):
            part_b[r * 8 + s] = total[:, s * 128 : (s + 1) * 128]
    each(32, lambda j: to_chip(part_b, got_b, bs_sem, br_sem, j, None).start())

    pl.loop(4, 8)(collect)

    for h in range(high):
        columns = slice(h * LOW, (h + 1) * LOW)
        back = acc[h * narrow : (h + 1) * narrow]
        back_pre[:, columns] = (back * silu_slope(pre_ref[:, columns])).astype(BF16)
    down = jnp.dot(back_pre[...], edge_ref[...], preferred_element_type=F32).astype(BF16)
    ups = up_ref[...].astype(BF16)
    for m in range(16):
        at, columns = slice(m // 4 * 16, m // 4 * 16 + 16), slice(m % 4 * 128, m % 4 * 128 + 128)
        send_t[m, :16] = down[at, columns]
        send_t[16 + m, :16] = ups[at, columns]
    for m in range(narrow // 16):
        send_t[m, 16:, :narrow] = bil_ref[m * 16 : (m + 1) * 16, :].astype(BF16)
    send_t[narrow // 16, 16:, :narrow] = grad[...].astype(BF16)
    each(32, lambda j: copy_t(j).start())

    got_b[chip] = part_b[chip]
    each(32, lambda j: from_chip(part_b, got_b, bs_sem, br_sem, j).wait_recv())
    total = got_b[0].astype(F32)
    for j in range(1, 32):
        total = total + got_b[j].astype(F32)
    full_b[chip] = (total * scale).astype(BF16)
    each(32, lambda j: to_chip(full_b, full_b, cs_sem, cr_sem, j, chip).start())

    down_t = down_ref[...].T
    steps = edge_ref.shape[0] // LOW

    def finish(i):
        at = pl.ds(pl.multiple_of(i * LOW, LOW), LOW)
        add = contract(back_pre[:, at], down_t, 0, 0)
        edge_out[at, :] = (summed_ref[at, :] + add).astype(BF16)

    pl.loop(0, steps // 2)(finish)

    got_t[0] = send_t[mine32]
    each(32, lambda j: copy_t(j).wait_recv())
    total = got_t[0].astype(F32)
    for j in range(1, 32):
        total = total + got_t[j].astype(F32)
    part_z[...] = total.astype(BF16)
    got_z[z] = total.astype(BF16)
    each(8, lambda j: copy_z(j).start())

    pl.loop(steps // 2, steps)(finish)

    each(32, lambda j: from_chip(full_b, full_b, cs_sem, cr_sem, j).wait_recv())
    each(8, lambda j: copy_d(j).start())
    held[mine8] = full_b[...]

    each(8, lambda j: copy_z(j).wait())
    total = got_z[0].astype(F32)
    for j in range(1, 8):
        total = total + got_z[j].astype(F32)
    total = (total * scale).astype(BF16)
    part_z[...] = total
    held_t[mine32] = total
    each(32, lambda j: copy_u(j).start())

    each(8, lambda j: copy_d(j).wait())

    @pl.loop(0, 8)
    def _(m):
        for r in range(4):
            at = pl.ds(pl.multiple_of(m * rows8 + r * 16, 16), 16)
            for s in range(4):
                columns = slice(s * 128, (s + 1) * 128)
                first_out[at, columns] = held[m, r * 8 + s].astype(F32)
                second_out[at, columns] = held[m, r * 8 + 4 + s].astype(F32)

    each(32, lambda j: copy_u(j).wait())
    for m in range(32):
        at, columns = slice(m // 4 * 16, m // 4 * 16 + 16), slice(m % 4 * 128, m % 4 * 128 + 128)
        tail_out[at, columns] = held_t[m, :16].astype(F32)
    for m in range(5):
        corner_out[m * 16 : (m + 1) * 16, :] = held_t[m, 16:].astype(F32)

    each(shards, lambda j: give((g + j) % shards).wait_send())
    each(8, lambda j: copy_a(j).wait_send())
    each(32, lambda j: copy_t(j).wait_send())
    each(32, lambda j: from_chip(part_b, got_b, bs_sem, br_sem, j).wait_send())
    each(32, lambda j: from_chip(full_b, full_b, cs_sem, cr_sem, j).wait_send())


def backward(scale, table, fetched, basis, out_index, basis_weight, wanted, pre_down, edge_rows,
             back_summed, down_weight, first, second, up, bilinear):
    shards, narrow, slots = fetched.shape
    rows, wide = edge_rows.shape
    dma = pltpu.SemaphoreType.DMA
    shape = jax.ShapeDtypeStruct
    vmem = pltpu.VMEM
    return pl.pallas_call(
        functools.partial(backward_kernel, scale),
        out_shape=(
            shape((rows, wide), BF16),
            shape(first.shape, F32),
            shape(second.shape, F32),
            shape((2 * narrow, wide), F32),
            shape((narrow + basis.shape[0], 128), F32),
        ),
        in_specs=[VM] * 14,
        out_specs=(VM,) * 5,
        scratch_shapes=[
            vmem((shards, narrow, slots), BF16),
            vmem((shards, narrow, slots), BF16),
            vmem((rows // LOW * narrow, LOW), F32),
            vmem(basis_weight.shape, F32),
            vmem((narrow, rows), BF16),
            vmem((8, wide // 8, 2 * wide), BF16),
            vmem((8, wide // 8, 2 * wide), BF16),
            vmem((32, 16, 128), BF16),
            vmem((32, 16, 128), BF16),
            vmem((32, 16, 128), BF16),
            vmem((8, 32, 16, 128), BF16),
            vmem((32, 32, 128), BF16),
            vmem((32, 32, 128), BF16),
            vmem((32, 128), BF16),
            vmem((8, 32, 128), BF16),
            vmem((32, 32, 128), BF16),
            dma((shards,)), dma((shards,)), dma((8,)), dma((8,)), dma((32,)), dma((32,)),
            dma((32,)), dma((32,)), dma((8,)), dma((8,)), dma((32,)), dma((32,)),
            dma((8,)), dma((8,)), dma((32,)), dma((32,)),
        ],
        compiler_params=pltpu.CompilerParams(
            collective_id=2, has_side_effects=True, vmem_limit_bytes=VMEM_LIMIT),
        name="backward_exchange",
    )(table, fetched, basis, out_index, basis_weight, wanted, pre_down, edge_rows, back_summed,
      down_weight, first, second, up, bilinear)


def local(
    edge_state,
    cotangent,
    edge_count,
    triplet_basis,
    triplet_in,
    triplet_out,
    down_weight,
    basis_weight,
    bilinear_weight,
    up_weight,
    first_weight,
    second_weight,
):
    edge_rows = edge_state[0]
    row_count, wide = edge_rows.shape
    shards = lax.axis_size("graph")
    narrow = down_weight.shape[1]
    tri_rows = triplet_in.shape[1]
    slot_count = tri_rows // shards
    basis = triplet_basis[0]
    out_index = triplet_out[0].reshape(tri_rows // LOW, 1, LOW)
    in_index = triplet_in[0].reshape(shards, 1, slot_count)
    fetched, wanted, pre_down, gathered = forward(
        edge_rows, in_index, out_index, basis, down_weight, basis_weight)
    back_summed, table, first_grad, second_grad, up_grad, bilinear_grad = dense(
        edge_rows, cotangent[0], edge_count, gathered, bilinear_weight, up_weight,
        first_weight, second_weight)
    grad_scale = 1.0 / math.sqrt(lax.axis_size("dp") * shards * row_count)
    edge_grad, first_grad, second_grad, tail, corner = backward(
        grad_scale, table, fetched, basis, out_index, basis_weight, wanted, pre_down, edge_rows,
        back_summed, down_weight, first_grad, second_grad, up_grad, bilinear_grad)
    return (
        edge_grad[None],
        tail[:narrow].T,
        corner[narrow:, :narrow],
        corner[:narrow, :narrow],
        tail[narrow:],
        first_grad,
        second_grad,
    )


def solution(mesh):
    in_specs = (
        P("dp", "graph", None),
        P("dp", "graph", None),
        P("dp", "graph"),
        P("dp", None, "graph"),
        P("dp", "graph"),
        P("dp", "graph"),
        P(),
        P(),
        P(),
        P(),
        P(),
        P(),
    )
    out_specs = (P("dp", "graph", None), P(), P(), P(), P(), P(), P())
    return jax.shard_map(local, mesh=mesh, in_specs=in_specs, out_specs=out_specs, check_vma=False)
```

```python
import functools
import math

import jax
import jax.numpy as jnp
from jax import lax
from jax.experimental import pallas as pl
from jax.experimental.pallas import tpu as pltpu
from jax.sharding import PartitionSpec as P

HALF = 0.7071067811865476
LOW = 256
MESH = pl.DeviceIdType.MESH
F32 = jnp.float32
BF16 = jnp.bfloat16
VMEM_LIMIT = 60 * 1024 * 1024


def sigmoid(value):
    return 0.5 * jnp.tanh(0.5 * value) + 0.5


def slope_from(value, logistic):
    return logistic * (1.0 + value * (1.0 - logistic))


def contract(left, right, left_dim, right_dim):
    return lax.dot_general(
        left, right, (((left_dim,), (right_dim,)), ((), ())), preferred_element_type=jnp.float32
    )


def low_hot(low, width):
    rows = lax.broadcasted_iota(jnp.int32, (LOW, width), 0)
    return jnp.where(rows == low, 1.0, 0.0).astype(BF16)


def pick(table, index, narrow):
    width = index.shape[1]
    high = table.shape[0] // narrow
    hot = low_hot(index & (LOW - 1), width)
    upper = index >> 8
    wide = jnp.dot(table, hot, preferred_element_type=F32)
    out = wide[:narrow]
    for h in range(1, high):
        out = jnp.where(upper == h, wide[h * narrow : (h + 1) * narrow], out)
    return out


def spread(value, index, high):
    hot = low_hot(index & (LOW - 1), index.shape[1])
    upper = index >> 8
    parts = [jnp.where(upper == h, value, 0.0).astype(BF16) for h in range(high)]
    return contract(jnp.concatenate(parts, axis=0), hot, 1, 1)


def coef_of(weight, basis):
    return contract(weight, basis, 0, 0)


def place():
    g = lax.axis_index("graph")
    return lax.axis_index("dp"), g // 8, (g // 2) % 4, g % 2


def chip_at(k, a, sign):
    _, z, x, _ = place()
    dz, dx = (k + 2 * a) % 8, a
    if sign < 0:
        dz, dx = 8 - dz, 4 - dx
    return (z + dz) % 8 * 4 + (x + dx) % 4


def for_peers(k, a, sign, fn):
    q = chip_at(k, a, sign)
    if a:
        fn(2 * q)
        fn(2 * q + 1)
        return

    @pl.when(k > 0)
    def _():
        fn(2 * q)
        fn(2 * q + 1)

    @pl.when(k == 0)
    def _():
        g = lax.axis_index("graph")
        fn(g + 1 - 2 * (g % 2))


def row_of(ref, k, sign):
    return jnp.concatenate([ref[chip_at(k, a, sign)] for a in range(4)], axis=1)


def pairs_of(ref, k, sign):
    chips = [chip_at(k, a, sign) for a in range(4)]
    return jnp.concatenate([ref[2 * q + c] for q in chips for c in range(2)], axis=1)


def columns_of(ref, k, sign):
    chips = [chip_at(k, a, sign) for a in range(4)]
    return jnp.concatenate(
        [ref[:, pl.ds(pl.multiple_of(q * LOW, LOW), LOW)] for q in chips], axis=1)


def put_pairs(ref, k, sign, value):
    for a in range(4):
        q = chip_at(k, a, sign)
        for c in range(2):
            at = (2 * a + c) * 128
            ref[2 * q + c] = value[:, at : at + 128]


def exchange(src, dst, send_sem, recv_sem):
    y = lax.axis_index("dp")
    g = lax.axis_index("graph")

    def out(p):
        return pltpu.make_async_remote_copy(
            src_ref=src.at[p], dst_ref=dst.at[g], send_sem=send_sem.at[p],
            recv_sem=recv_sem.at[g], device_id=(y, p), device_id_type=MESH)

    def back(p):
        return pltpu.make_async_remote_copy(
            src_ref=src.at[p], dst_ref=dst.at[p], send_sem=send_sem.at[p],
            recv_sem=recv_sem.at[p], device_id=(y, p), device_id_type=MESH)

    return out, back


VM = pl.BlockSpec(memory_space=pltpu.VMEM)
HB = pl.BlockSpec(memory_space=pl.ANY)
DENSE = 512
TILE = 16


def each(count, fn):
    @pl.loop(1, count)
    def _(j):
        fn(j)


def total_of(ref, count):
    total = ref[0].astype(F32)
    for j in range(1, count):
        total = total + ref[j].astype(F32)
    return total


def plane_sum(send, got, part, got_z, held, sems, scale):
    y, z, x, c = place()
    mine = y * 8 + x * 2 + c
    ts_sem, tr_sem, zs_sem, zr_sem, us_sem, ur_sem = sems

    def member(j):
        py, px, pc = (y + j // 8) % 4, (x + j // 2 % 4) % 4, (c + j % 2) % 2
        return (py, z * 8 + px * 2 + pc), py * 8 + px * 2 + pc

    def copy_t(j):
        device, index = member(j)
        return pltpu.make_async_remote_copy(
            src_ref=send.at[index], dst_ref=got.at[j], send_sem=ts_sem.at[j],
            recv_sem=tr_sem.at[j], device_id=device, device_id_type=MESH)

    def copy_z(j):
        return pltpu.make_async_remote_copy(
            src_ref=part.at[0], dst_ref=got_z.at[z], send_sem=zs_sem.at[j],
            recv_sem=zr_sem.at[j], device_id=(y, (z + j) % 8 * 8 + x * 2 + c), device_id_type=MESH)

    def copy_u(j):
        device, _ = member(j)
        return pltpu.make_async_remote_copy(
            src_ref=part.at[1], dst_ref=held.at[mine], send_sem=us_sem.at[j],
            recv_sem=ur_sem.at[j], device_id=device, device_id_type=MESH)

    def start():
        each(32, lambda j: copy_t(j).start())

    def along():
        got[0] = send[mine]
        each(32, lambda j: copy_t(j).wait_recv())
        total = total_of(got, 32).astype(part.dtype)
        part[0] = total
        got_z[z] = total
        each(8, lambda j: copy_z(j).start())

    def share():
        each(8, lambda j: copy_z(j).wait_recv())
        total = (total_of(got_z, 8) * scale).astype(part.dtype)
        part[1] = total
        held[mine] = total
        each(32, lambda j: copy_u(j).start())

    def end():
        each(32, lambda j: copy_u(j).wait())
        each(32, lambda j: copy_t(j).wait_send())
        each(8, lambda j: copy_z(j).wait_send())

    return start, along, share, end


def main_kernel(scale, edge_ref, in_ref, down_ref, count_ref, weight_ref, bil_ref,
                cot_hbm, basis_hbm, index_hbm, up_hbm, w1_hbm, w2_hbm,
                edge_hbm, big_ref, early_ref, late_ref,
                cot_ref, basis_ref, index_ref, up_ref, w1_ref, w2_ref,
                fetched, wanted, pre_ref, table, outbox, acc, gathered,
                summed, half_s, back1_s, rows1_s, back2_s, backup_s, mixed_s, bil_grad, grad,
                outbox2, returned, back_pre, edge_out,
                send_a, got_p, pair_s, got_a, part_b, got_b, full_b,
                send_e, got_e, part_e, gotz_e, send_t, got_t, part_t, gotz_t,
                load_sem, save_sem, is_sem, ir_sem, rs_sem, rr_sem, qs_sem, qr_sem,
                ps_sem, as_sem, ar_sem, bs_sem, br_sem, cs_sem, cr_sem, ds_sem, dr_sem,
                *plane_sems):
    shards, narrow = fetched.shape[:2]
    rows, wide = edge_ref.shape
    high = rows // LOW
    y, z, x, c = place()
    g = lax.axis_index("graph")
    chip = z * 4 + x
    barrier = pltpu.get_barrier_semaphore()

    def signal(device):
        pl.semaphore_signal(barrier, inc=1, device_id=device, device_id_type=MESH)

    @pl.loop(1, shards)
    def _(j):
        signal((y, (g + j) % shards))

    @pl.loop(8, 32)
    def _(j):
        signal(((y + j // 8) % 4, z * 8 + (x + j // 2 % 4) % 4 * 2 + (c + j % 2) % 2))

    loads = [
        pltpu.make_async_copy(src, dst, load_sem.at[i])
        for i, (src, dst) in enumerate((
            (basis_hbm, basis_ref), (index_hbm, index_ref), (up_hbm, up_ref), (w1_hbm, w1_ref),
            (w2_hbm, w2_ref), (cot_hbm, cot_ref)))
    ]
    for load in loads:
        load.start()

    wanted[g] = in_ref[g]
    for h in range(high):
        pre = jnp.dot(edge_ref[h * LOW : (h + 1) * LOW], down_ref[...], preferred_element_type=F32)
        pre = pre.T
        pre_ref[:, h * LOW : (h + 1) * LOW] = pre
        table[h * narrow : (h + 1) * narrow] = (pre * sigmoid(pre)).astype(BF16)
    acc[...] = jnp.zeros_like(acc)
    grad[...] = jnp.zeros_like(grad)
    bil_grad[...] = jnp.zeros_like(bil_grad)
    send_e[...] = jnp.zeros_like(send_e)
    pl.semaphore_wait(barrier, shards - 1 + 24)
    ask, asked = exchange(in_ref, wanted, is_sem, ir_sem)
    give, given = exchange(outbox, fetched, rs_sem, rr_sem)

    @pl.loop(0, 8)
    def _(k):
        for a in range(4):
            for_peers(k, a, -1, lambda p: ask(p).start())

    @pl.loop(0, 8)
    def _(k):
        for a in range(4):
            for_peers(k, a, 1, lambda p: asked(p).wait_recv())
        index = pairs_of(wanted, k, 1)
        put_pairs(outbox, k, 1, pick(table[...], index, narrow).astype(BF16))
        for a in range(4):
            for_peers(k, a, 1, lambda p: give(p).start())

    fetched[g] = outbox[g]
    for load in loads:
        load.wait()

    @pl.loop(0, 8)
    def _(k):
        for a in range(4):
            for_peers(k, a, -1, lambda p: given(p).wait_recv())
        coef = coef_of(weight_ref[...], columns_of(basis_ref, k, -1))
        message = coef * pairs_of(fetched, k, -1).astype(F32)
        acc[...] += spread(message, row_of(index_ref, k, -1), high)

    for h in range(high):
        gathered[:, h * LOW : (h + 1) * LOW] = acc[h * narrow : (h + 1) * narrow].astype(BF16)
    acc[...] = jnp.zeros_like(acc)

    count = count_ref[0, 0]

    @pl.loop(0, rows // DENSE)
    def _(i):
        at = pl.ds(pl.multiple_of(i * DENSE, DENSE), DENSE)
        gat = gathered[:, at]
        mixed = contract(bil_ref[...], gat, 0, 0).astype(BF16)
        mixed_s[:, at] = mixed
        pre_up = contract(mixed, up_ref[...], 0, 0)
        s_up = sigmoid(pre_up)
        half = (edge_ref[at, :].astype(F32) + pre_up * s_up).astype(BF16)
        half_s[at, :] = half
        pre_first = jnp.dot(half, w1_ref[...], preferred_element_type=F32)
        s_first = sigmoid(pre_first)
        rows1 = (pre_first * s_first).astype(BF16)
        rows1_s[at, :] = rows1
        pre_second = jnp.dot(rows1, w2_ref[...], preferred_element_type=F32)
        live = lax.broadcasted_iota(jnp.int32, (DENSE, 1), 0) + i * DENSE < count
        top = cot_ref[at, :].astype(F32) * jnp.where(live, HALF, 0.0)
        back2 = (top * slope_from(pre_second, sigmoid(pre_second))).astype(BF16)
        back2_s[at, :] = back2
        back1 = contract(back2, w2_ref[...], 1, 1) * slope_from(pre_first, s_first)
        back1 = back1.astype(BF16)
        back1_s[at, :] = back1
        total = top + contract(back1, w1_ref[...], 1, 1)
        summed[at, :] = total
        back_up = (total * slope_from(pre_up, s_up)).astype(BF16)
        backup_s[at, :] = back_up
        back_mixed = contract(up_ref[...], back_up, 1, 1).astype(BF16)
        bil_grad[...] += contract(gat, back_mixed, 1, 1)
        turned = jnp.dot(bil_ref[...], back_mixed, preferred_element_type=F32).astype(BF16)
        for q in range(DENSE // LOW):
            where = pl.multiple_of((i * (DENSE // LOW) + q) * narrow, narrow)
            table[pl.ds(where, narrow), :] = turned[:, q * LOW : (q + 1) * LOW]

    bring, brought = exchange(outbox2, returned, qs_sem, qr_sem)

    @pl.loop(0, 8)
    def _(k):
        basis = columns_of(basis_ref, k, 1)
        got = pick(table[...], row_of(index_ref, k, 1), narrow)
        put_pairs(outbox2, k, 1, (got * coef_of(weight_ref[...], basis)).astype(BF16))
        for a in range(4):
            for_peers(k, a, 1, lambda p: bring(p).start())
        back_coef = (got * pairs_of(fetched, k, 1).astype(F32)).astype(BF16)
        grad[...] += contract(basis, back_coef, 1, 1)

    returned[g] = outbox2[g]

    def collect(k):
        for a in range(4):
            for_peers(k, a, -1, lambda p: brought(p).wait_recv())
        value = pairs_of(returned, k, -1).astype(F32)
        acc[...] += spread(value, pairs_of(wanted, k, -1), high)

    eighth = wide // 8

    def pair_copy(src, dst, at):
        return pltpu.make_async_remote_copy(
            src_ref=src, dst_ref=dst, send_sem=ps_sem.at[at], recv_sem=ps_sem.at[at + 1],
            device_id=(y, g + 1 - 2 * c), device_id_type=MESH)

    def copy_a(j):
        py = (y + j) % 4
        return pltpu.make_async_remote_copy(
            src_ref=pair_s.at[py], dst_ref=got_a.at[j], send_sem=as_sem.at[j],
            recv_sem=ar_sem.at[j], device_id=(py, g), device_id_type=MESH)

    def to_chip(src, dst, send_sem, recv_sem, j, block):
        q = (chip + j) % 32
        return pltpu.make_async_remote_copy(
            src_ref=src.at[q if block is None else block], dst_ref=dst.at[chip],
            send_sem=send_sem.at[q], recv_sem=recv_sem.at[chip], device_id=(y, 2 * q + c),
            device_id_type=MESH)

    def from_chip(src, dst, send_sem, recv_sem, j):
        q = (chip + j) % 32
        return pltpu.make_async_remote_copy(
            src_ref=src.at[0], dst_ref=dst.at[q], send_sem=send_sem.at[q],
            recv_sem=recv_sem.at[q], device_id=(y, 2 * q + c), device_id_type=MESH)

    def copy_d(j):
        return pltpu.make_async_remote_copy(
            src_ref=full_b, dst_ref=big_ref.at[c * 4 + y], send_sem=ds_sem.at[j],
            recv_sem=dr_sem.at[j], device_id=((y + j) % 4, g), device_id_type=MESH)

    second = contract(rows1_s[...], back2_s[...], 0, 0).astype(BF16)
    for m in range(8):
        send_a[m % 2, m // 2, :, wide:] = second[m * eighth : (m + 1) * eighth]
    first = contract(half_s[...], back1_s[...], 0, 0).astype(BF16)
    for m in range(8):
        send_a[m % 2, m // 2, :, :wide] = first[m * eighth : (m + 1) * eighth]
    pair_a = pair_copy(send_a.at[1 - c], got_p, 0)
    pair_a.start()

    early = plane_sum(send_e, got_e, part_e, gotz_e, early_ref, plane_sems[:6], scale)
    late = plane_sum(send_t, got_t, part_t, gotz_t, late_ref, plane_sems[6:], scale)
    ups = jnp.dot(mixed_s[...], backup_s[...], preferred_element_type=F32).astype(BF16)
    for m in range(16):
        send_e[m] = ups[m // 4 * 16 : m // 4 * 16 + 16, m % 4 * 128 : m % 4 * 128 + 128]
    for m in range(narrow // 16):
        send_e[16 + m, :, :narrow] = bil_grad[m * 16 : (m + 1) * 16, :].astype(BF16)
    send_e[16 + narrow // 16, :, :narrow] = grad[...].astype(BF16)
    early[0]()

    collect(0)
    pair_a.wait()
    for j in range(4):
        for r in range(4):
            at = slice(r * TILE, (r + 1) * TILE)
            pair_s[j, at] = (send_a[c, j, at].astype(F32) + got_p[j, at].astype(F32)).astype(BF16)
    each(4, lambda j: copy_a(j).start())
    pl.loop(1, 4)(collect)
    early[1]()
    pl.loop(4, 6)(collect)
    got_a[0] = pair_s[y]
    each(4, lambda j: copy_a(j).wait_recv())
    for r in range(4):
        at = slice(r * TILE, (r + 1) * TILE)
        total = got_a[0, at].astype(F32)
        for j in range(1, 4):
            total = total + got_a[j, at].astype(F32)
        total = total.astype(BF16)
        for s in range(8):
            part_b[r * 8 + s] = total[:, s * 128 : (s + 1) * 128]
    each(32, lambda j: to_chip(part_b, got_b, bs_sem, br_sem, j, None).start())
    early[2]()
    pl.loop(6, 8)(collect)

    for h in range(high):
        columns = slice(h * LOW, (h + 1) * LOW)
        pre = pre_ref[:, columns]
        back = acc[h * narrow : (h + 1) * narrow]
        back_pre[:, columns] = (back * slope_from(pre, sigmoid(pre))).astype(BF16)
    down = jnp.dot(back_pre[...], edge_ref[...], preferred_element_type=F32)
    for m in range(32):
        send_t[m] = down[m // 4 * 8 : m // 4 * 8 + 8, m % 4 * 128 : m % 4 * 128 + 128]
    late[0]()

    got_b[chip] = part_b[chip]
    each(32, lambda j: from_chip(part_b, got_b, bs_sem, br_sem, j).wait_recv())
    full_b[chip] = (total_of(got_b, 32) * scale).astype(BF16)
    each(32, lambda j: to_chip(full_b, full_b, cs_sem, cr_sem, j, chip).start())

    down_t = down_ref[...].T
    blocks = rows // DENSE

    def save(i):
        at = pl.ds(pl.multiple_of(i * DENSE, DENSE), DENSE)
        return pltpu.make_async_copy(edge_out.at[at], edge_hbm.at[at], save_sem.at[i])

    def finish(i):
        at = pl.ds(pl.multiple_of(i * DENSE, DENSE), DENSE)
        add = contract(back_pre[:, at], down_t, 0, 0)
        edge_out[at, :] = (summed[at, :] + add).astype(BF16)

    pl.loop(0, blocks // 2)(finish)
    late[1]()
    each(32, lambda j: from_chip(full_b, full_b, cs_sem, cr_sem, j).wait_recv())
    each(4, lambda j: copy_d(j).start())
    big_ref[c * 4 + y] = full_b[...]
    pl.loop(blocks // 2, blocks)(finish)
    pl.loop(0, blocks)(lambda i: save(i).start())
    late[2]()
    each(4, lambda j: copy_d(j).wait_recv())
    mine = pl.ds(c * 4, 4)
    pair_d = pair_copy(big_ref.at[mine], big_ref.at[mine], 2)
    pair_d.start()
    pl.loop(0, blocks)(lambda i: save(i).wait())

    @pl.loop(1, shards)
    def _(j):
        p = (g + j) % shards
        ask(p).wait_send()
        give(p).wait_send()
        bring(p).wait_send()

    each(4, lambda j: copy_a(j).wait_send())
    each(4, lambda j: copy_d(j).wait_send())
    each(32, lambda j: from_chip(part_b, got_b, bs_sem, br_sem, j).wait_send())
    each(32, lambda j: from_chip(full_b, full_b, cs_sem, cr_sem, j).wait_send())
    early[3]()
    late[3]()
    pair_d.wait()


def main(scale, edge_rows, in_index, down_weight, count, basis_weight, bilinear, cotangent, basis,
         out_index, up, first, second):
    shards, _, slots = in_index.shape
    rows, wide = edge_rows.shape
    narrow = down_weight.shape[1]
    high = rows // LOW
    d = pltpu.SemaphoreType.DMA
    shape = jax.ShapeDtypeStruct
    v = pltpu.VMEM
    block = (shards, narrow, slots)
    tiles = (32, TILE, 128)
    halves = (32, TILE // 2, 128)
    plane = [d((32,)), d((32,)), d((8,)), d((8,)), d((32,)), d((32,))]
    return pl.pallas_call(
        functools.partial(main_kernel, scale),
        out_shape=(
            shape((rows, wide), BF16),
            shape((8,) + tiles, BF16),
            shape(tiles, BF16),
            shape(halves, F32),
        ),
        in_specs=[VM, VM, VM, pl.BlockSpec(memory_space=pltpu.SMEM), VM, VM] + [HB] * 6,
        out_specs=(HB, VM, VM, VM),
        scratch_shapes=[
            v(cotangent.shape, BF16), v(basis.shape, BF16), v(out_index.shape, jnp.int32),
            v(up.shape, BF16), v(first.shape, BF16), v(second.shape, BF16),
            v(block, BF16), v(in_index.shape, jnp.int32), v((narrow, rows), F32),
            v((high * narrow, LOW), BF16), v(block, BF16), v((high * narrow, LOW), F32),
            v((narrow, rows), BF16),
            v((rows, wide), F32), v((rows, wide), BF16), v((rows, wide), BF16),
            v((rows, wide), BF16), v((rows, wide), BF16), v((rows, wide), BF16),
            v((narrow, rows), BF16), v((narrow, narrow), F32), v(basis_weight.shape, F32),
            v(block, BF16), v(block, BF16), v((narrow, rows), BF16), v((rows, wide), BF16),
            v((2, 4, wide // 8, 2 * wide), BF16), v((4, wide // 8, 2 * wide), BF16),
            v((4, wide // 8, 2 * wide), BF16), v((4, wide // 8, 2 * wide), BF16),
            v(tiles, BF16), v(tiles, BF16), v(tiles, BF16),
            v(tiles, BF16), v(tiles, BF16), v((2,) + tiles[1:], BF16), v((8,) + tiles[1:], BF16),
            v(halves, F32), v(halves, F32), v((2,) + halves[1:], F32), v((8,) + halves[1:], F32),
            d((6,)), d((rows // DENSE,)),
            d((shards,)), d((shards,)), d((shards,)), d((shards,)), d((shards,)), d((shards,)),
            d((4,)), d((4,)), d((4,)), d((32,)), d((32,)), d((32,)), d((32,)), d((4,)), d((4,)),
        ] + plane + plane,
        compiler_params=pltpu.CompilerParams(
            collective_id=1, has_side_effects=True, vmem_limit_bytes=VMEM_LIMIT),
        name="main",
    )(edge_rows, in_index, down_weight, count, basis_weight, bilinear, cotangent, basis, out_index,
      up, first, second)


def final_kernel(edge_ref, big_ref, early_ref, late_ref,
                 edge_out, first_out, second_out, down_out, basis_out, bil_out, up_out):
    edge_out[...] = edge_ref[...]
    for r in range(4):
        for s in range(4):
            at, columns = slice(r * 16, r * 16 + 16), slice(s * 128, s * 128 + 128)
            first_out[at, columns] = big_ref[0, r * 8 + s].astype(F32)
            second_out[at, columns] = big_ref[0, r * 8 + 4 + s].astype(F32)

    @pl.when(pl.program_id(0) == 0)
    def _():
        narrow = bil_out.shape[0]
        for s in range(4):
            column = jnp.concatenate([late_ref[r * 4 + s] for r in range(8)], axis=0)
            down_out[s * 128 : (s + 1) * 128, :] = column.T
        for m in range(16):
            up_out[m // 4 * 16 : m // 4 * 16 + 16, m % 4 * 128 : m % 4 * 128 + 128] = (
                early_ref[m].astype(F32))
        for m in range(narrow // 16):
            bil_out[m * 16 : (m + 1) * 16, :] = early_ref[16 + m].astype(F32)[:, :narrow]
        basis_out[...] = early_ref[16 + narrow // 16].astype(F32)[:, :narrow]


def final(edge, big, early, late, narrow, bases):
    rows, wide = edge.shape
    shape = jax.ShapeDtypeStruct

    def whole(s):
        return pl.BlockSpec(s, lambda i: (0,) * len(s))

    edge_spec = pl.BlockSpec((rows // 8, wide), lambda i: (i, 0))
    grad_spec = pl.BlockSpec((wide // 8, wide), lambda i: (i, 0))
    smalls = [(wide, narrow), (bases, narrow), (narrow, narrow), (narrow, wide)]
    return pl.pallas_call(
        final_kernel,
        grid=(8,),
        out_shape=(shape((rows, wide), BF16), shape((wide, wide), F32), shape((wide, wide), F32))
        + tuple(shape(s, F32) for s in smalls),
        in_specs=[
            edge_spec,
            pl.BlockSpec((1,) + big.shape[1:], lambda i: (i % 2 * 4 + i // 2, 0, 0, 0)),
            whole(early.shape), whole(late.shape)],
        out_specs=(edge_spec, grad_spec, grad_spec) + tuple(whole(s) for s in smalls),
        compiler_params=pltpu.CompilerParams(dimension_semantics=("arbitrary",)),
        name="final",
    )(edge, big, early, late)


def local(
    edge_state,
    cotangent,
    edge_count,
    triplet_basis,
    triplet_in,
    triplet_out,
    down_weight,
    basis_weight,
    bilinear_weight,
    up_weight,
    first_weight,
    second_weight,
):
    edge_rows = edge_state[0]
    row_count = edge_rows.shape[0]
    shards = lax.axis_size("graph")
    bases, narrow = basis_weight.shape
    tri_rows = triplet_in.shape[1]
    out_index = triplet_out[0].reshape(tri_rows // LOW, 1, LOW)
    in_index = triplet_in[0].reshape(shards, 1, tri_rows // shards)
    grad_scale = 1.0 / math.sqrt(lax.axis_size("dp") * shards * row_count)
    edge_grad, big, early, late = main(
        grad_scale, edge_rows, in_index, down_weight, edge_count, basis_weight, bilinear_weight,
        cotangent[0], triplet_basis[0], out_index, up_weight, first_weight, second_weight)
    edge_grad, first_grad, second_grad, down_grad, basis_grad, bilinear_grad, up_grad = final(
        edge_grad, big, early, late, narrow, bases)
    return edge_grad[None], down_grad, basis_grad, bilinear_grad, up_grad, first_grad, second_grad


def solution(mesh):
    in_specs = (
        P("dp", "graph", None),
        P("dp", "graph", None),
        P("dp", "graph"),
        P("dp", None, "graph"),
        P("dp", "graph"),
        P("dp", "graph"),
        P(),
        P(),
        P(),
        P(),
        P(),
        P(),
    )
    out_specs = (P("dp", "graph", None), P(), P(), P(), P(), P(), P())
    return jax.shard_map(local, mesh=mesh, in_specs=in_specs, out_specs=out_specs, check_vma=False)
```

```python
import functools
import math

import jax
import jax.numpy as jnp
from jax import lax
from jax.experimental import pallas as pl
from jax.experimental.pallas import tpu as pltpu
from jax.sharding import PartitionSpec as P

HALF = 0.7071067811865476
LOW = 256
MESH = pl.DeviceIdType.MESH
F32 = jnp.float32
BF16 = jnp.bfloat16
VMEM_LIMIT = 60 * 1024 * 1024


def sigmoid(value):
    return 0.5 * jnp.tanh(0.5 * value) + 0.5


def slope_from(value, logistic):
    return logistic * (1.0 + value * (1.0 - logistic))


def contract(left, right, left_dim, right_dim):
    return lax.dot_general(
        left, right, (((left_dim,), (right_dim,)), ((), ())), preferred_element_type=jnp.float32
    )


def low_hot(low, width):
    rows = lax.broadcasted_iota(jnp.int32, (LOW, width), 0)
    return jnp.where(rows == low, 1.0, 0.0).astype(BF16)


def pick(table, index, narrow):
    width = index.shape[1]
    high = table.shape[0] // narrow
    hot = low_hot(index & (LOW - 1), width)
    upper = index >> 8
    wide = jnp.dot(table, hot, preferred_element_type=F32)
    out = wide[:narrow]
    for h in range(1, high):
        out = jnp.where(upper == h, wide[h * narrow : (h + 1) * narrow], out)
    return out


def spread(value, index, high):
    hot = low_hot(index & (LOW - 1), index.shape[1])
    upper = index >> 8
    parts = [jnp.where(upper == h, value, 0.0).astype(BF16) for h in range(high)]
    return contract(jnp.concatenate(parts, axis=0), hot, 1, 1)


def coef_of(weight, basis):
    return contract(weight, basis, 0, 0)


def place():
    g = lax.axis_index("graph")
    return lax.axis_index("dp"), lax.div(g, 8), lax.rem(lax.div(g, 2), 4), lax.rem(g, 2)


def turns():
    y, z, x, c = place()
    return (
        [y] + [lax.rem(y + d, 4) for d in range(1, 4)],
        [z] + [lax.rem(z + d, 8) for d in range(1, 8)],
        [x] + [lax.rem(x + d, 4) for d in range(1, 4)],
        [c, 1 - c],
    )


def far(k):
    odd = lax.rem(k, 2)
    return 4 + lax.div(k, 2) * (1 - odd) - lax.div(k + 1, 2) * odd


def chips_of(dz, sign):
    _, z, x, _ = place()
    own = isinstance(dz, int) and dz == 0
    row = z if own else lax.rem(z + (dz if sign > 0 else 8 - dz), 8)
    return [row * 4 + (lax.rem(x + (a if sign > 0 else 4 - a), 4) if a else x) for a in range(4)]


def for_peers(dz, sign, fn):
    own = isinstance(dz, int) and dz == 0
    for a, q in enumerate(chips_of(dz, sign)):
        if own and a == 0:
            g = lax.axis_index("graph")
            fn(g + 1 - 2 * lax.rem(g, 2))
        else:
            fn(2 * q)
            fn(2 * q + 1)


def row_of(ref, dz, sign):
    return jnp.concatenate([ref[q] for q in chips_of(dz, sign)], axis=1)


def pairs_of(ref, dz, sign):
    return jnp.concatenate(
        [ref[2 * q + c] for q in chips_of(dz, sign) for c in range(2)], axis=1)


def columns_of(ref, dz, sign):
    return jnp.concatenate(
        [ref[:, pl.ds(pl.multiple_of(q * LOW, LOW), LOW)] for q in chips_of(dz, sign)], axis=1)


def put_pairs(ref, dz, sign, value):
    for a, q in enumerate(chips_of(dz, sign)):
        for c in range(2):
            at = (2 * a + c) * 128
            ref[2 * q + c] = value[:, at : at + 128]


def exchange(src, dst, send_sem, recv_sem):
    y = lax.axis_index("dp")
    g = lax.axis_index("graph")

    def out(p):
        return pltpu.make_async_remote_copy(
            src_ref=src.at[p], dst_ref=dst.at[g], send_sem=send_sem.at[p],
            recv_sem=recv_sem.at[g], device_id=(y, p), device_id_type=MESH)

    def back(p):
        return pltpu.make_async_remote_copy(
            src_ref=src.at[p], dst_ref=dst.at[p], send_sem=send_sem.at[p],
            recv_sem=recv_sem.at[p], device_id=(y, p), device_id_type=MESH)

    return out, back


VM = pl.BlockSpec(memory_space=pltpu.VMEM)
HB = pl.BlockSpec(memory_space=pl.ANY)
DENSE = 512
TILE = 16


FAR32 = sorted(range(1, 32), key=lambda j: -(2 - abs(j // 8 - 2)) - (2 - abs(j // 2 % 4 - 2)))

FARCHIPS = sorted(range(1, 32), key=lambda j: -(4 - abs(j // 4 - 4)) - (2 - abs(j % 4 - 2)))


def each(count, fn):
    @pl.loop(1, count)
    def _(j):
        fn(j)


def total_of(ref, count):
    total = ref[0].astype(F32)
    for j in range(1, count):
        total = total + ref[j].astype(F32)
    return total


def plane_sum(send, got, part, got_z, held, sems, scale):
    y, z, x, c = place()
    mine = y * 8 + x * 2 + c
    ts_sem, tr_sem, zs_sem, zr_sem, us_sem, ur_sem = sems

    ys, zs, xs, cs = turns()

    def member(j):
        py, px, pc = ys[j // 8], xs[j // 2 % 4], cs[j % 2]
        return (py, z * 8 + px * 2 + pc), py * 8 + px * 2 + pc

    def copy_t(j):
        device, index = member(j) if isinstance(j, int) else ((y, z * 8 + x * 2 + 1 - c), mine)
        return pltpu.make_async_remote_copy(
            src_ref=send.at[index], dst_ref=got.at[j], send_sem=ts_sem.at[j],
            recv_sem=tr_sem.at[j], device_id=device, device_id_type=MESH)

    def copy_z(j):
        device = (y, zs[j] * 8 + x * 2 + c) if isinstance(j, int) else (y, z * 8 + x * 2 + 1 - c)
        return pltpu.make_async_remote_copy(
            src_ref=part.at[0], dst_ref=got_z.at[z], send_sem=zs_sem.at[j],
            recv_sem=zr_sem.at[j], device_id=device, device_id_type=MESH)

    def copy_u(j):
        device = member(j)[0] if isinstance(j, int) else (y, z * 8 + x * 2 + 1 - c)
        return pltpu.make_async_remote_copy(
            src_ref=part.at[1], dst_ref=held.at[mine], send_sem=us_sem.at[j],
            recv_sem=ur_sem.at[j], device_id=device, device_id_type=MESH)

    def start():
        for j in FAR32:
            copy_t(j).start()

    def along():
        got[0] = send[mine]
        each(32, lambda j: copy_t(j).wait_recv())
        total = total_of(got, 32).astype(part.dtype)
        part[0] = total
        got_z[z] = total
        for j in (4, 3, 5, 2, 6, 1, 7):
            copy_z(j).start()

    def share():
        each(8, lambda j: copy_z(j).wait_recv())
        total = (total_of(got_z, 8) * scale).astype(part.dtype)
        part[1] = total
        held[mine] = total
        for j in FAR32:
            copy_u(j).start()

    def end():
        each(32, lambda j: copy_u(j).wait())
        each(32, lambda j: copy_t(j).wait_send())
        each(8, lambda j: copy_z(j).wait_send())

    return start, along, share, end


def main_kernel(scale, in_ref, down_ref, count_ref, weight_ref, bil_ref,
                edge_in, cot_hbm, basis_hbm, index_hbm, up_hbm, w1_hbm, w2_hbm,
                edge_hbm, big_ref, early_ref, late_ref,
                edge_ref, cot_ref, basis_ref, index_ref, up_ref, w1_ref, w2_ref,
                fetched, wanted, pre_ref, table, outbox, acc, gathered,
                summed, half_s, back1_s, rows1_s, back2_s, backup_s, mixed_s, bil_grad, grad,
                outbox2, returned, back_pre, edge_out,
                send_a, got_p, pair_s, got_a, part_b, got_b, full_b,
                send_e, got_e, part_e, gotz_e, send_t, got_t, part_t, gotz_t,
                load_sem, save_sem, is_sem, ir_sem, rs_sem, rr_sem, qs_sem, qr_sem,
                ps_sem, as_sem, ar_sem, bs_sem, br_sem, cs_sem, cr_sem, ds_sem, dr_sem,
                *plane_sems):
    shards, narrow = fetched.shape[:2]
    rows, wide = edge_ref.shape
    high = rows // LOW
    y, z, x, c = place()
    g = lax.axis_index("graph")
    chip = z * 4 + x
    barrier = pltpu.get_barrier_semaphore()

    def signal(device):
        pl.semaphore_signal(barrier, inc=1, device_id=device, device_id_type=MESH)

    ys, zs, xs, cs = turns()
    for dz in (4, 3, 5, 2, 6, 1, 7, 0):
        for j in range(8):
            if dz or j:
                signal((y, zs[dz] * 8 + xs[j // 2] * 2 + cs[j % 2]))
    for j in range(8, 32):
        signal((ys[j // 8], z * 8 + xs[j // 2 % 4] * 2 + cs[j % 2]))

    parts = 4
    span = rows // parts
    edges = [
        pltpu.make_async_copy(
            edge_in.at[pl.ds(i * span, span)], edge_ref.at[pl.ds(i * span, span)],
            load_sem.at[6 + i])
        for i in range(parts)
    ]
    loads = [
        pltpu.make_async_copy(src, dst, load_sem.at[i])
        for i, (src, dst) in enumerate((
            (basis_hbm, basis_ref), (index_hbm, index_ref), (up_hbm, up_ref), (w1_hbm, w1_ref),
            (w2_hbm, w2_ref), (cot_hbm, cot_ref)))
    ]
    for load in edges + loads:
        load.start()

    wanted[g] = in_ref[g]
    for h in range(high):
        if h * LOW % span == 0:
            edges[h * LOW // span].wait()
        pre = contract(down_ref[...], edge_ref[h * LOW : (h + 1) * LOW], 1, 1)
        pre_ref[:, h * LOW : (h + 1) * LOW] = pre
        table[h * narrow : (h + 1) * narrow] = (pre * sigmoid(pre)).astype(BF16)
    acc[...] = jnp.zeros_like(acc)
    grad[...] = jnp.zeros_like(grad)
    bil_grad[...] = jnp.zeros_like(bil_grad)
    send_e[...] = jnp.zeros_like(send_e)
    pl.semaphore_wait(barrier, shards - 1 + 24)
    ask, asked = exchange(in_ref, wanted, is_sem, ir_sem)
    give, given = exchange(outbox, fetched, rs_sem, rr_sem)

    for dz in (4, 3, 5, 2, 6, 1, 7, 0):
        for j in range(8):
            if dz or j:
                ask(zs[dz] * 8 + xs[j // 2] * 2 + cs[j % 2]).start()

    def serve(dz):
        for_peers(dz, 1, lambda p: asked(p).wait_recv())
        index = pairs_of(wanted, dz, 1)
        put_pairs(outbox, dz, 1, pick(table[...], index, narrow).astype(BF16))
        for_peers(dz, 1, lambda p: give(p).start())

    pl.loop(0, 2)(lambda k: serve(1 + 6 * k))
    pl.loop(0, 5)(lambda k: serve(far(k)))
    serve(0)
    fetched[g] = outbox[g]
    for load in loads:
        load.wait()

    def gather(dz):
        for_peers(dz, -1, lambda p: given(p).wait_recv())
        coef = coef_of(weight_ref[...], columns_of(basis_ref, dz, -1))
        message = coef * pairs_of(fetched, dz, -1).astype(F32)
        acc[...] += spread(message, row_of(index_ref, dz, -1), high)

    pl.loop(0, 2)(lambda k: gather(1 + 6 * k))
    pl.loop(0, 5)(lambda k: gather(far(k)))
    gather(0)

    for h in range(high):
        gathered[:, h * LOW : (h + 1) * LOW] = acc[h * narrow : (h + 1) * narrow].astype(BF16)
    acc[...] = jnp.zeros_like(acc)

    count = count_ref[0, 0]

    @pl.loop(0, rows // DENSE)
    def _(i):
        at = pl.ds(pl.multiple_of(i * DENSE, DENSE), DENSE)
        gat = gathered[:, at]
        mixed = contract(bil_ref[...], gat, 0, 0).astype(BF16)
        mixed_s[:, at] = mixed
        pre_up = contract(mixed, up_ref[...], 0, 0)
        s_up = sigmoid(pre_up)
        half = (edge_ref[at, :].astype(F32) + pre_up * s_up).astype(BF16)
        half_s[at, :] = half
        pre_first = jnp.dot(half, w1_ref[...], preferred_element_type=F32)
        s_first = sigmoid(pre_first)
        rows1 = (pre_first * s_first).astype(BF16)
        rows1_s[at, :] = rows1
        pre_second = jnp.dot(rows1, w2_ref[...], preferred_element_type=F32)
        live = lax.broadcasted_iota(jnp.int32, (DENSE, 1), 0) + i * DENSE < count
        top = cot_ref[at, :].astype(F32) * jnp.where(live, HALF, 0.0)
        back2 = (top * slope_from(pre_second, sigmoid(pre_second))).astype(BF16)
        back2_s[at, :] = back2
        back1 = contract(back2, w2_ref[...], 1, 1) * slope_from(pre_first, s_first)
        back1 = back1.astype(BF16)
        back1_s[at, :] = back1
        total = top + contract(back1, w1_ref[...], 1, 1)
        summed[at, :] = total
        back_up = (total * slope_from(pre_up, s_up)).astype(BF16)
        backup_s[at, :] = back_up
        back_mixed = contract(up_ref[...], back_up, 1, 1).astype(BF16)
        bil_grad[...] += contract(gat, back_mixed, 1, 1)
        turned = jnp.dot(bil_ref[...], back_mixed, preferred_element_type=F32).astype(BF16)
        for q in range(DENSE // LOW):
            where = pl.multiple_of((i * (DENSE // LOW) + q) * narrow, narrow)
            table[pl.ds(where, narrow), :] = turned[:, q * LOW : (q + 1) * LOW]

    bring, brought = exchange(outbox2, returned, qs_sem, qr_sem)

    def answer(dz):
        basis = columns_of(basis_ref, dz, 1)
        got = pick(table[...], row_of(index_ref, dz, 1), narrow)
        put_pairs(outbox2, dz, 1, (got * coef_of(weight_ref[...], basis)).astype(BF16))
        for_peers(dz, 1, lambda p: bring(p).start())
        back_coef = (got * pairs_of(fetched, dz, 1).astype(F32)).astype(BF16)
        grad[...] += contract(basis, back_coef, 1, 1)

    def collect(dz):
        for_peers(dz, -1, lambda p: brought(p).wait_recv())
        value = pairs_of(returned, dz, -1).astype(F32)
        acc[...] += spread(value, pairs_of(wanted, dz, -1), high)

    eighth = wide // 8

    def pair_copy(src, dst, at):
        return pltpu.make_async_remote_copy(
            src_ref=src, dst_ref=dst, send_sem=ps_sem.at[at], recv_sem=ps_sem.at[at + 1],
            device_id=(y, g + 1 - 2 * c), device_id_type=MESH)

    def copy_a(j):
        py = lax.rem(y + j, 4)
        return pltpu.make_async_remote_copy(
            src_ref=pair_s.at[py], dst_ref=got_a.at[j], send_sem=as_sem.at[j],
            recv_sem=ar_sem.at[j], device_id=(py, g), device_id_type=MESH)

    def to_chip(src, dst, send_sem, recv_sem, j, block):
        q = zs[j // 4] * 4 + xs[j % 4]
        return pltpu.make_async_remote_copy(
            src_ref=src.at[q if block is None else block], dst_ref=dst.at[chip],
            send_sem=send_sem.at[q], recv_sem=recv_sem.at[chip], device_id=(y, 2 * q + c),
            device_id_type=MESH)

    def from_chip(src, dst, send_sem, recv_sem, j):
        q = lax.rem(chip + j, 32)
        return pltpu.make_async_remote_copy(
            src_ref=src.at[0], dst_ref=dst.at[q], send_sem=send_sem.at[q],
            recv_sem=recv_sem.at[q], device_id=(y, 2 * q + c), device_id_type=MESH)

    def copy_d(j):
        return pltpu.make_async_remote_copy(
            src_ref=full_b, dst_ref=big_ref.at[c * 4 + y], send_sem=ds_sem.at[j],
            recv_sem=dr_sem.at[j], device_id=(lax.rem(y + j, 4), g), device_id_type=MESH)

    def store_grad(value, columns):
        value = value.astype(BF16)
        for m in range(8):
            send_a[m % 2, m // 2, :, columns] = value[m * eighth : (m + 1) * eighth]

    pl.loop(0, 2)(lambda k: answer(far(k)))
    store_grad(contract(rows1_s[...], back2_s[...], 0, 0), slice(wide, 2 * wide))
    pl.loop(2, 4)(lambda k: answer(far(k)))
    store_grad(contract(half_s[...], back1_s[...], 0, 0), slice(0, wide))
    pair_a = pair_copy(send_a.at[1 - c], got_p, 0)
    pair_a.start()
    pl.loop(4, 7)(lambda k: answer(far(k)))
    answer(0)
    returned[g] = outbox2[g]

    early = plane_sum(send_e, got_e, part_e, gotz_e, early_ref, plane_sems[:6], scale)
    late = plane_sum(send_t, got_t, part_t, gotz_t, late_ref, plane_sems[6:], scale)
    ups = jnp.dot(mixed_s[...], backup_s[...], preferred_element_type=F32).astype(BF16)
    for m in range(16):
        send_e[m] = ups[m // 4 * 16 : m // 4 * 16 + 16, m % 4 * 128 : m % 4 * 128 + 128]
    for m in range(narrow // 16):
        send_e[16 + m, :, :narrow] = bil_grad[m * 16 : (m + 1) * 16, :].astype(BF16)
    send_e[16 + narrow // 16, :, :narrow] = grad[...].astype(BF16)
    early[0]()

    pair_a.wait()
    for j in range(4):
        for r in range(4):
            at = slice(r * TILE, (r + 1) * TILE)
            pair_s[j, at] = (send_a[c, j, at].astype(F32) + got_p[j, at].astype(F32)).astype(BF16)
    each(4, lambda j: copy_a(j).start())
    pl.loop(0, 4)(lambda k: collect(far(k)))
    early[1]()
    collect(far(jnp.int32(4)))
    got_a[0] = pair_s[y]
    each(4, lambda j: copy_a(j).wait_recv())
    for r in range(4):
        at = slice(r * TILE, (r + 1) * TILE)
        total = got_a[0, at].astype(F32)
        for j in range(1, 4):
            total = total + got_a[j, at].astype(F32)
        total = total.astype(BF16)
        for s in range(8):
            part_b[r * 8 + s] = total[:, s * 128 : (s + 1) * 128]
    for j in FARCHIPS:
        to_chip(part_b, got_b, bs_sem, br_sem, j, None).start()
    pl.loop(5, 7)(lambda k: collect(far(k)))
    early[2]()
    collect(0)

    for h in range(high):
        columns = slice(h * LOW, (h + 1) * LOW)
        pre = pre_ref[:, columns]
        back = acc[h * narrow : (h + 1) * narrow]
        back_pre[:, columns] = (back * slope_from(pre, sigmoid(pre))).astype(BF16)
    down = jnp.dot(back_pre[...], edge_ref[...], preferred_element_type=F32)
    for m in range(32):
        send_t[m] = down[m // 4 * 8 : m // 4 * 8 + 8, m % 4 * 128 : m % 4 * 128 + 128]
    late[0]()

    got_b[chip] = part_b[chip]
    each(32, lambda j: from_chip(part_b, got_b, bs_sem, br_sem, j).wait_recv())
    full_b[chip] = (total_of(got_b, 32) * scale).astype(BF16)
    for j in FARCHIPS:
        to_chip(full_b, full_b, cs_sem, cr_sem, j, chip).start()

    blocks = rows // DENSE

    def save(i):
        at = pl.ds(pl.multiple_of(i * DENSE, DENSE), DENSE)
        return pltpu.make_async_copy(edge_out.at[at], edge_hbm.at[at], save_sem.at[i])

    def finish(i):
        at = pl.ds(pl.multiple_of(i * DENSE, DENSE), DENSE)
        add = contract(back_pre[:, at], down_ref[...], 0, 0)
        edge_out[at, :] = (summed[at, :] + add).astype(BF16)

    pl.loop(0, blocks // 2)(finish)
    late[1]()
    each(32, lambda j: from_chip(full_b, full_b, cs_sem, cr_sem, j).wait_recv())
    each(4, lambda j: copy_d(j).start())
    big_ref[c * 4 + y] = full_b[...]
    pl.loop(blocks // 2, blocks)(finish)
    pl.loop(0, blocks)(lambda i: save(i).start())
    late[2]()
    each(4, lambda j: copy_d(j).wait_recv())
    mine = pl.ds(c * 4, 4)
    pair_d = pair_copy(big_ref.at[mine], big_ref.at[mine], 2)
    pair_d.start()
    pl.loop(0, blocks)(lambda i: save(i).wait())

    @pl.loop(1, shards)
    def _(j):
        p = lax.rem(g + j, shards)
        ask(p).wait_send()
        give(p).wait_send()
        bring(p).wait_send()

    each(4, lambda j: copy_a(j).wait_send())
    each(4, lambda j: copy_d(j).wait_send())
    each(32, lambda j: from_chip(part_b, got_b, bs_sem, br_sem, j).wait_send())
    each(32, lambda j: from_chip(full_b, full_b, cs_sem, cr_sem, j).wait_send())
    early[3]()
    late[3]()
    pair_d.wait()


def main(scale, edge_rows, in_index, down_weight, count, basis_weight, bilinear, cotangent, basis,
         out_index, up, first, second):
    shards, _, slots = in_index.shape
    rows, wide = edge_rows.shape
    narrow = down_weight.shape[0]
    high = rows // LOW
    d = pltpu.SemaphoreType.DMA
    shape = jax.ShapeDtypeStruct
    v = pltpu.VMEM
    block = (shards, narrow, slots)
    tiles = (32, TILE, 128)
    halves = (32, TILE // 2, 128)
    plane = [d((32,)), d((32,)), d((8,)), d((8,)), d((32,)), d((32,))]
    return pl.pallas_call(
        functools.partial(main_kernel, scale),
        out_shape=(
            shape((rows, wide), BF16),
            shape((8,) + tiles, BF16),
            shape(tiles, BF16),
            shape(halves, F32),
        ),
        in_specs=[VM, VM, pl.BlockSpec(memory_space=pltpu.SMEM), VM, VM] + [HB] * 7,
        out_specs=(HB, VM, VM, VM),
        scratch_shapes=[
            v(edge_rows.shape, BF16), v(cotangent.shape, BF16), v(basis.shape, BF16), v(out_index.shape, jnp.int32),
            v(up.shape, BF16), v(first.shape, BF16), v(second.shape, BF16),
            v(block, BF16), v(in_index.shape, jnp.int32), v((narrow, rows), F32),
            v((high * narrow, LOW), BF16), v(block, BF16), v((high * narrow, LOW), F32),
            v((narrow, rows), BF16),
            v((rows, wide), F32), v((rows, wide), BF16), v((rows, wide), BF16),
            v((rows, wide), BF16), v((rows, wide), BF16), v((rows, wide), BF16),
            v((narrow, rows), BF16), v((narrow, narrow), F32), v(basis_weight.shape, F32),
            v(block, BF16), v(block, BF16), v((narrow, rows), BF16), v((rows, wide), BF16),
            v((2, 4, wide // 8, 2 * wide), BF16), v((4, wide // 8, 2 * wide), BF16),
            v((4, wide // 8, 2 * wide), BF16), v((4, wide // 8, 2 * wide), BF16),
            v(tiles, BF16), v(tiles, BF16), v(tiles, BF16),
            v(tiles, BF16), v(tiles, BF16), v((2,) + tiles[1:], BF16), v((8,) + tiles[1:], BF16),
            v(halves, F32), v(halves, F32), v((2,) + halves[1:], F32), v((8,) + halves[1:], F32),
            d((10,)), d((rows // DENSE,)),
            d((shards,)), d((shards,)), d((shards,)), d((shards,)), d((shards,)), d((shards,)),
            d((4,)), d((4,)), d((4,)), d((32,)), d((32,)), d((32,)), d((32,)), d((4,)), d((4,)),
        ] + plane + plane,
        compiler_params=pltpu.CompilerParams(
            collective_id=1, has_side_effects=True, vmem_limit_bytes=VMEM_LIMIT),
        name="main",
    )(in_index, down_weight, count, basis_weight, bilinear, edge_rows, cotangent, basis, out_index,
      up, first, second)


def final_kernel(edge_in, big_in, early_ref, late_ref,
                 edge_out, first_out, second_out, down_out, basis_out, bil_out, up_out,
                 edge_buf, big_buf, first_buf, second_buf, in_sem, out_sem, big_sem, grad_sem):
    rows, wide = edge_buf.shape
    parts = in_sem.shape[0]
    span = rows // parts
    narrow = bil_out.shape[0]

    def big(m):
        return pltpu.make_async_copy(big_in.at[m], big_buf.at[m], big_sem.at[m])

    def piece(i):
        at = pl.ds(i * span, span)
        return (
            pltpu.make_async_copy(edge_in.at[at], edge_buf.at[at], in_sem.at[i]),
            pltpu.make_async_copy(edge_buf.at[at], edge_out.at[at], out_sem.at[i]),
        )

    def grads(i):
        at = pl.ds(i * (wide // 2), wide // 2)
        return (
            pltpu.make_async_copy(first_buf.at[at], first_out.at[at], grad_sem.at[i]),
            pltpu.make_async_copy(second_buf.at[at], second_out.at[at], grad_sem.at[2 + i]),
        )

    for m in range(8):
        big(m % 2 * 4 + m // 2).start()
    for i in range(parts):
        piece(i)[0].start()
    for s in range(4):
        for r in range(8):
            down_out[r * 8 : r * 8 + 8, s * 128 : s * 128 + 128] = late_ref[r * 4 + s]
    for m in range(16):
        up_out[m // 4 * 16 : m // 4 * 16 + 16, m % 4 * 128 : m % 4 * 128 + 128] = (
            early_ref[m].astype(F32))
    for m in range(narrow // 16):
        bil_out[m * 16 : (m + 1) * 16, :] = early_ref[16 + m].astype(F32)[:, :narrow]
    basis_out[...] = early_ref[16 + narrow // 16].astype(F32)[:, :narrow]
    for m in range(8):
        block = m % 2 * 4 + m // 2
        big(block).wait()
        for r in range(4):
            at = slice(m * 64 + r * 16, m * 64 + r * 16 + 16)
            for s in range(4):
                columns = slice(s * 128, s * 128 + 128)
                first_buf[at, columns] = big_buf[block, r * 8 + s].astype(F32)
                second_buf[at, columns] = big_buf[block, r * 8 + 4 + s].astype(F32)
        if m % 4 == 3:
            for copy in grads(m // 4):
                copy.start()
    for i in range(parts):
        piece(i)[0].wait()
        piece(i)[1].start()
    for i in range(parts):
        piece(i)[1].wait()
    for i in range(2):
        for copy in grads(i):
            copy.wait()


def final(edge, big, early, late, narrow, bases):
    rows, wide = edge.shape
    shape = jax.ShapeDtypeStruct
    d = pltpu.SemaphoreType.DMA
    smalls = [(narrow, wide), (bases, narrow), (narrow, narrow), (narrow, wide)]
    return pl.pallas_call(
        final_kernel,
        out_shape=(shape((rows, wide), BF16), shape((wide, wide), F32), shape((wide, wide), F32))
        + tuple(shape(s, F32) for s in smalls),
        in_specs=[HB, HB, VM, VM],
        out_specs=(HB, HB, HB) + (VM,) * 4,
        scratch_shapes=[
            pltpu.VMEM((rows, wide), BF16), pltpu.VMEM(big.shape, BF16),
            pltpu.VMEM((wide, wide), F32), pltpu.VMEM((wide, wide), F32),
            d((8,)), d((8,)), d((8,)), d((4,)),
        ],
        compiler_params=pltpu.CompilerParams(vmem_limit_bytes=VMEM_LIMIT),
        name="final",
    )(edge, big, early, late)


def local(
    edge_state,
    cotangent,
    edge_count,
    triplet_basis,
    triplet_in,
    triplet_out,
    down_weight,
    basis_weight,
    bilinear_weight,
    up_weight,
    first_weight,
    second_weight,
):
    edge_rows = edge_state[0]
    row_count = edge_rows.shape[0]
    shards = lax.axis_size("graph")
    bases, narrow = basis_weight.shape
    tri_rows = triplet_in.shape[1]
    out_index = triplet_out[0].reshape(tri_rows // LOW, 1, LOW)
    in_index = triplet_in[0].reshape(shards, 1, tri_rows // shards)
    grad_scale = 1.0 / math.sqrt(lax.axis_size("dp") * shards * row_count)
    edge_grad, big, early, late = main(
        grad_scale, edge_rows, in_index, down_weight.T, edge_count, basis_weight, bilinear_weight,
        cotangent[0], triplet_basis[0], out_index, up_weight, first_weight, second_weight)
    edge_grad, first_grad, second_grad, down_grad, basis_grad, bilinear_grad, up_grad = final(
        edge_grad, big, early, late, narrow, bases)
    return edge_grad[None], down_grad.T, basis_grad, bilinear_grad, up_grad, first_grad, second_grad


def solution(mesh):
    in_specs = (
        P("dp", "graph", None),
        P("dp", "graph", None),
        P("dp", "graph"),
        P("dp", None, "graph"),
        P("dp", "graph"),
        P("dp", "graph"),
        P(),
        P(),
        P(),
        P(),
        P(),
        P(),
    )
    out_specs = (P("dp", "graph", None), P(), P(), P(), P(), P(), P())
    return jax.shard_map(local, mesh=mesh, in_specs=in_specs, out_specs=out_specs, check_vma=False)
```

```python
import functools
import math

import jax
import jax.numpy as jnp
from jax import lax
from jax.experimental import pallas as pl
from jax.experimental.pallas import tpu as pltpu
from jax.sharding import PartitionSpec as P

HALF = 0.7071067811865476
LOW = 256
MESH = pl.DeviceIdType.MESH
F32 = jnp.float32
BF16 = jnp.bfloat16
VMEM_LIMIT = 60 * 1024 * 1024


def sigmoid(value):
    return 0.5 * jnp.tanh(0.5 * value) + 0.5


def slope_from(value, logistic):
    return logistic * (1.0 + value * (1.0 - logistic))


def contract(left, right, left_dim, right_dim):
    return lax.dot_general(
        left, right, (((left_dim,), (right_dim,)), ((), ())), preferred_element_type=jnp.float32
    )


def low_hot(low, width):
    rows = lax.broadcasted_iota(jnp.int32, (LOW, width), 0)
    return jnp.where(rows == low, 1.0, 0.0).astype(BF16)


def pick(table, index, narrow):
    width = index.shape[1]
    high = table.shape[0] // narrow
    hot = low_hot(index & (LOW - 1), width)
    upper = index >> 8
    wide = jnp.dot(table, hot, preferred_element_type=F32)
    out = wide[:narrow]
    for h in range(1, high):
        out = jnp.where(upper == h, wide[h * narrow : (h + 1) * narrow], out)
    return out


def spread(value, index, high):
    hot = low_hot(index & (LOW - 1), index.shape[1])
    upper = index >> 8
    parts = [jnp.where(upper == h, value, 0.0).astype(BF16) for h in range(high)]
    return contract(jnp.concatenate(parts, axis=0), hot, 1, 1)


def coef_of(weight, basis):
    return contract(weight, basis, 0, 0)


def place():
    g = lax.axis_index("graph")
    return lax.axis_index("dp"), lax.div(g, 8), lax.rem(lax.div(g, 2), 4), lax.rem(g, 2)


def turns():
    y, z, x, c = place()
    return (
        [y] + [lax.rem(y + d, 4) for d in range(1, 4)],
        [z] + [lax.rem(z + d, 8) for d in range(1, 8)],
        [x] + [lax.rem(x + d, 4) for d in range(1, 4)],
        [c, 1 - c],
    )


def far(k):
    return 4 - lax.div(k + 1, 2), lax.rem(k + 1, 2)


def chips_of(group, sign):
    _, z, x, _ = place()
    columns = [x] + [lax.rem(x + (a if sign > 0 else 4 - a), 4) for a in range(1, 4)]
    if group is None:
        return [z * 4 + q for q in columns]
    distance, turn = group
    ahead = distance + turn * (8 - 2 * distance)
    back = 8 - ahead
    rows = [lax.rem(z + (d if sign > 0 else 8 - d), 8) for d in (ahead, back)]
    return [rows[a // 2] * 4 + columns[a] for a in range(4)]


def for_peers(group, sign, fn):
    chips = chips_of(group, sign)
    for a in (0, 2, 1, 3):
        q = chips[a]
        if group is None and a == 0:
            g = lax.axis_index("graph")
            fn(g + 1 - 2 * lax.rem(g, 2))
        else:
            fn(2 * q)
            fn(2 * q + 1)


def row_of(ref, group, sign):
    return jnp.concatenate([ref[q] for q in chips_of(group, sign)], axis=1)


def pairs_of(ref, group, sign):
    return jnp.concatenate(
        [ref[2 * q + c] for q in chips_of(group, sign) for c in range(2)], axis=1)


def columns_of(ref, group, sign):
    return jnp.concatenate(
        [ref[:, pl.ds(pl.multiple_of(q * LOW, LOW), LOW)] for q in chips_of(group, sign)], axis=1)


def put_pairs(ref, group, sign, value):
    for a, q in enumerate(chips_of(group, sign)):
        for c in range(2):
            at = (2 * a + c) * 128
            ref[2 * q + c] = value[:, at : at + 128]


def exchange(src, dst, send_sem, recv_sem):
    y = lax.axis_index("dp")
    g = lax.axis_index("graph")

    def out(p):
        return pltpu.make_async_remote_copy(
            src_ref=src.at[p], dst_ref=dst.at[g], send_sem=send_sem.at[p],
            recv_sem=recv_sem.at[g], device_id=(y, p), device_id_type=MESH)

    def back(p):
        return pltpu.make_async_remote_copy(
            src_ref=src.at[p], dst_ref=dst.at[p], send_sem=send_sem.at[p],
            recv_sem=recv_sem.at[p], device_id=(y, p), device_id_type=MESH)

    return out, back


VM = pl.BlockSpec(memory_space=pltpu.VMEM)
HB = pl.BlockSpec(memory_space=pltpu.HBM)
DENSE = 512
TILE = 16


FAR32 = sorted(range(1, 32), key=lambda j: -(2 - abs(j // 8 - 2)) - (2 - abs(j // 2 % 4 - 2)))

FARCHIPS = sorted(range(1, 32), key=lambda j: -(4 - abs(j // 4 - 4)) - (2 - abs(j % 4 - 2)))


def each(count, fn):
    @pl.loop(1, count)
    def _(j):
        fn(j)


def total_of(ref, count):
    total = ref[0].astype(F32)
    for j in range(1, count):
        total = total + ref[j].astype(F32)
    return total


def plane_sum(send, got, part, got_z, held, sems, scale):
    y, z, x, c = place()
    mine = y * 8 + x * 2 + c
    ts_sem, tr_sem, zs_sem, zr_sem, us_sem, ur_sem = sems

    ys, zs, xs, cs = turns()

    def member(j):
        py, px, pc = ys[j // 8], xs[j // 2 % 4], cs[j % 2]
        return (py, z * 8 + px * 2 + pc), py * 8 + px * 2 + pc

    def copy_t(j):
        device, index = member(j) if isinstance(j, int) else ((y, z * 8 + x * 2 + 1 - c), mine)
        return pltpu.make_async_remote_copy(
            src_ref=send.at[index], dst_ref=got.at[j], send_sem=ts_sem.at[j],
            recv_sem=tr_sem.at[j], device_id=device, device_id_type=MESH)

    def copy_z(j):
        device = (y, zs[j] * 8 + x * 2 + c) if isinstance(j, int) else (y, z * 8 + x * 2 + 1 - c)
        return pltpu.make_async_remote_copy(
            src_ref=part.at[0], dst_ref=got_z.at[z], send_sem=zs_sem.at[j],
            recv_sem=zr_sem.at[j], device_id=device, device_id_type=MESH)

    def copy_u(j):
        device = member(j)[0] if isinstance(j, int) else (y, z * 8 + x * 2 + 1 - c)
        return pltpu.make_async_remote_copy(
            src_ref=part.at[1], dst_ref=held.at[mine], send_sem=us_sem.at[j],
            recv_sem=ur_sem.at[j], device_id=device, device_id_type=MESH)

    def start():
        for j in FAR32:
            copy_t(j).start()

    def along():
        got[0] = send[mine]
        each(32, lambda j: copy_t(j).wait_recv())
        total = total_of(got, 32).astype(part.dtype)
        part[0] = total
        got_z[z] = total
        for j in (4, 3, 5, 2, 6, 1, 7):
            copy_z(j).start()

    def share():
        each(8, lambda j: copy_z(j).wait_recv())
        total = (total_of(got_z, 8) * scale).astype(part.dtype)
        part[1] = total
        held[mine] = total
        for j in FAR32:
            copy_u(j).start()

    def end():
        each(32, lambda j: copy_u(j).wait())
        each(32, lambda j: copy_t(j).wait_send())
        each(8, lambda j: copy_z(j).wait_send())

    return start, along, share, end


def main_kernel(scale, in_ref, down_ref, count_ref, weight_ref, bil_ref,
                edge_in, cot_hbm, basis_hbm, index_hbm, up_hbm, w1_hbm, w2_hbm,
                edge_out, big_ref, early_ref, late_ref,
                edge_ref, cot_ref, basis_ref, index_ref, up_ref, w1_ref, w2_ref,
                fetched, wanted, pre_ref, table, outbox, acc, gathered,
                summed, half_s, back1_s, rows1_s, back2_s, backup_s, mixed_s, bil_grad, grad,
                outbox2, returned, back_pre,
                send_a, got_p, pair_s, got_a, part_b, got_b, full_b,
                send_e, got_e, part_e, gotz_e, send_t, got_t, part_t, gotz_t,
                load_sem, is_sem, ir_sem, rs_sem, rr_sem, qs_sem, qr_sem,
                ps_sem, as_sem, ar_sem, bs_sem, br_sem, cs_sem, cr_sem, ds_sem, dr_sem,
                *plane_sems):
    shards, narrow = fetched.shape[:2]
    rows, wide = edge_ref.shape
    high = rows // LOW
    y, z, x, c = place()
    g = lax.axis_index("graph")
    chip = z * 4 + x
    barrier = pltpu.get_barrier_semaphore()

    def signal(device):
        pl.semaphore_signal(barrier, inc=1, device_id=device, device_id_type=MESH)

    ys, zs, xs, cs = turns()
    for dz in (4, 3, 5, 2, 6, 1, 7, 0):
        for j in range(8):
            if dz or j:
                signal((y, zs[dz] * 8 + xs[j // 2] * 2 + cs[j % 2]))
    for j in range(8, 32):
        signal((ys[j // 8], z * 8 + xs[j // 2 % 4] * 2 + cs[j % 2]))

    parts = 4
    span = rows // parts
    edges = [
        pltpu.make_async_copy(
            edge_in.at[pl.ds(i * span, span)], edge_ref.at[pl.ds(i * span, span)],
            load_sem.at[6 + i])
        for i in range(parts)
    ]
    loads = [
        pltpu.make_async_copy(src, dst, load_sem.at[i])
        for i, (src, dst) in enumerate((
            (basis_hbm, basis_ref), (index_hbm, index_ref), (up_hbm, up_ref), (w1_hbm, w1_ref),
            (w2_hbm, w2_ref), (cot_hbm, cot_ref)))
    ]
    for load in edges + loads:
        load.start()

    wanted[g] = in_ref[g]
    for h in range(high):
        if h * LOW % span == 0:
            edges[h * LOW // span].wait()
        pre = contract(down_ref[...], edge_ref[h * LOW : (h + 1) * LOW], 1, 1)
        pre_ref[:, h * LOW : (h + 1) * LOW] = pre
        table[h * narrow : (h + 1) * narrow] = (pre * sigmoid(pre)).astype(BF16)
    acc[...] = jnp.zeros_like(acc)
    grad[...] = jnp.zeros_like(grad)
    bil_grad[...] = jnp.zeros_like(bil_grad)
    send_e[...] = jnp.zeros_like(send_e)
    pl.semaphore_wait(barrier, shards - 1 + 24)
    ask, asked = exchange(in_ref, wanted, is_sem, ir_sem)
    give, given = exchange(outbox, fetched, rs_sem, rr_sem)

    for dz in (4, 3, 5, 2, 6, 1, 7, 0):
        for j in range(8):
            if dz or j:
                ask(zs[dz] * 8 + xs[j // 2] * 2 + cs[j % 2]).start()

    def serve(group):
        for_peers(group, 1, lambda p: asked(p).wait_recv())
        index = pairs_of(wanted, group, 1)
        put_pairs(outbox, group, 1, pick(table[...], index, narrow).astype(BF16))
        for_peers(group, 1, lambda p: give(p).start())

    pl.loop(5, 7)(lambda k: serve(far(k)))
    pl.loop(0, 5)(lambda k: serve(far(k)))
    serve(None)
    fetched[g] = outbox[g]
    for load in loads:
        load.wait()

    def gather(group):
        for_peers(group, -1, lambda p: given(p).wait_recv())
        coef = coef_of(weight_ref[...], columns_of(basis_ref, group, -1))
        message = coef * pairs_of(fetched, group, -1).astype(F32)
        acc[...] += spread(message, row_of(index_ref, group, -1), high)

    pl.loop(5, 7)(lambda k: gather(far(k)))
    pl.loop(0, 5)(lambda k: gather(far(k)))
    gather(None)

    for h in range(high):
        gathered[:, h * LOW : (h + 1) * LOW] = acc[h * narrow : (h + 1) * narrow].astype(BF16)
    acc[...] = jnp.zeros_like(acc)

    count = count_ref[0, 0]

    @pl.loop(0, rows // DENSE)
    def _(i):
        at = pl.ds(pl.multiple_of(i * DENSE, DENSE), DENSE)
        gat = gathered[:, at]
        mixed = contract(bil_ref[...], gat, 0, 0).astype(BF16)
        mixed_s[:, at] = mixed
        pre_up = contract(mixed, up_ref[...], 0, 0)
        s_up = sigmoid(pre_up)
        half = (edge_ref[at, :].astype(F32) + pre_up * s_up).astype(BF16)
        half_s[at, :] = half
        pre_first = jnp.dot(half, w1_ref[...], preferred_element_type=F32)
        s_first = sigmoid(pre_first)
        rows1 = (pre_first * s_first).astype(BF16)
        rows1_s[at, :] = rows1
        pre_second = jnp.dot(rows1, w2_ref[...], preferred_element_type=F32)
        live = lax.broadcasted_iota(jnp.int32, (DENSE, 1), 0) + i * DENSE < count
        top = cot_ref[at, :].astype(F32) * jnp.where(live, HALF, 0.0)
        back2 = (top * slope_from(pre_second, sigmoid(pre_second))).astype(BF16)
        back2_s[at, :] = back2
        back1 = contract(back2, w2_ref[...], 1, 1) * slope_from(pre_first, s_first)
        back1 = back1.astype(BF16)
        back1_s[at, :] = back1
        total = top + contract(back1, w1_ref[...], 1, 1)
        summed[at, :] = total
        back_up = (total * slope_from(pre_up, s_up)).astype(BF16)
        backup_s[at, :] = back_up
        back_mixed = contract(up_ref[...], back_up, 1, 1).astype(BF16)
        bil_grad[...] += contract(gat, back_mixed, 1, 1)
        turned = jnp.dot(bil_ref[...], back_mixed, preferred_element_type=F32).astype(BF16)
        for q in range(DENSE // LOW):
            where = pl.multiple_of((i * (DENSE // LOW) + q) * narrow, narrow)
            table[pl.ds(where, narrow), :] = turned[:, q * LOW : (q + 1) * LOW]

    bring, brought = exchange(outbox2, returned, qs_sem, qr_sem)

    def answer(group):
        basis = columns_of(basis_ref, group, 1)
        got = pick(table[...], row_of(index_ref, group, 1), narrow)
        put_pairs(outbox2, group, 1, (got * coef_of(weight_ref[...], basis)).astype(BF16))
        for_peers(group, 1, lambda p: bring(p).start())
        back_coef = (got * pairs_of(fetched, group, 1).astype(F32)).astype(BF16)
        grad[...] += contract(basis, back_coef, 1, 1)

    def collect(group):
        for_peers(group, -1, lambda p: brought(p).wait_recv())
        value = pairs_of(returned, group, -1).astype(F32)
        acc[...] += spread(value, pairs_of(wanted, group, -1), high)

    eighth = wide // 8

    def pair_copy(src, dst, at):
        return pltpu.make_async_remote_copy(
            src_ref=src, dst_ref=dst, send_sem=ps_sem.at[at], recv_sem=ps_sem.at[at + 1],
            device_id=(y, g + 1 - 2 * c), device_id_type=MESH)

    def copy_a(j):
        py = lax.rem(y + j, 4)
        return pltpu.make_async_remote_copy(
            src_ref=pair_s.at[py], dst_ref=got_a.at[j], send_sem=as_sem.at[j],
            recv_sem=ar_sem.at[j], device_id=(py, g), device_id_type=MESH)

    def to_chip(src, dst, send_sem, recv_sem, j, block):
        q = zs[j // 4] * 4 + xs[j % 4]
        return pltpu.make_async_remote_copy(
            src_ref=src.at[q if block is None else block], dst_ref=dst.at[chip],
            send_sem=send_sem.at[q], recv_sem=recv_sem.at[chip], device_id=(y, 2 * q + c),
            device_id_type=MESH)

    def from_chip(src, dst, send_sem, recv_sem, j):
        q = lax.rem(chip + j, 32)
        return pltpu.make_async_remote_copy(
            src_ref=src.at[0], dst_ref=dst.at[q], send_sem=send_sem.at[q],
            recv_sem=recv_sem.at[q], device_id=(y, 2 * q + c), device_id_type=MESH)

    def copy_d(j):
        return pltpu.make_async_remote_copy(
            src_ref=full_b, dst_ref=big_ref.at[c * 4 + y], send_sem=ds_sem.at[j],
            recv_sem=dr_sem.at[j], device_id=(lax.rem(y + j, 4), g), device_id_type=MESH)

    def store_grad(value, columns):
        value = value.astype(BF16)
        for m in range(8):
            send_a[m % 2, m // 2, :, columns] = value[m * eighth : (m + 1) * eighth]

    pl.loop(0, 2)(lambda k: answer(far(k)))
    store_grad(contract(rows1_s[...], back2_s[...], 0, 0), slice(wide, 2 * wide))
    pl.loop(2, 4)(lambda k: answer(far(k)))
    store_grad(contract(half_s[...], back1_s[...], 0, 0), slice(0, wide))
    pair_a = pair_copy(send_a.at[1 - c], got_p, 0)
    pair_a.start()
    pl.loop(4, 7)(lambda k: answer(far(k)))
    answer(None)
    returned[g] = outbox2[g]

    early = plane_sum(send_e, got_e, part_e, gotz_e, early_ref, plane_sems[:6], scale)
    late = plane_sum(send_t, got_t, part_t, gotz_t, late_ref, plane_sems[6:], scale)
    ups = jnp.dot(mixed_s[...], backup_s[...], preferred_element_type=F32).astype(BF16)
    for m in range(16):
        send_e[m] = ups[m // 4 * 16 : m // 4 * 16 + 16, m % 4 * 128 : m % 4 * 128 + 128]
    for m in range(narrow // 16):
        send_e[16 + m, :, :narrow] = bil_grad[m * 16 : (m + 1) * 16, :].astype(BF16)
    send_e[16 + narrow // 16, :, :narrow] = grad[...].astype(BF16)
    early[0]()

    pair_a.wait()
    for j in range(4):
        for r in range(4):
            at = slice(r * TILE, (r + 1) * TILE)
            pair_s[j, at] = (send_a[c, j, at].astype(F32) + got_p[j, at].astype(F32)).astype(BF16)
    each(4, lambda j: copy_a(j).start())
    pl.loop(0, 4)(lambda k: collect(far(k)))
    early[1]()
    collect(far(jnp.int32(4)))
    got_a[0] = pair_s[y]
    each(4, lambda j: copy_a(j).wait_recv())
    for r in range(4):
        at = slice(r * TILE, (r + 1) * TILE)
        total = got_a[0, at].astype(F32)
        for j in range(1, 4):
            total = total + got_a[j, at].astype(F32)
        total = total.astype(BF16)
        for s in range(8):
            part_b[r * 8 + s] = total[:, s * 128 : (s + 1) * 128]
    for j in FARCHIPS:
        to_chip(part_b, got_b, bs_sem, br_sem, j, None).start()
    pl.loop(5, 7)(lambda k: collect(far(k)))
    early[2]()
    collect(None)

    for h in range(high):
        columns = slice(h * LOW, (h + 1) * LOW)
        pre = pre_ref[:, columns]
        back = acc[h * narrow : (h + 1) * narrow]
        back_pre[:, columns] = (back * slope_from(pre, sigmoid(pre))).astype(BF16)
    down = jnp.dot(back_pre[...], edge_ref[...], preferred_element_type=F32)
    for m in range(32):
        send_t[m] = down[m // 4 * 8 : m // 4 * 8 + 8, m % 4 * 128 : m % 4 * 128 + 128]
    late[0]()

    got_b[chip] = part_b[chip]
    each(32, lambda j: from_chip(part_b, got_b, bs_sem, br_sem, j).wait_recv())
    full_b[chip] = (total_of(got_b, 32) * scale).astype(BF16)
    for j in FARCHIPS:
        to_chip(full_b, full_b, cs_sem, cr_sem, j, chip).start()

    blocks = rows // DENSE

    def finish(i):
        at = pl.ds(pl.multiple_of(i * DENSE, DENSE), DENSE)
        add = contract(back_pre[:, at], down_ref[...], 0, 0)
        edge_out[at, :] = (summed[at, :] + add).astype(BF16)

    pl.loop(0, blocks // 2)(finish)
    late[1]()
    each(32, lambda j: from_chip(full_b, full_b, cs_sem, cr_sem, j).wait_recv())
    each(4, lambda j: copy_d(j).start())
    big_ref[c * 4 + y] = full_b[...]
    pl.loop(blocks // 2, blocks)(finish)
    late[2]()
    each(4, lambda j: copy_d(j).wait_recv())
    mine = pl.ds(c * 4, 4)
    pair_d = pair_copy(big_ref.at[mine], big_ref.at[mine], 2)
    pair_d.start()

    @pl.loop(1, shards)
    def _(j):
        p = lax.rem(g + j, shards)
        ask(p).wait_send()
        give(p).wait_send()
        bring(p).wait_send()

    each(4, lambda j: copy_a(j).wait_send())
    each(4, lambda j: copy_d(j).wait_send())
    each(32, lambda j: from_chip(part_b, got_b, bs_sem, br_sem, j).wait_send())
    each(32, lambda j: from_chip(full_b, full_b, cs_sem, cr_sem, j).wait_send())
    early[3]()
    late[3]()
    pair_d.wait()


def main(scale, edge_rows, in_index, down_weight, count, basis_weight, bilinear, cotangent, basis,
         out_index, up, first, second):
    shards, _, slots = in_index.shape
    rows, wide = edge_rows.shape
    narrow = down_weight.shape[0]
    high = rows // LOW
    d = pltpu.SemaphoreType.DMA
    shape = jax.ShapeDtypeStruct
    v = pltpu.VMEM
    block = (shards, narrow, slots)
    tiles = (32, TILE, 128)
    halves = (32, TILE // 2, 128)
    plane = [d((32,)), d((32,)), d((8,)), d((8,)), d((32,)), d((32,))]
    return pl.pallas_call(
        functools.partial(main_kernel, scale),
        out_shape=(
            shape((rows, wide), BF16),
            shape((8,) + tiles, BF16),
            shape(tiles, BF16),
            shape(halves, F32),
        ),
        in_specs=[VM, VM, pl.BlockSpec(memory_space=pltpu.SMEM), VM, VM] + [HB] * 7,
        out_specs=(VM,) * 4,
        scratch_shapes=[
            v(edge_rows.shape, BF16), v(cotangent.shape, BF16), v(basis.shape, BF16), v(out_index.shape, jnp.int32),
            v(up.shape, BF16), v(first.shape, BF16), v(second.shape, BF16),
            v(block, BF16), v(in_index.shape, jnp.int32), v((narrow, rows), F32),
            v((high * narrow, LOW), BF16), v(block, BF16), v((high * narrow, LOW), F32),
            v((narrow, rows), BF16),
            v((rows, wide), F32), v((rows, wide), BF16), v((rows, wide), BF16),
            v((rows, wide), BF16), v((rows, wide), BF16), v((rows, wide), BF16),
            v((narrow, rows), BF16), v((narrow, narrow), F32), v(basis_weight.shape, F32),
            v(block, BF16), v(block, BF16), v((narrow, rows), BF16),
            v((2, 4, wide // 8, 2 * wide), BF16), v((4, wide // 8, 2 * wide), BF16),
            v((4, wide // 8, 2 * wide), BF16), v((4, wide // 8, 2 * wide), BF16),
            v(tiles, BF16), v(tiles, BF16), v(tiles, BF16),
            v(tiles, BF16), v(tiles, BF16), v((2,) + tiles[1:], BF16), v((8,) + tiles[1:], BF16),
            v(halves, F32), v(halves, F32), v((2,) + halves[1:], F32), v((8,) + halves[1:], F32),
            d((10,)),
            d((shards,)), d((shards,)), d((shards,)), d((shards,)), d((shards,)), d((shards,)),
            d((4,)), d((4,)), d((4,)), d((32,)), d((32,)), d((32,)), d((32,)), d((4,)), d((4,)),
        ] + plane + plane,
        compiler_params=pltpu.CompilerParams(
            collective_id=1, has_side_effects=True, vmem_limit_bytes=48 * 1024 * 1024),
        name="main",
    )(in_index, down_weight, count, basis_weight, bilinear, edge_rows, cotangent, basis, out_index,
      up, first, second)


def final_kernel(edge_ref, big_ref, early_ref, late_ref,
                 edge_out, first_out, second_out, down_out, basis_out, bil_out, up_out,
                 first_buf, second_buf, edge_sem, grad_sem):
    rows, wide = edge_ref.shape
    parts = edge_sem.shape[0]
    span = rows // parts
    narrow = bil_out.shape[0]

    def piece(i):
        at = pl.ds(i * span, span)
        return pltpu.make_async_copy(edge_ref.at[at], edge_out.at[at], edge_sem.at[i])

    def grads(i, buf, out, sem):
        at = pl.ds(i * (wide // 2), wide // 2)
        return pltpu.make_async_copy(buf.at[at], out.at[at], grad_sem.at[sem])

    for i in range(parts):
        piece(i).start()
    for m in range(8):
        block = m % 2 * 4 + m // 2
        for r in range(4):
            at = slice(m * 64 + r * 16, m * 64 + r * 16 + 16)
            for s in range(4):
                columns = slice(s * 128, s * 128 + 128)
                first_buf[at, columns] = big_ref[block, r * 8 + s].astype(F32)
                second_buf[at, columns] = big_ref[block, r * 8 + 4 + s].astype(F32)
        if m % 4 == 3:
            grads(m // 4, first_buf, first_out, m // 4).start()
            grads(m // 4, second_buf, second_out, 2 + m // 4).start()
    for s in range(4):
        for r in range(8):
            down_out[r * 8 : r * 8 + 8, s * 128 : s * 128 + 128] = late_ref[r * 4 + s]
    for m in range(16):
        up_out[m // 4 * 16 : m // 4 * 16 + 16, m % 4 * 128 : m % 4 * 128 + 128] = (
            early_ref[m].astype(F32))
    for m in range(narrow // 16):
        bil_out[m * 16 : (m + 1) * 16, :] = early_ref[16 + m].astype(F32)[:, :narrow]
    basis_out[...] = early_ref[16 + narrow // 16].astype(F32)[:, :narrow]
    for i in range(2):
        grads(i, first_buf, first_out, i).wait()
        grads(i, second_buf, second_out, 2 + i).wait()
    for i in range(parts):
        piece(i).wait()


def final(edge, big, early, late, narrow, bases):
    rows, wide = edge.shape
    shape = jax.ShapeDtypeStruct
    d = pltpu.SemaphoreType.DMA
    smalls = [(narrow, wide), (bases, narrow), (narrow, narrow), (narrow, wide)]
    return pl.pallas_call(
        final_kernel,
        out_shape=(shape((rows, wide), BF16), shape((wide, wide), F32), shape((wide, wide), F32))
        + tuple(shape(s, F32) for s in smalls),
        in_specs=[VM] * 4,
        out_specs=(HB, HB, HB) + (VM,) * 4,
        scratch_shapes=[
            pltpu.VMEM((wide, wide), F32), pltpu.VMEM((wide, wide), F32), d((4,)), d((4,)),
        ],
        compiler_params=pltpu.CompilerParams(vmem_limit_bytes=12 * 1024 * 1024),
        name="final",
    )(edge, big, early, late)


def local(
    edge_state,
    cotangent,
    edge_count,
    triplet_basis,
    triplet_in,
    triplet_out,
    down_weight,
    basis_weight,
    bilinear_weight,
    up_weight,
    first_weight,
    second_weight,
):
    edge_rows = edge_state[0]
    row_count = edge_rows.shape[0]
    shards = lax.axis_size("graph")
    bases, narrow = basis_weight.shape
    tri_rows = triplet_in.shape[1]
    out_index = triplet_out[0].reshape(tri_rows // LOW, 1, LOW)
    in_index = triplet_in[0].reshape(shards, 1, tri_rows // shards)
    grad_scale = 1.0 / math.sqrt(lax.axis_size("dp") * shards * row_count)
    edge_grad, big, early, late = main(
        grad_scale, edge_rows, in_index, down_weight.T, edge_count, basis_weight, bilinear_weight,
        cotangent[0], triplet_basis[0], out_index, up_weight, first_weight, second_weight)
    edge_grad, first_grad, second_grad, down_grad, basis_grad, bilinear_grad, up_grad = final(
        edge_grad, big, early, late, narrow, bases)
    return edge_grad[None], down_grad.T, basis_grad, bilinear_grad, up_grad, first_grad, second_grad


def solution(mesh):
    in_specs = (
        P("dp", "graph", None),
        P("dp", "graph", None),
        P("dp", "graph"),
        P("dp", None, "graph"),
        P("dp", "graph"),
        P("dp", "graph"),
        P(),
        P(),
        P(),
        P(),
        P(),
        P(),
    )
    out_specs = (P("dp", "graph", None), P(), P(), P(), P(), P(), P())
    return jax.shard_map(local, mesh=mesh, in_specs=in_specs, out_specs=out_specs, check_vma=False)
```

```python
import functools
import math

import jax
import jax.numpy as jnp
from jax import lax
from jax.experimental import pallas as pl
from jax.experimental.pallas import tpu as pltpu
from jax.sharding import PartitionSpec as P

HALF = 0.7071067811865476
LOW = 256
MESH = pl.DeviceIdType.MESH
F32 = jnp.float32
BF16 = jnp.bfloat16
VMEM_LIMIT = 60 * 1024 * 1024


def sigmoid(value):
    return 0.5 * jnp.tanh(0.5 * value) + 0.5


def slope_from(value, logistic):
    return logistic * (1.0 + value * (1.0 - logistic))


def contract(left, right, left_dim, right_dim):
    return lax.dot_general(
        left, right, (((left_dim,), (right_dim,)), ((), ())), preferred_element_type=jnp.float32
    )


def low_hot(low, width):
    rows = lax.broadcasted_iota(jnp.int32, (LOW, width), 0)
    return jnp.where(rows == low, 1.0, 0.0).astype(BF16)


def pick(table, index, narrow):
    width = index.shape[1]
    high = table.shape[0] // narrow
    hot = low_hot(index & (LOW - 1), width)
    upper = index >> 8
    wide = jnp.dot(table, hot, preferred_element_type=F32)
    out = wide[:narrow]
    for h in range(1, high):
        out = jnp.where(upper == h, wide[h * narrow : (h + 1) * narrow], out)
    return out


def spread(value, index, high):
    hot = low_hot(index & (LOW - 1), index.shape[1])
    upper = index >> 8
    parts = [jnp.where(upper == h, value, 0.0).astype(BF16) for h in range(high)]
    return contract(jnp.concatenate(parts, axis=0), hot, 1, 1)


def coef_of(weight, basis):
    return contract(weight, basis, 0, 0)


def place():
    g = lax.axis_index("graph")
    return lax.axis_index("dp"), lax.div(g, 8), lax.rem(lax.div(g, 2), 4), lax.rem(g, 2)


def turns():
    y, z, x, c = place()
    return (
        [y] + [lax.rem(y + d, 4) for d in range(1, 4)],
        [z] + [lax.rem(z + d, 8) for d in range(1, 8)],
        [x] + [lax.rem(x + d, 4) for d in range(1, 4)],
        [c, 1 - c],
    )


def far(k):
    return 4 - lax.div(k + 1, 2), lax.rem(k + 1, 2)


def chips_of(group, sign):
    _, z, x, _ = place()
    columns = [x] + [lax.rem(x + (a if sign > 0 else 4 - a), 4) for a in range(1, 4)]
    if group is None:
        return [z * 4 + q for q in columns]
    distance, turn = group
    ahead = distance + turn * (8 - 2 * distance)
    back = 8 - ahead
    rows = [lax.rem(z + (d if sign > 0 else 8 - d), 8) for d in (ahead, back)]
    return [rows[a // 2] * 4 + columns[a] for a in range(4)]


def for_peers(group, sign, fn):
    chips = chips_of(group, sign)
    for a in (0, 2, 1, 3):
        q = chips[a]
        if group is None and a == 0:
            g = lax.axis_index("graph")
            fn(g + 1 - 2 * lax.rem(g, 2))
        else:
            fn(2 * q)
            fn(2 * q + 1)


def row_of(ref, group, sign):
    return jnp.concatenate([ref[q] for q in chips_of(group, sign)], axis=1)


def pairs_of(ref, group, sign):
    return jnp.concatenate(
        [ref[2 * q + c] for q in chips_of(group, sign) for c in range(2)], axis=1)


def columns_of(ref, group, sign):
    return jnp.concatenate(
        [ref[:, pl.ds(pl.multiple_of(q * LOW, LOW), LOW)] for q in chips_of(group, sign)], axis=1)


def put_pairs(ref, group, sign, value):
    for a, q in enumerate(chips_of(group, sign)):
        for c in range(2):
            at = (2 * a + c) * 128
            ref[2 * q + c] = value[:, at : at + 128]


def exchange(src, dst, send_sem, recv_sem):
    y = lax.axis_index("dp")
    g = lax.axis_index("graph")

    def out(p):
        return pltpu.make_async_remote_copy(
            src_ref=src.at[p], dst_ref=dst.at[g], send_sem=send_sem.at[p],
            recv_sem=recv_sem.at[g], device_id=(y, p), device_id_type=MESH)

    def back(p):
        return pltpu.make_async_remote_copy(
            src_ref=src.at[p], dst_ref=dst.at[p], send_sem=send_sem.at[p],
            recv_sem=recv_sem.at[p], device_id=(y, p), device_id_type=MESH)

    return out, back


VM = pl.BlockSpec(memory_space=pltpu.VMEM)
HB = pl.BlockSpec(memory_space=pltpu.HBM)
DENSE = 512
TILE = 16


FAR32 = sorted(range(1, 32), key=lambda j: -(2 - abs(j // 8 - 2)) - (2 - abs(j // 2 % 4 - 2)))

FARCHIPS = sorted(range(1, 32), key=lambda j: -(4 - abs(j // 4 - 4)) - (2 - abs(j % 4 - 2)))


def each(count, fn):
    @pl.loop(1, count)
    def _(j):
        fn(j)


def total_of(ref, count):
    total = ref[0].astype(F32)
    for j in range(1, count):
        total = total + ref[j].astype(F32)
    return total


def plane_sum(send, got, part, got_z, held, sems, scale):
    y, z, x, c = place()
    mine = y * 8 + x * 2 + c
    ts_sem, tr_sem, zs_sem, zr_sem, us_sem, ur_sem = sems

    ys, zs, xs, cs = turns()

    def member(j):
        py, px, pc = ys[j // 8], xs[j // 2 % 4], cs[j % 2]
        return (py, z * 8 + px * 2 + pc), py * 8 + px * 2 + pc

    def copy_t(j):
        device, index = member(j) if isinstance(j, int) else ((y, z * 8 + x * 2 + 1 - c), mine)
        return pltpu.make_async_remote_copy(
            src_ref=send.at[index], dst_ref=got.at[j], send_sem=ts_sem.at[j],
            recv_sem=tr_sem.at[j], device_id=device, device_id_type=MESH)

    def copy_z(j):
        device = (y, zs[j] * 8 + x * 2 + c) if isinstance(j, int) else (y, z * 8 + x * 2 + 1 - c)
        return pltpu.make_async_remote_copy(
            src_ref=part.at[0], dst_ref=got_z.at[z], send_sem=zs_sem.at[j],
            recv_sem=zr_sem.at[j], device_id=device, device_id_type=MESH)

    def copy_u(j):
        device = member(j)[0] if isinstance(j, int) else (y, z * 8 + x * 2 + 1 - c)
        return pltpu.make_async_remote_copy(
            src_ref=part.at[1], dst_ref=held.at[mine], send_sem=us_sem.at[j],
            recv_sem=ur_sem.at[j], device_id=device, device_id_type=MESH)

    def start():
        for j in FAR32:
            copy_t(j).start()

    def along():
        got[0] = send[mine]
        each(32, lambda j: copy_t(j).wait_recv())
        total = total_of(got, 32).astype(part.dtype)
        part[0] = total
        got_z[z] = total
        for j in (4, 3, 5, 2, 6, 1, 7):
            copy_z(j).start()

    def share():
        each(8, lambda j: copy_z(j).wait_recv())
        total = (total_of(got_z, 8) * scale).astype(part.dtype)
        part[1] = total
        held[mine] = total
        for j in FAR32:
            copy_u(j).start()

    def end():
        each(32, lambda j: copy_u(j).wait())
        each(32, lambda j: copy_t(j).wait_send())
        each(8, lambda j: copy_z(j).wait_send())

    return start, along, share, end


def main_kernel(scale, count_ref, in_hbm, down_hbm, weight_hbm, bil_hbm, edge_in, cot_hbm, basis_hbm, index_hbm, up_hbm, w1_hbm, w2_hbm,
                edge_out, big_ref, early_ref, late_ref,
                in_ref, down_ref, weight_ref, bil_ref, edge_ref, cot_ref, basis_ref, index_ref, up_ref, w1_ref, w2_ref,
                fetched, wanted, pre_ref, table, outbox, acc, gathered,
                summed, half_s, back1_s, rows1_s, back2_s, backup_s, mixed_s, bil_grad, grad,
                outbox2, returned, back_pre,
                send_a, got_p, pair_s, got_a, part_b, got_b, full_b,
                send_e, got_e, part_e, gotz_e, send_t, got_t, part_t, gotz_t,
                load_sem, is_sem, ir_sem, rs_sem, rr_sem, qs_sem, qr_sem,
                ps_sem, as_sem, ar_sem, bs_sem, br_sem, cs_sem, cr_sem, ds_sem, dr_sem,
                *plane_sems):
    shards, narrow = fetched.shape[:2]
    rows, wide = edge_ref.shape
    high = rows // LOW
    y, z, x, c = place()
    g = lax.axis_index("graph")
    chip = z * 4 + x
    barrier = pltpu.get_barrier_semaphore()

    def signal(device):
        pl.semaphore_signal(barrier, inc=1, device_id=device, device_id_type=MESH)

    ys, zs, xs, cs = turns()
    for dz in (4, 3, 5, 2, 6, 1, 7, 0):
        for j in range(8):
            if dz or j:
                signal((y, zs[dz] * 8 + xs[j // 2] * 2 + cs[j % 2]))
    for j in range(8, 32):
        signal((ys[j // 8], z * 8 + xs[j // 2 % 4] * 2 + cs[j % 2]))

    parts = 4
    span = rows // parts
    edges = [
        pltpu.make_async_copy(
            edge_in.at[pl.ds(i * span, span)], edge_ref.at[pl.ds(i * span, span)],
            load_sem.at[8 + i])
        for i in range(parts)
    ]
    loads = [
        pltpu.make_async_copy(src, dst, load_sem.at[i])
        for i, (src, dst) in enumerate((
            (basis_hbm, basis_ref), (index_hbm, index_ref), (up_hbm, up_ref), (w1_hbm, w1_ref),
            (w2_hbm, w2_ref), (cot_hbm, cot_ref), (weight_hbm, weight_ref), (bil_hbm, bil_ref)))
    ]
    heads = [
        pltpu.make_async_copy(in_hbm, in_ref, load_sem.at[12]),
        pltpu.make_async_copy(down_hbm, down_ref, load_sem.at[13]),
    ]
    for load in heads + edges + loads:
        load.start()

    for load in heads:
        load.wait()
    wanted[g] = in_ref[g]
    for h in range(high):
        if h * LOW % span == 0:
            edges[h * LOW // span].wait()
        pre = contract(down_ref[...], edge_ref[h * LOW : (h + 1) * LOW], 1, 1)
        pre_ref[:, h * LOW : (h + 1) * LOW] = pre
        table[h * narrow : (h + 1) * narrow] = (pre * sigmoid(pre)).astype(BF16)
    acc[...] = jnp.zeros_like(acc)
    grad[...] = jnp.zeros_like(grad)
    bil_grad[...] = jnp.zeros_like(bil_grad)
    send_e[...] = jnp.zeros_like(send_e)
    pl.semaphore_wait(barrier, shards - 1 + 24)
    ask, asked = exchange(in_ref, wanted, is_sem, ir_sem)
    give, given = exchange(outbox, fetched, rs_sem, rr_sem)

    for dz in (4, 3, 5, 2, 6, 1, 7, 0):
        for j in range(8):
            if dz or j:
                ask(zs[dz] * 8 + xs[j // 2] * 2 + cs[j % 2]).start()

    def serve(group):
        for_peers(group, 1, lambda p: asked(p).wait_recv())
        index = pairs_of(wanted, group, 1)
        put_pairs(outbox, group, 1, pick(table[...], index, narrow).astype(BF16))
        for_peers(group, 1, lambda p: give(p).start())

    pl.loop(5, 7)(lambda k: serve(far(k)))
    pl.loop(0, 5)(lambda k: serve(far(k)))
    serve(None)
    fetched[g] = outbox[g]
    for load in loads:
        load.wait()

    def gather(group):
        for_peers(group, -1, lambda p: given(p).wait_recv())
        coef = coef_of(weight_ref[...], columns_of(basis_ref, group, -1))
        message = coef * pairs_of(fetched, group, -1).astype(F32)
        acc[...] += spread(message, row_of(index_ref, group, -1), high)

    pl.loop(5, 7)(lambda k: gather(far(k)))
    pl.loop(0, 5)(lambda k: gather(far(k)))
    gather(None)

    for h in range(high):
        gathered[:, h * LOW : (h + 1) * LOW] = acc[h * narrow : (h + 1) * narrow].astype(BF16)
    acc[...] = jnp.zeros_like(acc)

    count = count_ref[0, 0]

    @pl.loop(0, rows // DENSE)
    def _(i):
        at = pl.ds(pl.multiple_of(i * DENSE, DENSE), DENSE)
        gat = gathered[:, at]
        mixed = contract(bil_ref[...], gat, 0, 0).astype(BF16)
        mixed_s[:, at] = mixed
        pre_up = contract(mixed, up_ref[...], 0, 0)
        s_up = sigmoid(pre_up)
        half = (edge_ref[at, :].astype(F32) + pre_up * s_up).astype(BF16)
        half_s[at, :] = half
        pre_first = jnp.dot(half, w1_ref[...], preferred_element_type=F32)
        s_first = sigmoid(pre_first)
        rows1 = (pre_first * s_first).astype(BF16)
        rows1_s[at, :] = rows1
        pre_second = jnp.dot(rows1, w2_ref[...], preferred_element_type=F32)
        live = lax.broadcasted_iota(jnp.int32, (DENSE, 1), 0) + i * DENSE < count
        top = cot_ref[at, :].astype(F32) * jnp.where(live, HALF, 0.0)
        back2 = (top * slope_from(pre_second, sigmoid(pre_second))).astype(BF16)
        back2_s[at, :] = back2
        back1 = contract(back2, w2_ref[...], 1, 1) * slope_from(pre_first, s_first)
        back1 = back1.astype(BF16)
        back1_s[at, :] = back1
        total = top + contract(back1, w1_ref[...], 1, 1)
        summed[at, :] = total
        back_up = (total * slope_from(pre_up, s_up)).astype(BF16)
        backup_s[at, :] = back_up
        back_mixed = contract(up_ref[...], back_up, 1, 1).astype(BF16)
        bil_grad[...] += contract(gat, back_mixed, 1, 1)
        turned = jnp.dot(bil_ref[...], back_mixed, preferred_element_type=F32).astype(BF16)
        for q in range(DENSE // LOW):
            where = pl.multiple_of((i * (DENSE // LOW) + q) * narrow, narrow)
            table[pl.ds(where, narrow), :] = turned[:, q * LOW : (q + 1) * LOW]

    bring, brought = exchange(outbox2, returned, qs_sem, qr_sem)

    def answer(group):
        basis = columns_of(basis_ref, group, 1)
        got = pick(table[...], row_of(index_ref, group, 1), narrow)
        put_pairs(outbox2, group, 1, (got * coef_of(weight_ref[...], basis)).astype(BF16))
        for_peers(group, 1, lambda p: bring(p).start())
        back_coef = (got * pairs_of(fetched, group, 1).astype(F32)).astype(BF16)
        grad[...] += contract(basis, back_coef, 1, 1)

    def collect(group):
        for_peers(group, -1, lambda p: brought(p).wait_recv())
        value = pairs_of(returned, group, -1).astype(F32)
        acc[...] += spread(value, pairs_of(wanted, group, -1), high)

    eighth = wide // 8

    def pair_copy(src, dst, at):
        return pltpu.make_async_remote_copy(
            src_ref=src, dst_ref=dst, send_sem=ps_sem.at[at], recv_sem=ps_sem.at[at + 1],
            device_id=(y, g + 1 - 2 * c), device_id_type=MESH)

    def copy_a(j):
        py = lax.rem(y + j, 4)
        return pltpu.make_async_remote_copy(
            src_ref=pair_s.at[py], dst_ref=got_a.at[j], send_sem=as_sem.at[j],
            recv_sem=ar_sem.at[j], device_id=(py, g), device_id_type=MESH)

    def to_chip(src, dst, send_sem, recv_sem, j, block):
        q = zs[j // 4] * 4 + xs[j % 4]
        return pltpu.make_async_remote_copy(
            src_ref=src.at[q if block is None else block], dst_ref=dst.at[chip],
            send_sem=send_sem.at[q], recv_sem=recv_sem.at[chip], device_id=(y, 2 * q + c),
            device_id_type=MESH)

    def from_chip(src, dst, send_sem, recv_sem, j):
        q = lax.rem(chip + j, 32)
        return pltpu.make_async_remote_copy(
            src_ref=src.at[0], dst_ref=dst.at[q], send_sem=send_sem.at[q],
            recv_sem=recv_sem.at[q], device_id=(y, 2 * q + c), device_id_type=MESH)

    def copy_d(j):
        return pltpu.make_async_remote_copy(
            src_ref=full_b, dst_ref=big_ref.at[c * 4 + y], send_sem=ds_sem.at[j],
            recv_sem=dr_sem.at[j], device_id=(lax.rem(y + j, 4), g), device_id_type=MESH)

    def store_grad(value, columns):
        value = value.astype(BF16)
        for m in range(8):
            send_a[m % 2, m // 2, :, columns] = value[m * eighth : (m + 1) * eighth]

    pl.loop(0, 2)(lambda k: answer(far(k)))
    store_grad(contract(rows1_s[...], back2_s[...], 0, 0), slice(wide, 2 * wide))
    pl.loop(2, 4)(lambda k: answer(far(k)))
    store_grad(contract(half_s[...], back1_s[...], 0, 0), slice(0, wide))
    pair_a = pair_copy(send_a.at[1 - c], got_p, 0)
    pair_a.start()
    pl.loop(4, 7)(lambda k: answer(far(k)))
    answer(None)
    returned[g] = outbox2[g]

    early = plane_sum(send_e, got_e, part_e, gotz_e, early_ref, plane_sems[:6], scale)
    late = plane_sum(send_t, got_t, part_t, gotz_t, late_ref, plane_sems[6:], scale)
    ups = jnp.dot(mixed_s[...], backup_s[...], preferred_element_type=F32).astype(BF16)
    for m in range(16):
        send_e[m] = ups[m // 4 * 16 : m // 4 * 16 + 16, m % 4 * 128 : m % 4 * 128 + 128]
    for m in range(narrow // 16):
        send_e[16 + m, :, :narrow] = bil_grad[m * 16 : (m + 1) * 16, :].astype(BF16)
    send_e[16 + narrow // 16, :, :narrow] = grad[...].astype(BF16)
    early[0]()

    pair_a.wait()
    for j in range(4):
        for r in range(4):
            at = slice(r * TILE, (r + 1) * TILE)
            pair_s[j, at] = (send_a[c, j, at].astype(F32) + got_p[j, at].astype(F32)).astype(BF16)
    each(4, lambda j: copy_a(j).start())
    pl.loop(0, 4)(lambda k: collect(far(k)))
    early[1]()
    collect(far(jnp.int32(4)))
    got_a[0] = pair_s[y]
    each(4, lambda j: copy_a(j).wait_recv())
    for r in range(4):
        at = slice(r * TILE, (r + 1) * TILE)
        total = got_a[0, at].astype(F32)
        for j in range(1, 4):
            total = total + got_a[j, at].astype(F32)
        total = total.astype(BF16)
        for s in range(8):
            part_b[r * 8 + s] = total[:, s * 128 : (s + 1) * 128]
    for j in FARCHIPS:
        to_chip(part_b, got_b, bs_sem, br_sem, j, None).start()
    pl.loop(5, 7)(lambda k: collect(far(k)))
    early[2]()
    collect(None)

    for h in range(high):
        columns = slice(h * LOW, (h + 1) * LOW)
        pre = pre_ref[:, columns]
        back = acc[h * narrow : (h + 1) * narrow]
        back_pre[:, columns] = (back * slope_from(pre, sigmoid(pre))).astype(BF16)
    down = jnp.dot(back_pre[...], edge_ref[...], preferred_element_type=F32)
    for m in range(32):
        send_t[m] = down[m // 4 * 8 : m // 4 * 8 + 8, m % 4 * 128 : m % 4 * 128 + 128]
    late[0]()

    got_b[chip] = part_b[chip]
    each(32, lambda j: from_chip(part_b, got_b, bs_sem, br_sem, j).wait_recv())
    full_b[chip] = (total_of(got_b, 32) * scale).astype(BF16)
    for j in FARCHIPS:
        to_chip(full_b, full_b, cs_sem, cr_sem, j, chip).start()

    blocks = rows // DENSE

    def finish(i):
        at = pl.ds(pl.multiple_of(i * DENSE, DENSE), DENSE)
        add = contract(back_pre[:, at], down_ref[...], 0, 0)
        edge_out[at, :] = (summed[at, :] + add).astype(BF16)

    pl.loop(0, blocks // 2)(finish)
    late[1]()
    each(32, lambda j: from_chip(full_b, full_b, cs_sem, cr_sem, j).wait_recv())
    each(4, lambda j: copy_d(j).start())
    big_ref[c * 4 + y] = full_b[...]
    pl.loop(blocks // 2, blocks)(finish)
    late[2]()
    each(4, lambda j: copy_d(j).wait_recv())
    mine = pl.ds(c * 4, 4)
    pair_d = pair_copy(big_ref.at[mine], big_ref.at[mine], 2)
    pair_d.start()

    @pl.loop(1, shards)
    def _(j):
        p = lax.rem(g + j, shards)
        ask(p).wait_send()
        give(p).wait_send()
        bring(p).wait_send()

    each(4, lambda j: copy_a(j).wait_send())
    each(4, lambda j: copy_d(j).wait_send())
    each(32, lambda j: from_chip(part_b, got_b, bs_sem, br_sem, j).wait_send())
    each(32, lambda j: from_chip(full_b, full_b, cs_sem, cr_sem, j).wait_send())
    early[3]()
    late[3]()
    pair_d.wait()


def main(scale, edge_rows, in_index, down_weight, count, basis_weight, bilinear, cotangent, basis,
         out_index, up, first, second):
    shards, _, slots = in_index.shape
    rows, wide = edge_rows.shape
    narrow = down_weight.shape[0]
    high = rows // LOW
    d = pltpu.SemaphoreType.DMA
    shape = jax.ShapeDtypeStruct
    v = pltpu.VMEM
    block = (shards, narrow, slots)
    tiles = (32, TILE, 128)
    halves = (32, TILE // 2, 128)
    plane = [d((32,)), d((32,)), d((8,)), d((8,)), d((32,)), d((32,))]
    return pl.pallas_call(
        functools.partial(main_kernel, scale),
        out_shape=(
            shape((rows, wide), BF16),
            shape((8,) + tiles, BF16),
            shape(tiles, BF16),
            shape(halves, F32),
        ),
        in_specs=[pl.BlockSpec(memory_space=pltpu.SMEM)] + [HB] * 11,
        out_specs=(VM,) * 4,
        scratch_shapes=[
            v(in_index.shape, jnp.int32), v(down_weight.shape, BF16), v(basis_weight.shape, BF16),
            v(bilinear.shape, BF16), v(edge_rows.shape, BF16), v(cotangent.shape, BF16), v(basis.shape, BF16), v(out_index.shape, jnp.int32),
            v(up.shape, BF16), v(first.shape, BF16), v(second.shape, BF16),
            v(block, BF16), v(in_index.shape, jnp.int32), v((narrow, rows), F32),
            v((high * narrow, LOW), BF16), v(block, BF16), v((high * narrow, LOW), F32),
            v((narrow, rows), BF16),
            v((rows, wide), F32), v((rows, wide), BF16), v((rows, wide), BF16),
            v((rows, wide), BF16), v((rows, wide), BF16), v((rows, wide), BF16),
            v((narrow, rows), BF16), v((narrow, narrow), F32), v(basis_weight.shape, F32),
            v(block, BF16), v(block, BF16), v((narrow, rows), BF16),
            v((2, 4, wide // 8, 2 * wide), BF16), v((4, wide // 8, 2 * wide), BF16),
            v((4, wide // 8, 2 * wide), BF16), v((4, wide // 8, 2 * wide), BF16),
            v(tiles, BF16), v(tiles, BF16), v(tiles, BF16),
            v(tiles, BF16), v(tiles, BF16), v((2,) + tiles[1:], BF16), v((8,) + tiles[1:], BF16),
            v(halves, F32), v(halves, F32), v((2,) + halves[1:], F32), v((8,) + halves[1:], F32),
            d((14,)),
            d((shards,)), d((shards,)), d((shards,)), d((shards,)), d((shards,)), d((shards,)),
            d((4,)), d((4,)), d((4,)), d((32,)), d((32,)), d((32,)), d((32,)), d((4,)), d((4,)),
        ] + plane + plane,
        compiler_params=pltpu.CompilerParams(
            collective_id=1, has_side_effects=True, vmem_limit_bytes=48 * 1024 * 1024),
        name="main",
    )(count, *(
        pltpu.with_memory_space_constraint(a, memory_space=pltpu.HBM)
        for a in (in_index, down_weight, basis_weight, bilinear, edge_rows, cotangent, basis,
                  out_index, up, first, second)))


def final_kernel(edge_ref, big_ref, early_ref, late_ref,
                 edge_out, first_out, second_out, down_out, basis_out, bil_out, up_out,
                 first_buf, second_buf, edge_sem, grad_sem):
    rows, wide = edge_ref.shape
    parts = edge_sem.shape[0]
    span = rows // parts
    narrow = bil_out.shape[0]

    def piece(i):
        at = pl.ds(i * span, span)
        return pltpu.make_async_copy(edge_ref.at[at], edge_out.at[at], edge_sem.at[i])

    def grads(i, buf, out, sem):
        at = pl.ds(i * (wide // 2), wide // 2)
        return pltpu.make_async_copy(buf.at[at], out.at[at], grad_sem.at[sem])

    for i in range(parts):
        piece(i).start()
    for m in range(8):
        block = m % 2 * 4 + m // 2
        for r in range(4):
            at = slice(m * 64 + r * 16, m * 64 + r * 16 + 16)
            for s in range(4):
                columns = slice(s * 128, s * 128 + 128)
                first_buf[at, columns] = big_ref[block, r * 8 + s].astype(F32)
                second_buf[at, columns] = big_ref[block, r * 8 + 4 + s].astype(F32)
        if m % 4 == 3:
            grads(m // 4, first_buf, first_out, m // 4).start()
            grads(m // 4, second_buf, second_out, 2 + m // 4).start()
    for s in range(4):
        for r in range(8):
            down_out[r * 8 : r * 8 + 8, s * 128 : s * 128 + 128] = late_ref[r * 4 + s]
    for m in range(16):
        up_out[m // 4 * 16 : m // 4 * 16 + 16, m % 4 * 128 : m % 4 * 128 + 128] = (
            early_ref[m].astype(F32))
    for m in range(narrow // 16):
        bil_out[m * 16 : (m + 1) * 16, :] = early_ref[16 + m].astype(F32)[:, :narrow]
    basis_out[...] = early_ref[16 + narrow // 16].astype(F32)[:, :narrow]
    for i in range(2):
        grads(i, first_buf, first_out, i).wait()
        grads(i, second_buf, second_out, 2 + i).wait()
    for i in range(parts):
        piece(i).wait()


def final(edge, big, early, late, narrow, bases):
    rows, wide = edge.shape
    shape = jax.ShapeDtypeStruct
    d = pltpu.SemaphoreType.DMA
    smalls = [(narrow, wide), (bases, narrow), (narrow, narrow), (narrow, wide)]
    return pl.pallas_call(
        final_kernel,
        out_shape=(shape((rows, wide), BF16), shape((wide, wide), F32), shape((wide, wide), F32))
        + tuple(shape(s, F32) for s in smalls),
        in_specs=[VM] * 4,
        out_specs=(HB, HB, HB) + (VM,) * 4,
        scratch_shapes=[
            pltpu.VMEM((wide, wide), F32), pltpu.VMEM((wide, wide), F32), d((4,)), d((4,)),
        ],
        compiler_params=pltpu.CompilerParams(vmem_limit_bytes=12 * 1024 * 1024),
        name="final",
    )(edge, big, early, late)


def local(
    edge_state,
    cotangent,
    edge_count,
    triplet_basis,
    triplet_in,
    triplet_out,
    down_weight,
    basis_weight,
    bilinear_weight,
    up_weight,
    first_weight,
    second_weight,
):
    edge_rows = edge_state[0]
    row_count = edge_rows.shape[0]
    shards = lax.axis_size("graph")
    bases, narrow = basis_weight.shape
    tri_rows = triplet_in.shape[1]
    out_index = triplet_out[0].reshape(tri_rows // LOW, 1, LOW)
    in_index = triplet_in[0].reshape(shards, 1, tri_rows // shards)
    grad_scale = 1.0 / math.sqrt(lax.axis_size("dp") * shards * row_count)
    edge_grad, big, early, late = main(
        grad_scale, edge_rows, in_index, down_weight.T, edge_count, basis_weight, bilinear_weight,
        cotangent[0], triplet_basis[0], out_index, up_weight, first_weight, second_weight)
    edge_grad, first_grad, second_grad, down_grad, basis_grad, bilinear_grad, up_grad = final(
        edge_grad, big, early, late, narrow, bases)
    return edge_grad[None], down_grad.T, basis_grad, bilinear_grad, up_grad, first_grad, second_grad


def solution(mesh):
    in_specs = (
        P("dp", "graph", None),
        P("dp", "graph", None),
        P("dp", "graph"),
        P("dp", None, "graph"),
        P("dp", "graph"),
        P("dp", "graph"),
        P(),
        P(),
        P(),
        P(),
        P(),
        P(),
    )
    out_specs = (P("dp", "graph", None), P(), P(), P(), P(), P(), P())
    return jax.shard_map(local, mesh=mesh, in_specs=in_specs, out_specs=out_specs, check_vma=False)
```

```python
import functools
import math

import jax
import jax.numpy as jnp
from jax import lax
from jax.experimental import pallas as pl
from jax.experimental.pallas import tpu as pltpu
from jax.sharding import PartitionSpec as P

HALF = 0.7071067811865476
LOW = 256
MESH = pl.DeviceIdType.MESH
F32 = jnp.float32
BF16 = jnp.bfloat16
VMEM_LIMIT = 60 * 1024 * 1024


def sigmoid(value):
    return 0.5 * jnp.tanh(0.5 * value) + 0.5


def slope_from(value, logistic):
    return logistic * (1.0 + value * (1.0 - logistic))


def contract(left, right, left_dim, right_dim):
    return lax.dot_general(
        left, right, (((left_dim,), (right_dim,)), ((), ())), preferred_element_type=jnp.float32
    )


def low_hot(low, width):
    rows = lax.broadcasted_iota(jnp.int32, (LOW, width), 0)
    return jnp.where(rows == low, 1.0, 0.0).astype(BF16)


def pick(table, index, narrow):
    width = index.shape[1]
    high = table.shape[0] // narrow
    hot = low_hot(index & (LOW - 1), width)
    upper = index >> 8
    wide = jnp.dot(table, hot, preferred_element_type=F32)
    out = wide[:narrow]
    for h in range(1, high):
        out = jnp.where(upper == h, wide[h * narrow : (h + 1) * narrow], out)
    return out


def spread(value, index, high):
    hot = low_hot(index & (LOW - 1), index.shape[1])
    upper = index >> 8
    parts = [jnp.where(upper == h, value, 0.0).astype(BF16) for h in range(high)]
    return contract(jnp.concatenate(parts, axis=0), hot, 1, 1)


def coef_of(weight, basis):
    return contract(weight, basis, 0, 0)


def place():
    g = lax.axis_index("graph")
    return lax.axis_index("dp"), lax.div(g, 8), lax.rem(lax.div(g, 2), 4), lax.rem(g, 2)


def turns():
    y, z, x, c = place()
    return (
        [y] + [lax.rem(y + d, 4) for d in range(1, 4)],
        [z] + [lax.rem(z + d, 8) for d in range(1, 8)],
        [x] + [lax.rem(x + d, 4) for d in range(1, 4)],
        [c, 1 - c],
    )


def far(k):
    return 4 - lax.div(k + 1, 2), lax.rem(k + 1, 2)


def chips_of(group, sign):
    _, z, x, _ = place()
    columns = [x] + [lax.rem(x + (a if sign > 0 else 4 - a), 4) for a in range(1, 4)]
    if group is None:
        return [z * 4 + q for q in columns]
    distance, turn = group
    ahead = distance + turn * (8 - 2 * distance)
    back = 8 - ahead
    rows = [lax.rem(z + (d if sign > 0 else 8 - d), 8) for d in (ahead, back)]
    return [rows[a // 2] * 4 + columns[a] for a in range(4)]


def for_peers(group, sign, fn):
    chips = chips_of(group, sign)
    for a in (0, 2, 1, 3):
        q = chips[a]
        if group is None and a == 0:
            g = lax.axis_index("graph")
            fn(g + 1 - 2 * lax.rem(g, 2))
        else:
            fn(2 * q)
            fn(2 * q + 1)


def row_of(ref, group, sign):
    return jnp.concatenate([ref[q] for q in chips_of(group, sign)], axis=1)


def pairs_of(ref, group, sign):
    return jnp.concatenate(
        [ref[2 * q + c] for q in chips_of(group, sign) for c in range(2)], axis=1)


def columns_of(ref, group, sign):
    return jnp.concatenate(
        [ref[:, pl.ds(pl.multiple_of(q * LOW, LOW), LOW)] for q in chips_of(group, sign)], axis=1)


def put_pairs(ref, group, sign, value):
    for a, q in enumerate(chips_of(group, sign)):
        for c in range(2):
            at = (2 * a + c) * 128
            ref[2 * q + c] = value[:, at : at + 128]


def exchange(src, dst, send_sem, recv_sem):
    y = lax.axis_index("dp")
    g = lax.axis_index("graph")

    def out(p):
        return pltpu.make_async_remote_copy(
            src_ref=src.at[p], dst_ref=dst.at[g], send_sem=send_sem.at[p],
            recv_sem=recv_sem.at[g], device_id=(y, p), device_id_type=MESH)

    def back(p):
        return pltpu.make_async_remote_copy(
            src_ref=src.at[p], dst_ref=dst.at[p], send_sem=send_sem.at[p],
            recv_sem=recv_sem.at[p], device_id=(y, p), device_id_type=MESH)

    return out, back


VM = pl.BlockSpec(memory_space=pltpu.VMEM)
HB = pl.BlockSpec(memory_space=pltpu.HBM)
DENSE = 1024
TILE = 16


FAR32 = sorted(range(1, 32), key=lambda j: -(2 - abs(j // 8 - 2)) - (2 - abs(j // 2 % 4 - 2)))

FARCHIPS = sorted(range(1, 32), key=lambda j: -(4 - abs(j // 4 - 4)) - (2 - abs(j % 4 - 2)))


def each(count, fn):
    @pl.loop(1, count)
    def _(j):
        fn(j)


def total_of(ref, count):
    total = ref[0].astype(F32)
    for j in range(1, count):
        total = total + ref[j].astype(F32)
    return total


def plane_sum(send, got, part, got_z, held, sems, scale):
    y, z, x, c = place()
    mine = y * 8 + x * 2 + c
    ts_sem, tr_sem, zs_sem, zr_sem, us_sem, ur_sem = sems

    ys, zs, xs, cs = turns()

    def member(j):
        py, px, pc = ys[j // 8], xs[j // 2 % 4], cs[j % 2]
        return (py, z * 8 + px * 2 + pc), py * 8 + px * 2 + pc

    def copy_t(j):
        device, index = member(j) if isinstance(j, int) else ((y, z * 8 + x * 2 + 1 - c), mine)
        return pltpu.make_async_remote_copy(
            src_ref=send.at[index], dst_ref=got.at[j], send_sem=ts_sem.at[j],
            recv_sem=tr_sem.at[j], device_id=device, device_id_type=MESH)

    def copy_z(j):
        device = (y, zs[j] * 8 + x * 2 + c) if isinstance(j, int) else (y, z * 8 + x * 2 + 1 - c)
        return pltpu.make_async_remote_copy(
            src_ref=part.at[0], dst_ref=got_z.at[z], send_sem=zs_sem.at[j],
            recv_sem=zr_sem.at[j], device_id=device, device_id_type=MESH)

    def copy_u(j):
        device = member(j)[0] if isinstance(j, int) else (y, z * 8 + x * 2 + 1 - c)
        return pltpu.make_async_remote_copy(
            src_ref=part.at[1], dst_ref=held.at[mine], send_sem=us_sem.at[j],
            recv_sem=ur_sem.at[j], device_id=device, device_id_type=MESH)

    def start():
        for j in FAR32:
            copy_t(j).start()

    def along():
        got[0] = send[mine]
        each(32, lambda j: copy_t(j).wait_recv())
        total = total_of(got, 32).astype(part.dtype)
        part[0] = total
        got_z[z] = total
        for j in (4, 3, 5, 2, 6, 1, 7):
            copy_z(j).start()

    def share():
        each(8, lambda j: copy_z(j).wait_recv())
        total = (total_of(got_z, 8) * scale).astype(part.dtype)
        part[1] = total
        held[mine] = total
        for j in FAR32:
            copy_u(j).start()

    def end():
        each(32, lambda j: copy_u(j).wait())
        each(32, lambda j: copy_t(j).wait_send())
        each(8, lambda j: copy_z(j).wait_send())

    return start, along, share, end


def main_kernel(scale, count_ref, in_hbm, down_hbm, weight_hbm, bil_hbm, edge_in, cot_hbm, basis_hbm, index_hbm, up_hbm, w1_hbm, w2_hbm,
                edge_out, big_ref, early_ref, late_ref,
                in_ref, down_ref, weight_ref, bil_ref, edge_ref, cot_ref, basis_ref, index_ref, up_ref, w1_ref, w2_ref,
                fetched, wanted, pre_ref, table, outbox, acc, gathered,
                summed, half_s, back1_s, rows1_s, back2_s, backup_s, mixed_s, bil_grad, grad,
                outbox2, returned, back_pre,
                send_a, got_p, pair_s, got_a, part_b, got_b, full_b,
                send_e, got_e, part_e, gotz_e, send_t, got_t, part_t, gotz_t,
                load_sem, is_sem, ir_sem, rs_sem, rr_sem, qs_sem, qr_sem,
                ps_sem, as_sem, ar_sem, bs_sem, br_sem, cs_sem, cr_sem, ds_sem, dr_sem,
                *plane_sems):
    shards, narrow = fetched.shape[:2]
    rows, wide = edge_ref.shape
    high = rows // LOW
    y, z, x, c = place()
    g = lax.axis_index("graph")
    chip = z * 4 + x
    barrier = pltpu.get_barrier_semaphore()

    def signal(device):
        pl.semaphore_signal(barrier, inc=1, device_id=device, device_id_type=MESH)

    ys, zs, xs, cs = turns()
    for dz in (4, 3, 5, 2, 6, 1, 7, 0):
        for j in range(8):
            if dz or j:
                signal((y, zs[dz] * 8 + xs[j // 2] * 2 + cs[j % 2]))
    for j in range(8, 32):
        signal((ys[j // 8], z * 8 + xs[j // 2 % 4] * 2 + cs[j % 2]))

    parts = 4
    span = rows // parts
    edges = [
        pltpu.make_async_copy(
            edge_in.at[pl.ds(i * span, span)], edge_ref.at[pl.ds(i * span, span)],
            load_sem.at[8 + i])
        for i in range(parts)
    ]
    loads = [
        pltpu.make_async_copy(src, dst, load_sem.at[i])
        for i, (src, dst) in enumerate((
            (basis_hbm, basis_ref), (index_hbm, index_ref), (up_hbm, up_ref), (w1_hbm, w1_ref),
            (w2_hbm, w2_ref), (cot_hbm, cot_ref), (weight_hbm, weight_ref), (bil_hbm, bil_ref)))
    ]
    heads = [
        pltpu.make_async_copy(in_hbm, in_ref, load_sem.at[12]),
        pltpu.make_async_copy(down_hbm, down_ref, load_sem.at[13]),
    ]
    for load in heads + edges + loads:
        load.start()

    for load in heads:
        load.wait()
    wanted[g] = in_ref[g]
    for h in range(high):
        if h * LOW % span == 0:
            edges[h * LOW // span].wait()
        pre = contract(down_ref[...], edge_ref[h * LOW : (h + 1) * LOW], 1, 1)
        pre_ref[:, h * LOW : (h + 1) * LOW] = pre
        table[h * narrow : (h + 1) * narrow] = (pre * sigmoid(pre)).astype(BF16)
    acc[...] = jnp.zeros_like(acc)
    grad[...] = jnp.zeros_like(grad)
    bil_grad[...] = jnp.zeros_like(bil_grad)
    send_e[...] = jnp.zeros_like(send_e)
    pl.semaphore_wait(barrier, shards - 1 + 24)
    ask, asked = exchange(in_ref, wanted, is_sem, ir_sem)
    give, given = exchange(outbox, fetched, rs_sem, rr_sem)

    for dz in (4, 3, 5, 2, 6, 1, 7, 0):
        for j in range(8):
            if dz or j:
                ask(zs[dz] * 8 + xs[j // 2] * 2 + cs[j % 2]).start()

    def serve(group):
        for_peers(group, 1, lambda p: asked(p).wait_recv())
        index = pairs_of(wanted, group, 1)
        put_pairs(outbox, group, 1, pick(table[...], index, narrow).astype(BF16))
        for_peers(group, 1, lambda p: give(p).start())

    pl.loop(5, 7)(lambda k: serve(far(k)))
    pl.loop(0, 5)(lambda k: serve(far(k)))
    serve(None)
    fetched[g] = outbox[g]
    for load in loads:
        load.wait()

    def gather(group):
        for_peers(group, -1, lambda p: given(p).wait_recv())
        coef = coef_of(weight_ref[...], columns_of(basis_ref, group, -1))
        message = coef * pairs_of(fetched, group, -1).astype(F32)
        acc[...] += spread(message, row_of(index_ref, group, -1), high)

    pl.loop(5, 7)(lambda k: gather(far(k)))
    pl.loop(0, 5)(lambda k: gather(far(k)))
    gather(None)

    for h in range(high):
        gathered[:, h * LOW : (h + 1) * LOW] = acc[h * narrow : (h + 1) * narrow].astype(BF16)
    acc[...] = jnp.zeros_like(acc)

    count = count_ref[0, 0]

    @pl.loop(0, rows // DENSE)
    def _(i):
        at = pl.ds(pl.multiple_of(i * DENSE, DENSE), DENSE)
        gat = gathered[:, at]
        mixed = contract(bil_ref[...], gat, 0, 0).astype(BF16)
        mixed_s[:, at] = mixed
        pre_up = contract(mixed, up_ref[...], 0, 0)
        s_up = sigmoid(pre_up)
        half = (edge_ref[at, :].astype(F32) + pre_up * s_up).astype(BF16)
        half_s[at, :] = half
        pre_first = jnp.dot(half, w1_ref[...], preferred_element_type=F32)
        s_first = sigmoid(pre_first)
        rows1 = (pre_first * s_first).astype(BF16)
        rows1_s[at, :] = rows1
        pre_second = jnp.dot(rows1, w2_ref[...], preferred_element_type=F32)
        live = lax.broadcasted_iota(jnp.int32, (DENSE, 1), 0) + i * DENSE < count
        top = cot_ref[at, :].astype(F32) * jnp.where(live, HALF, 0.0)
        back2 = (top * slope_from(pre_second, sigmoid(pre_second))).astype(BF16)
        back2_s[at, :] = back2
        back1 = contract(back2, w2_ref[...], 1, 1) * slope_from(pre_first, s_first)
        back1 = back1.astype(BF16)
        back1_s[at, :] = back1
        total = top + contract(back1, w1_ref[...], 1, 1)
        summed[at, :] = total
        back_up = (total * slope_from(pre_up, s_up)).astype(BF16)
        backup_s[at, :] = back_up
        back_mixed = contract(up_ref[...], back_up, 1, 1).astype(BF16)
        bil_grad[...] += contract(gat, back_mixed, 1, 1)
        turned = jnp.dot(bil_ref[...], back_mixed, preferred_element_type=F32).astype(BF16)
        for q in range(DENSE // LOW):
            where = pl.multiple_of((i * (DENSE // LOW) + q) * narrow, narrow)
            table[pl.ds(where, narrow), :] = turned[:, q * LOW : (q + 1) * LOW]

    bring, brought = exchange(outbox2, returned, qs_sem, qr_sem)

    def answer(group):
        basis = columns_of(basis_ref, group, 1)
        got = pick(table[...], row_of(index_ref, group, 1), narrow)
        put_pairs(outbox2, group, 1, (got * coef_of(weight_ref[...], basis)).astype(BF16))
        for_peers(group, 1, lambda p: bring(p).start())
        back_coef = (got * pairs_of(fetched, group, 1).astype(F32)).astype(BF16)
        grad[...] += contract(basis, back_coef, 1, 1)

    def collect(group):
        for_peers(group, -1, lambda p: brought(p).wait_recv())
        value = pairs_of(returned, group, -1).astype(F32)
        acc[...] += spread(value, pairs_of(wanted, group, -1), high)

    eighth = wide // 8

    def pair_copy(src, dst, at):
        return pltpu.make_async_remote_copy(
            src_ref=src, dst_ref=dst, send_sem=ps_sem.at[at], recv_sem=ps_sem.at[at + 1],
            device_id=(y, g + 1 - 2 * c), device_id_type=MESH)

    def copy_a(j):
        py = lax.rem(y + j, 4)
        return pltpu.make_async_remote_copy(
            src_ref=pair_s.at[py], dst_ref=got_a.at[j], send_sem=as_sem.at[j],
            recv_sem=ar_sem.at[j], device_id=(py, g), device_id_type=MESH)

    def to_chip(src, dst, send_sem, recv_sem, j, block):
        q = zs[j // 4] * 4 + xs[j % 4]
        return pltpu.make_async_remote_copy(
            src_ref=src.at[q if block is None else block], dst_ref=dst.at[chip],
            send_sem=send_sem.at[q], recv_sem=recv_sem.at[chip], device_id=(y, 2 * q + c),
            device_id_type=MESH)

    def from_chip(src, dst, send_sem, recv_sem, j):
        q = lax.rem(chip + j, 32)
        return pltpu.make_async_remote_copy(
            src_ref=src.at[0], dst_ref=dst.at[q], send_sem=send_sem.at[q],
            recv_sem=recv_sem.at[q], device_id=(y, 2 * q + c), device_id_type=MESH)

    def copy_d(j):
        return pltpu.make_async_remote_copy(
            src_ref=full_b, dst_ref=big_ref.at[c * 4 + y], send_sem=ds_sem.at[j],
            recv_sem=dr_sem.at[j], device_id=(lax.rem(y + j, 4), g), device_id_type=MESH)

    def store_grad(value, columns):
        value = value.astype(BF16)
        for m in range(8):
            send_a[m % 2, m // 2, :, columns] = value[m * eighth : (m + 1) * eighth]

    pl.loop(0, 2)(lambda k: answer(far(k)))
    store_grad(contract(rows1_s[...], back2_s[...], 0, 0), slice(wide, 2 * wide))
    pl.loop(2, 4)(lambda k: answer(far(k)))
    store_grad(contract(half_s[...], back1_s[...], 0, 0), slice(0, wide))
    pair_a = pair_copy(send_a.at[1 - c], got_p, 0)
    pair_a.start()
    pl.loop(4, 7)(lambda k: answer(far(k)))
    answer(None)
    returned[g] = outbox2[g]

    early = plane_sum(send_e, got_e, part_e, gotz_e, early_ref, plane_sems[:6], scale)
    late = plane_sum(send_t, got_t, part_t, gotz_t, late_ref, plane_sems[6:], scale)
    ups = jnp.dot(mixed_s[...], backup_s[...], preferred_element_type=F32).astype(BF16)
    for m in range(16):
        send_e[m] = ups[m // 4 * 16 : m // 4 * 16 + 16, m % 4 * 128 : m % 4 * 128 + 128]
    for m in range(narrow // 16):
        send_e[16 + m, :, :narrow] = bil_grad[m * 16 : (m + 1) * 16, :].astype(BF16)
    send_e[16 + narrow // 16, :, :narrow] = grad[...].astype(BF16)
    early[0]()

    pair_a.wait()
    for j in range(4):
        for r in range(4):
            at = slice(r * TILE, (r + 1) * TILE)
            pair_s[j, at] = (send_a[c, j, at].astype(F32) + got_p[j, at].astype(F32)).astype(BF16)
    each(4, lambda j: copy_a(j).start())
    pl.loop(0, 4)(lambda k: collect(far(k)))
    early[1]()
    collect(far(jnp.int32(4)))
    got_a[0] = pair_s[y]
    each(4, lambda j: copy_a(j).wait_recv())
    for r in range(4):
        at = slice(r * TILE, (r + 1) * TILE)
        total = got_a[0, at].astype(F32)
        for j in range(1, 4):
            total = total + got_a[j, at].astype(F32)
        total = total.astype(BF16)
        for s in range(8):
            part_b[r * 8 + s] = total[:, s * 128 : (s + 1) * 128]
    for j in FARCHIPS:
        to_chip(part_b, got_b, bs_sem, br_sem, j, None).start()
    pl.loop(5, 7)(lambda k: collect(far(k)))
    early[2]()
    got_b[chip] = part_b[chip]
    each(32, lambda j: from_chip(part_b, got_b, bs_sem, br_sem, j).wait_recv())
    full_b[chip] = (total_of(got_b, 32) * scale).astype(BF16)
    for j in FARCHIPS:
        to_chip(full_b, full_b, cs_sem, cr_sem, j, chip).start()
    collect(None)

    for h in range(high):
        columns = slice(h * LOW, (h + 1) * LOW)
        pre = pre_ref[:, columns]
        back = acc[h * narrow : (h + 1) * narrow]
        back_pre[:, columns] = (back * slope_from(pre, sigmoid(pre))).astype(BF16)
    down = jnp.dot(back_pre[...], edge_ref[...], preferred_element_type=F32)
    for m in range(32):
        send_t[m] = down[m // 4 * 8 : m // 4 * 8 + 8, m % 4 * 128 : m % 4 * 128 + 128]
    late[0]()

    blocks = rows // DENSE

    def finish(i):
        at = pl.ds(pl.multiple_of(i * DENSE, DENSE), DENSE)
        add = contract(back_pre[:, at], down_ref[...], 0, 0)
        edge_out[at, :] = (summed[at, :] + add).astype(BF16)

    pl.loop(0, blocks // 2)(finish)
    late[1]()
    each(32, lambda j: from_chip(full_b, full_b, cs_sem, cr_sem, j).wait_recv())
    each(4, lambda j: copy_d(j).start())
    big_ref[c * 4 + y] = full_b[...]
    pl.loop(blocks // 2, blocks)(finish)
    late[2]()
    each(4, lambda j: copy_d(j).wait_recv())
    mine = pl.ds(c * 4, 4)
    pair_d = pair_copy(big_ref.at[mine], big_ref.at[mine], 2)
    pair_d.start()

    @pl.loop(1, shards)
    def _(j):
        p = lax.rem(g + j, shards)
        ask(p).wait_send()
        give(p).wait_send()
        bring(p).wait_send()

    each(4, lambda j: copy_a(j).wait_send())
    each(4, lambda j: copy_d(j).wait_send())
    each(32, lambda j: from_chip(part_b, got_b, bs_sem, br_sem, j).wait_send())
    each(32, lambda j: from_chip(full_b, full_b, cs_sem, cr_sem, j).wait_send())
    early[3]()
    late[3]()
    pair_d.wait()


def main(scale, edge_rows, in_index, down_weight, count, basis_weight, bilinear, cotangent, basis,
         out_index, up, first, second):
    shards, _, slots = in_index.shape
    rows, wide = edge_rows.shape
    narrow = down_weight.shape[0]
    high = rows // LOW
    d = pltpu.SemaphoreType.DMA
    shape = jax.ShapeDtypeStruct
    v = pltpu.VMEM
    block = (shards, narrow, slots)
    tiles = (32, TILE, 128)
    halves = (32, TILE // 2, 128)
    plane = [d((32,)), d((32,)), d((8,)), d((8,)), d((32,)), d((32,))]
    return pl.pallas_call(
        functools.partial(main_kernel, scale),
        out_shape=(
            shape((rows, wide), BF16),
            shape((8,) + tiles, BF16),
            shape(tiles, BF16),
            shape(halves, F32),
        ),
        in_specs=[pl.BlockSpec(memory_space=pltpu.SMEM)] + [HB] * 11,
        out_specs=(VM,) * 4,
        scratch_shapes=[
            v(in_index.shape, jnp.int32), v(down_weight.shape, BF16), v(basis_weight.shape, BF16),
            v(bilinear.shape, BF16), v(edge_rows.shape, BF16), v(cotangent.shape, BF16), v(basis.shape, BF16), v(out_index.shape, jnp.int32),
            v(up.shape, BF16), v(first.shape, BF16), v(second.shape, BF16),
            v(block, BF16), v(in_index.shape, jnp.int32), v((narrow, rows), F32),
            v((high * narrow, LOW), BF16), v(block, BF16), v((high * narrow, LOW), F32),
            v((narrow, rows), BF16),
            v((rows, wide), F32), v((rows, wide), BF16), v((rows, wide), BF16),
            v((rows, wide), BF16), v((rows, wide), BF16), v((rows, wide), BF16),
            v((narrow, rows), BF16), v((narrow, narrow), F32), v(basis_weight.shape, F32),
            v(block, BF16), v(block, BF16), v((narrow, rows), BF16),
            v((2, 4, wide // 8, 2 * wide), BF16), v((4, wide // 8, 2 * wide), BF16),
            v((4, wide // 8, 2 * wide), BF16), v((4, wide // 8, 2 * wide), BF16),
            v(tiles, BF16), v(tiles, BF16), v(tiles, BF16),
            v(tiles, BF16), v(tiles, BF16), v((2,) + tiles[1:], BF16), v((8,) + tiles[1:], BF16),
            v(halves, F32), v(halves, F32), v((2,) + halves[1:], F32), v((8,) + halves[1:], F32),
            d((14,)),
            d((shards,)), d((shards,)), d((shards,)), d((shards,)), d((shards,)), d((shards,)),
            d((4,)), d((4,)), d((4,)), d((32,)), d((32,)), d((32,)), d((32,)), d((4,)), d((4,)),
        ] + plane + plane,
        compiler_params=pltpu.CompilerParams(
            collective_id=1, has_side_effects=True, vmem_limit_bytes=48 * 1024 * 1024),
        name="main",
    )(count, *(
        pltpu.with_memory_space_constraint(a, memory_space=pltpu.HBM)
        for a in (in_index, down_weight, basis_weight, bilinear, edge_rows, cotangent, basis,
                  out_index, up, first, second)))


def final_kernel(edge_ref, big_ref, early_ref, late_ref,
                 edge_out, first_out, second_out, down_out, basis_out, bil_out, up_out,
                 first_buf, second_buf, edge_sem, grad_sem):
    rows, wide = edge_ref.shape
    parts = edge_sem.shape[0]
    span = rows // parts
    narrow = bil_out.shape[0]

    def piece(i):
        at = pl.ds(i * span, span)
        return pltpu.make_async_copy(edge_ref.at[at], edge_out.at[at], edge_sem.at[i])

    def grads(i, buf, out, sem):
        at = pl.ds(i * (wide // 2), wide // 2)
        return pltpu.make_async_copy(buf.at[at], out.at[at], grad_sem.at[sem])

    for i in range(parts):
        piece(i).start()
    for m in range(8):
        block = m % 2 * 4 + m // 2
        for r in range(4):
            at = slice(m * 64 + r * 16, m * 64 + r * 16 + 16)
            for s in range(4):
                columns = slice(s * 128, s * 128 + 128)
                first_buf[at, columns] = big_ref[block, r * 8 + s].astype(F32)
                second_buf[at, columns] = big_ref[block, r * 8 + 4 + s].astype(F32)
        if m % 4 == 3:
            grads(m // 4, first_buf, first_out, m // 4).start()
            grads(m // 4, second_buf, second_out, 2 + m // 4).start()
    for s in range(4):
        for r in range(8):
            down_out[r * 8 : r * 8 + 8, s * 128 : s * 128 + 128] = late_ref[r * 4 + s]
    for m in range(16):
        up_out[m // 4 * 16 : m // 4 * 16 + 16, m % 4 * 128 : m % 4 * 128 + 128] = (
            early_ref[m].astype(F32))
    for m in range(narrow // 16):
        bil_out[m * 16 : (m + 1) * 16, :] = early_ref[16 + m].astype(F32)[:, :narrow]
    basis_out[...] = early_ref[16 + narrow // 16].astype(F32)[:, :narrow]
    for i in range(2):
        grads(i, first_buf, first_out, i).wait()
        grads(i, second_buf, second_out, 2 + i).wait()
    for i in range(parts):
        piece(i).wait()


def final(edge, big, early, late, narrow, bases):
    rows, wide = edge.shape
    shape = jax.ShapeDtypeStruct
    d = pltpu.SemaphoreType.DMA
    smalls = [(narrow, wide), (bases, narrow), (narrow, narrow), (narrow, wide)]
    return pl.pallas_call(
        final_kernel,
        out_shape=(shape((rows, wide), BF16), shape((wide, wide), F32), shape((wide, wide), F32))
        + tuple(shape(s, F32) for s in smalls),
        in_specs=[VM] * 4,
        out_specs=(HB, HB, HB) + (VM,) * 4,
        scratch_shapes=[
            pltpu.VMEM((wide, wide), F32), pltpu.VMEM((wide, wide), F32), d((4,)), d((4,)),
        ],
        compiler_params=pltpu.CompilerParams(vmem_limit_bytes=12 * 1024 * 1024),
        name="final",
    )(edge, big, early, late)


def local(
    edge_state,
    cotangent,
    edge_count,
    triplet_basis,
    triplet_in,
    triplet_out,
    down_weight,
    basis_weight,
    bilinear_weight,
    up_weight,
    first_weight,
    second_weight,
):
    edge_rows = edge_state[0]
    row_count = edge_rows.shape[0]
    shards = lax.axis_size("graph")
    bases, narrow = basis_weight.shape
    tri_rows = triplet_in.shape[1]
    out_index = triplet_out[0].reshape(tri_rows // LOW, 1, LOW)
    in_index = triplet_in[0].reshape(shards, 1, tri_rows // shards)
    grad_scale = 1.0 / math.sqrt(lax.axis_size("dp") * shards * row_count)
    edge_grad, big, early, late = main(
        grad_scale, edge_rows, in_index, down_weight.T, edge_count, basis_weight, bilinear_weight,
        cotangent[0], triplet_basis[0], out_index, up_weight, first_weight, second_weight)
    edge_grad, first_grad, second_grad, down_grad, basis_grad, bilinear_grad, up_grad = final(
        edge_grad, big, early, late, narrow, bases)
    return edge_grad[None], down_grad.T, basis_grad, bilinear_grad, up_grad, first_grad, second_grad


def solution(mesh):
    in_specs = (
        P("dp", "graph", None),
        P("dp", "graph", None),
        P("dp", "graph"),
        P("dp", None, "graph"),
        P("dp", "graph"),
        P("dp", "graph"),
        P(),
        P(),
        P(),
        P(),
        P(),
        P(),
    )
    out_specs = (P("dp", "graph", None), P(), P(), P(), P(), P(), P())
    return jax.shard_map(local, mesh=mesh, in_specs=in_specs, out_specs=out_specs, check_vma=False)
```
